128 devices in a mesh: au: 8 (over z_hi, y), pa: 8 (over x, z_lo), dev: 2 (over core).
Axes of the slice: x: 4, y: 4, z: 4 (z_hi: 2, z_lo: 2; z = z_hi * 2 + z_lo), core: 2. Of those that a mesh axis runs over, the one named last changes fastest.
Arguments:
- features: bfloat16 [8192, 64, 256], P('au', 'pa'), may hold values from -6 to 6
- item_ids: int32 [8192, 64], P('au', 'pa'), may hold values from 0 to 4095
- item_table: bfloat16 [4096, 256], replicated, may hold values from -4 to 4
- lengths: int32 [8192], P('au'), may hold values from 1 to 64
- routing_seed: int32 [4, 64], replicated, may hold values from 0 to 15
- w_qkv: bfloat16 [3, 256, 256], P(None, None, 'dev'), may hold values from -0.375 to 0.375
- w_out: bfloat16 [256, 256], P('dev'), may hold values from -0.375 to 0.375
- w_bilinear: bfloat16 [256, 256], P(None, 'dev'), may hold values from -0.375 to 0.375
- w_up: bfloat16 [256, 1024], P(None, 'dev'), may hold values from -0.375 to 0.375
- w_down: bfloat16 [1024, 256], P('dev'), may hold values from -0.1875 to 0.1875
Outputs:
- capsules: float32 [8192, 4, 256], P(('au', 'pa'), None, 'dev')
The draws below stay inside these ranges and needn't reach their ends.
All inputs are finite; a program needn't handle non-finite values.
Results may differ from the reference program's by a relative error of at most 0.012.
The reference program's roundings to bfloat16 on the way (of `inputs`, `rounded`, `attended`, `hidden` and `interest`) count: a program that leaves them out, or rounds other values in their place, can miss the bound.
Values may be sent and summed in bfloat16 or wider, within the bound.
No kernel may reach another device: no remote copies, remote signals or barrier semaphores. Data moves between devices by JAX's collectives and lax.ppermute only.
A program may use at most 128 MiB of HBM per device.

```python
import math
import jax
import jax.numpy as jnp
import numpy as np
from jax import lax

D = 256
HEADS = 4
FF = 1024
CATS = 4096
HISTORY = 64
CAPS = 4
ITERS = 3
USERS_DEV = 1024
USERS = 8192


def set_ends(entries, rng, least, top_value):
    longest = entries.shape.index(max(entries.shape))
    spots = []
    for shift in (0, 1):
        where = [jax.random.randint(jax.random.fold_in(rng, axis), (), 0, length) for axis, length in enumerate(entries.shape)]
        where[longest] = (where[longest] + shift) % entries.shape[longest]
        spots.append(tuple(where))
    return entries.at[spots[0]].set(least).at[spots[1]].set(top_value)


def block_scale(stream_key, shape, shards, smallest, top_value):
    def one(dim, shards_of):
        heights = jax.random.uniform(jax.random.fold_in(jax.random.fold_in(stream_key, 6), dim), (shards_of,), jnp.float32, smallest / len(shards), top_value / len(shards))
        return jnp.repeat(jnp.exp(heights), shape[dim] // shards_of).reshape((-1,) + (1,) * (len(shape) - dim - 1))

    level = one(*shards[0])
    for cut in shards[1:]:
        level = level * one(*cut)
    return level


def rank_bounds(number_of, lean):
    portions = [(1 << 20) // math.isqrt(grade ** lean) + 1 for grade in range(1, number_of + 1)]
    width = 1 + sum(portions) // (1 << 30)
    return np.cumsum(np.array([max(1, weight // width) for weight in portions]))


def ranked_ids(key, extent, count, lean):
    grid = rank_bounds(count, lean)
    lot = jax.random.randint(jax.random.fold_in(key, 1), extent, 0, int(grid[count - 1]))
    standing = jnp.searchsorted(jnp.asarray(grid, jnp.int32), lot, side="right")
    return jax.random.permutation(jax.random.fold_in(key, 2), count)[standing].astype(jnp.int32)


def bell_draw(key, extent, spread, bound, split=(), kind=jnp.bfloat16):
    gain = block_scale(key, extent, split, -0.22, 0.18) if split else 1.0
    values = jax.random.normal(key, extent, jnp.float32) * spread * gain
    return jnp.minimum(jnp.maximum(values, -bound), bound).astype(kind)


def setup_inputs(seed: int = 0) -> dict:
    keys = jax.random.split(jax.random.key(seed), 11)
    return {
        "features": bell_draw(keys[0], (USERS, HISTORY, D), 1.0, 6.0, ((0, 8), (1, 8))),
        "item_ids": set_ends(ranked_ids(keys[1], (USERS, HISTORY), CATS, 2), jax.random.fold_in(keys[1], 3), 0, CATS - 1).astype(jnp.int32),
        "item_table": bell_draw(keys[2], (CATS, D), 0.7, 4.0),
        "lengths": set_ends(jax.random.randint(keys[3], (USERS,), 1, HISTORY + 1), jax.random.fold_in(keys[3], 1), 1, HISTORY).astype(jnp.int32),
        "routing_seed": set_ends(jax.random.randint(keys[4], (CAPS, HISTORY), 0, 16), jax.random.fold_in(keys[4], 1), 0, 15).astype(jnp.int32),
        "w_qkv": bell_draw(keys[5], (3, D, D), D ** -0.5, 0.375, ((2, 2),)),
        "w_out": bell_draw(keys[6], (D, D), D ** -0.5, 0.375, ((0, 2),)),
        "w_bilinear": bell_draw(keys[7], (D, D), D ** -0.5, 0.375, ((1, 2),)),
        "w_up": bell_draw(keys[8], (D, FF), D ** -0.5, 0.375, ((1, 2),)),
        "w_down": bell_draw(keys[9], (FF, D), FF ** -0.5, 0.1875, ((0, 2),)),
    }


def widen(array):
    return lax.optimization_barrier(array).astype(jnp.float32)

def route(interest, valid, routing_seed):
    vectors = widen(interest)
    user_count = vectors.shape[0]
    base = (routing_seed.astype(jnp.float32) - 7.5) * 0.25
    logits = jnp.broadcast_to(base[None], (user_count, CAPS, HISTORY))
    capsules = jnp.zeros((user_count, CAPS, vectors.shape[2]), jnp.float32)
    for sweep in range(ITERS):
        weights = jax.nn.softmax(logits, axis=1) * valid[:, None, :]
        summed = jnp.einsum('ukl,uld->ukd', weights, vectors, precision=lax.Precision.HIGHEST)
        squares = lax.optimization_barrier(jnp.sum(summed * summed, axis=-1))
        factor = jnp.sqrt(squares) / (1.0 + squares)
        capsules = summed * factor[..., None]
        if sweep + 1 < ITERS:
            logits = logits + jnp.einsum('ukd,uld->ukl', capsules, vectors, precision=lax.Precision.HIGHEST)
    return capsules

def encode(feats, ids, user_lengths, item_table, routing_seed, w_qkv, w_out, w_bilinear, w_up, w_down):
    user_count = feats.shape[0]
    head_size = D // HEADS
    inputs = (feats.astype(jnp.float32) + item_table[ids].astype(jnp.float32)).astype(jnp.bfloat16)
    flat_rows = inputs.reshape(-1, D)

    def project(index):
        made = jnp.dot(flat_rows, w_qkv[index], preferred_element_type=jnp.float32).astype(jnp.bfloat16)
        return widen(made.reshape(user_count, HISTORY, HEADS, head_size))
    queries = project(0)
    key_block = project(1)
    value_block = project(2)
    scores = jnp.einsum('uqhe,ukhe->uqhk', queries, key_block, precision=lax.Precision.HIGHEST) * (1.0 / head_size ** 0.5)
    valid_keys = jnp.arange(HISTORY)[None, :] < user_lengths[:, None]
    mask_four = valid_keys[:, None, None, :]
    probs = jnp.where(mask_four, jnp.exp(scores), 0.0)
    totals = lax.optimization_barrier(jnp.sum(probs, axis=-1))
    rounded = widen(probs.astype(jnp.bfloat16))
    weighted = jnp.einsum('uqhk,ukhe->uqhe', rounded, value_block, precision=lax.Precision.HIGHEST)
    attended = (weighted / totals[..., None]).astype(jnp.bfloat16).reshape(-1, D)
    hidden = jax.nn.gelu(jnp.dot(flat_rows, w_up, preferred_element_type=jnp.float32)).astype(jnp.bfloat16)
    interest = (jnp.dot(flat_rows, w_bilinear, preferred_element_type=jnp.float32) + jnp.dot(attended, w_out, preferred_element_type=jnp.float32) + jnp.dot(hidden, w_down, preferred_element_type=jnp.float32)).astype(jnp.bfloat16)
    interest = interest.reshape(user_count, HISTORY, D)
    return route(interest, valid_keys.astype(jnp.float32), routing_seed)

def reference(features, item_ids, item_table, lengths, routing_seed, w_qkv, w_out, w_bilinear, w_up, w_down):
    blocks = USERS // USERS_DEV
    feat_blocks = features.reshape(blocks, USERS_DEV, HISTORY, D)
    id_blocks = item_ids.reshape(blocks, USERS_DEV, HISTORY)
    length_blocks = lengths.reshape(blocks, USERS_DEV)

    def one_block(group):
        return encode(group[0], group[1], group[2], item_table, routing_seed, w_qkv, w_out, w_bilinear, w_up, w_down)
    result = lax.map(one_block, (feat_blocks, id_blocks, length_blocks))
    return result.reshape(USERS, CAPS, D)
```

```python
import functools

import jax
import jax.numpy as jnp
from jax import lax
from jax.experimental import pallas as pl
from jax.experimental.pallas import tpu as pltpu
from jax.sharding import PartitionSpec as P

D = 256
HEADS = 4
CAPS = 4
ITERS = 3
CHUNKS = 2
BLOCK = 8
GROUP = 4
F32 = jnp.float32
BF16 = jnp.bfloat16


def lookup_kernel(core_ref, ids_ref, feat_ref, table_ref, out_ref, wide_ref, *, chunk, per_pair, per_core):
    users, spots, _ = feat_ref.shape
    step = pl.program_id(0)

    @pl.when(step == 0)
    def _():
        rows = 256

        def widen(i, carry):
            at = pl.ds(pl.multiple_of(i * rows, rows), rows)
            wide_ref[at, :] = table_ref[at, :].astype(F32)
            return carry

        lax.fori_loop(0, table_ref.shape[0] // rows, widen, 0)

    first = step * per_pair + core_ref[0] * per_core + chunk * users
    spot = lax.broadcasted_iota(jnp.int32, (spots, D), 0)

    def one(user, carry):
        rows = jnp.broadcast_to(wide_ref[pl.ds(ids_ref[0, first + user], 1), :], (spots, D))
        for p in range(1, spots):
            row = jnp.broadcast_to(wide_ref[pl.ds(ids_ref[p, first + user], 1), :], (spots, D))
            rows = jnp.where(spot == p, row, rows)
        out_ref[user] = (feat_ref[user].astype(F32) + rows).astype(BF16)
        return carry

    lax.fori_loop(0, users, one, 0, unroll=8)


def lookup(core, ids, features, table, chunk, pa_count, dev_count):
    all_users, spots, width = features.shape
    per_pair = all_users // pa_count
    per_core = per_pair // dev_count
    users = per_core // CHUNKS
    return pl.pallas_call(
        functools.partial(lookup_kernel, chunk=chunk, per_pair=per_pair, per_core=per_core),
        out_shape=jax.ShapeDtypeStruct((pa_count * users, spots, width), BF16),
        grid_spec=pltpu.PrefetchScalarGridSpec(
            num_scalar_prefetch=2,
            grid=(pa_count,),
            in_specs=[
                pl.BlockSpec(
                    (users, spots, width),
                    lambda d, c, i: (d * (per_pair // users) + c[0] * CHUNKS + chunk, 0, 0),
                ),
                pl.BlockSpec(table.shape, lambda d, c, i: (0, 0), pipeline_mode=pl.Buffered(1)),
            ],
            out_specs=pl.BlockSpec((users, spots, width), lambda d, c, i: (d, 0, 0)),
            scratch_shapes=[pltpu.VMEM(table.shape, F32)],
        ),
        compiler_params=pltpu.CompilerParams(vmem_limit_bytes=24 << 20),
        name="lookup",
    )(core, ids, features, table)


def weights_kernel(
    core_ref, qkv_a, qkv_b, out_a, out_b, bil_a, bil_b, up_a, up_b, down_a, down_b, qkv, up, tail
):
    half = D // 2
    for i in range(3):
        qkv[:, i * D : i * D + half] = qkv_a[i]
        qkv[:, i * D + half : (i + 1) * D] = qkv_b[i]
    ff = up_a.shape[1]
    up[:, :ff] = up_a[...]
    up[:, ff:] = up_b[...]

    @pl.when(core_ref[0] == 0)
    def _():
        tail[:D, :half] = bil_a[...]
        tail[:D, half:] = bil_b[...]

    @pl.when(core_ref[0] != 0)
    def _():
        tail[:D, :half] = bil_b[...]
        tail[:D, half:] = bil_a[...]

    tail[D : D + half, :] = out_a[...]
    tail[D + half : 2 * D, :] = out_b[...]
    tail[2 * D : 2 * D + ff, :] = down_a[...]
    tail[2 * D + ff :, :] = down_b[...]


def finish_weights(core, own, other):
    ff = own[3].shape[1]
    operands = [w for pair in zip(own, other) for w in pair]
    return pl.pallas_call(
        weights_kernel,
        out_shape=[
            jax.ShapeDtypeStruct((D, 3 * D), BF16),
            jax.ShapeDtypeStruct((D, 2 * ff), BF16),
            jax.ShapeDtypeStruct((2 * D + 2 * ff, D), BF16),
        ],
        in_specs=[pl.BlockSpec(memory_space=pltpu.SMEM)]
        + [pl.BlockSpec(memory_space=pltpu.VMEM)] * len(operands),
        out_specs=[pl.BlockSpec(memory_space=pltpu.VMEM)] * 3,
        compiler_params=pltpu.CompilerParams(vmem_limit_bytes=16 << 20),
        name="weights",
    )(core, *operands)


def split(x):
    high = x.astype(BF16)
    return jnp.concatenate([high, (x - high.astype(F32)).astype(BF16)], axis=0)


def joined(x):
    half = x.shape[0] // 2
    return x[:half] + x[half:]


def encode_kernel(core_ref, x_ref, lens_ref, seed_ref, qkv_ref, up_ref, tail_ref, own_ref, other_ref, interest_ref):
    step = pl.program_id(0)
    history = x_ref.shape[0] * x_ref.shape[2]
    rows = BLOCK * history
    head = D // HEADS
    lanes = HEADS * history
    x = x_ref[...].astype(F32)
    x = jnp.swapaxes(x, 0, 1).reshape(rows, D).astype(BF16)
    qkv = jnp.dot(x, qkv_ref[...], preferred_element_type=F32)
    queries = (qkv[:, :D] * (1.0 / head**0.5)).astype(BF16)
    keys = qkv[:, D : 2 * D].astype(BF16)
    values = qkv[:, 2 * D :].astype(BF16)

    lane_head = lax.broadcasted_iota(jnp.int32, (history, D), 1) // head
    own_head = [(lane_head == h).astype(F32).astype(BF16) for h in range(HEADS)]
    row_head = lax.broadcasted_iota(jnp.int32, (lanes, D), 0) // history
    col_head = lax.broadcasted_iota(jnp.int32, (lanes, D), 1) // head
    ones = (row_head == col_head).astype(F32).astype(BF16)
    position = lax.broadcasted_iota(jnp.int32, (BLOCK, lanes), 1) % history
    lens = lens_ref[pl.ds(pl.multiple_of(step * BLOCK, BLOCK), BLOCK), :]
    key_valid = (position < lens).astype(F32)
    attended = []
    for u in range(BLOCK):
        at = slice(u * history, (u + 1) * history)
        key_wide = jnp.concatenate([keys[at] * m for m in own_head], axis=0)
        value_wide = jnp.concatenate([values[at] * m for m in own_head], axis=0)
        scores = lax.dot_general(
            queries[at], key_wide, (((1,), (1,)), ((), ())), preferred_element_type=F32
        )
        probs = jnp.where(key_valid[u : u + 1] > 0.0, jnp.exp(scores), 0.0)
        rounded = probs.astype(BF16)
        rest = (probs - rounded.astype(F32)).astype(BF16)
        totals = jnp.dot(rounded, ones, preferred_element_type=F32) + jnp.dot(
            rest, ones, preferred_element_type=F32
        )
        weighted = jnp.dot(rounded, value_wide, preferred_element_type=F32)
        attended.append((weighted / totals).astype(BF16))
    attended = jnp.concatenate(attended, axis=0)
    hidden = jax.nn.gelu(jnp.dot(x, up_ref[...], preferred_element_type=F32)).astype(BF16)
    everything = jnp.concatenate([x, attended, hidden], axis=1)
    interest = jnp.dot(everything, tail_ref[...], preferred_element_type=F32).astype(BF16)
    interest_ref[step] = interest

    @pl.when(step == pl.num_programs(0) - 1)
    def _():
        route(core_ref, lens_ref, seed_ref, own_ref, other_ref, interest_ref, history)


def route(core_ref, lens_ref, seed_ref, own_ref, other_ref, interest_ref, history):
    blocks = interest_ref.shape[0]
    lanes = GROUP * history
    groups = BLOCK // GROUP
    lane = lax.broadcasted_iota(jnp.int32, (BLOCK, lanes), 1)
    user = lax.broadcasted_iota(jnp.int32, (BLOCK, lanes), 0)
    mine = (lane // history) == (user % GROUP)
    base = (seed_ref[...].astype(F32) - 7.5) * 0.25
    base = jnp.concatenate([base] * GROUP, axis=1)
    base = jnp.broadcast_to(base[:, None, :], (CAPS, BLOCK, lanes))
    logits = [base] * blocks
    valid = []
    for b in range(blocks):
        real = mine & ((lane % history) < lens_ref[b * BLOCK : (b + 1) * BLOCK, :])
        valid.append([(real & ((user // GROUP) == g)).astype(F32) for g in range(groups)])
    capsules = [None] * blocks
    for sweep in range(ITERS):
        for b in range(blocks):
            top = jnp.max(logits[b], axis=0, keepdims=True)
            weights = jnp.exp(logits[b] - top)
            weights = weights / jnp.sum(weights, axis=0, keepdims=True)
            summed = 0.0
            for g in range(groups):
                part = (weights * valid[b][g][None]).reshape(CAPS * BLOCK, lanes)
                vectors = interest_ref[b, g * lanes : (g + 1) * lanes, :]
                summed = summed + jnp.dot(split(part), vectors, preferred_element_type=F32)
            summed = joined(summed)
            squares = jnp.sum(summed * summed, axis=1, keepdims=True)
            capsules[b] = summed * (jnp.sqrt(squares) / (1.0 + squares))
            if sweep + 1 < ITERS:
                caps = split(capsules[b])
                near = []
                for g in range(groups):
                    vectors = interest_ref[b, g * lanes : (g + 1) * lanes, :]
                    near.append(
                        joined(
                            lax.dot_general(
                                caps, vectors, (((1,), (1,)), ((), ())), preferred_element_type=F32
                            )
                        ).reshape(CAPS, BLOCK, lanes)
                    )
                added = near[-1]
                for g in range(groups - 1):
                    added = jnp.where(((user // GROUP) == g)[None], near[g], added)
                logits[b] = logits[b] + added
    half = D // 2
    low_own = core_ref[0] == 0
    for b in range(blocks):
        made = capsules[b].reshape(CAPS, BLOCK, D)
        low, high = made[:, :, :half], made[:, :, half:]
        own_ref[:, b * BLOCK : (b + 1) * BLOCK, :] = jnp.where(low_own, low, high)
        other_ref[:, b * BLOCK : (b + 1) * BLOCK, :] = jnp.where(low_own, high, low)


def encode(core, gathered, lens, seed, qkv, up, tail):
    pa_count, users, spots, _ = gathered.shape
    history = pa_count * spots
    half = D // 2
    fixed = lambda a: pl.BlockSpec(a.shape, lambda s, c: (0,) * a.ndim, pipeline_mode=pl.Buffered(1))
    made = jax.ShapeDtypeStruct((CAPS, users, half), F32)
    return pl.pallas_call(
        encode_kernel,
        out_shape=[made, made],
        grid_spec=pltpu.PrefetchScalarGridSpec(
            num_scalar_prefetch=1,
            grid=(users // BLOCK,),
            in_specs=[
                pl.BlockSpec((pa_count, BLOCK, spots, D), lambda s, c: (0, s, 0, 0)),
                fixed(lens),
                fixed(seed),
                fixed(qkv),
                fixed(up),
                fixed(tail),
            ],
            out_specs=[pl.BlockSpec(made.shape, lambda s, c: (0, 0, 0))] * 2,
            scratch_shapes=[pltpu.VMEM((users // BLOCK, BLOCK * history, D), BF16)],
        ),
        compiler_params=pltpu.CompilerParams(vmem_limit_bytes=40 << 20),
        name="encode",
    )(core, gathered, lens, seed, qkv, up, tail)


def body(
    features, item_ids, item_table, lengths, routing_seed, w_qkv, w_out, w_bilinear, w_up, w_down
):
    pa_count = lax.axis_size("pa")
    dev_count = lax.axis_size("dev")
    spots = features.shape[1]
    per_core = lengths.shape[0] // (pa_count * dev_count)
    users = per_core // CHUNKS
    core_index = lax.axis_index("dev").astype(jnp.int32)
    core = core_index.reshape(1)
    swap = [(i, dev_count - 1 - i) for i in range(dev_count)]
    own = (w_qkv, w_out, w_bilinear, w_up, w_down)
    other = tuple(lax.ppermute(w, "dev", swap) for w in own)
    qkv, up, tail = finish_weights(core, own, other)
    first = (lax.axis_index("pa") * dev_count + core_index) * per_core
    lens = lax.dynamic_slice_in_dim(lengths, first, per_core).reshape(per_core, 1)
    ids = item_ids.T
    halves = []
    for chunk in range(CHUNKS):
        sent = lookup(core, ids, features, item_table, chunk, pa_count, dev_count)
        got = lax.all_to_all(sent, "pa", split_axis=0, concat_axis=0, tiled=True)
        got = got.reshape(pa_count, users, spots, D)
        kept, passed = encode(
            core, got, lens[chunk * users : (chunk + 1) * users], routing_seed, qkv, up, tail
        )
        halves.append((kept, lax.ppermute(passed, "dev", swap)))
    kept = jnp.concatenate([h[0] for h in halves], axis=1)
    came = jnp.concatenate([h[1] for h in halves], axis=1)
    made = jnp.where(
        core_index == 0,
        jnp.concatenate([kept, came], axis=1),
        jnp.concatenate([came, kept], axis=1),
    )
    return jnp.swapaxes(made, 0, 1)


def solution(mesh):
    in_specs = (
        P("au", "pa", None),
        P("au", "pa"),
        P(),
        P("au"),
        P(),
        P(None, None, "dev"),
        P("dev", None),
        P(None, "dev"),
        P(None, "dev"),
        P("dev", None),
    )
    out_specs = P(("au", "pa"), None, "dev")
    return jax.shard_map(body, mesh=mesh, in_specs=in_specs, out_specs=out_specs, check_vma=False)
```

```python
import functools

import jax
import jax.numpy as jnp
from jax import lax
from jax.experimental import pallas as pl
from jax.experimental.pallas import tpu as pltpu
from jax.sharding import PartitionSpec as P

D = 256
HEADS = 4
CAPS = 4
ITERS = 3
CHUNKS = 2
BLOCK = 8
GROUP = 4
F32 = jnp.float32
BF16 = jnp.bfloat16


def in_hbm(*arrays):
    return tuple(pltpu.with_memory_space_constraint(a, pltpu.HBM) for a in arrays)


def lookup_kernel(core_ref, ids_ref, feat_ref, table_ref, out_ref, wide_ref, *, chunk, per_pair, per_core):
    users, spots, _ = feat_ref.shape
    step = pl.program_id(0)

    @pl.when(step == 0)
    def _():
        rows = 256

        def widen(i, carry):
            at = pl.ds(pl.multiple_of(i * rows, rows), rows)
            wide_ref[at, :] = table_ref[at, :].astype(F32)
            return carry

        lax.fori_loop(0, table_ref.shape[0] // rows, widen, 0)

    first = step * per_pair + core_ref[0] * per_core + chunk * users
    spot = lax.broadcasted_iota(jnp.int32, (spots, D), 0)

    def one(user, carry):
        rows = jnp.broadcast_to(wide_ref[pl.ds(ids_ref[0, first + user], 1), :], (spots, D))
        for p in range(1, spots):
            row = jnp.broadcast_to(wide_ref[pl.ds(ids_ref[p, first + user], 1), :], (spots, D))
            rows = jnp.where(spot == p, row, rows)
        out_ref[user] = (feat_ref[user].astype(F32) + rows).astype(BF16)
        return carry

    lax.fori_loop(0, users, one, 0, unroll=8)


def lookup(core, ids, features, table, chunk, pa_count, dev_count):
    all_users, spots, width = features.shape
    per_pair = all_users // pa_count
    per_core = per_pair // dev_count
    users = per_core // CHUNKS
    return pl.pallas_call(
        functools.partial(lookup_kernel, chunk=chunk, per_pair=per_pair, per_core=per_core),
        out_shape=pltpu.HBM((pa_count * users, spots, width), BF16),
        grid_spec=pltpu.PrefetchScalarGridSpec(
            num_scalar_prefetch=2,
            grid=(pa_count,),
            in_specs=[
                pl.BlockSpec(
                    (users, spots, width),
                    lambda d, c, i: (d * (per_pair // users) + c[0] * CHUNKS + chunk, 0, 0),
                ),
                pl.BlockSpec(table.shape, lambda d, c, i: (0, 0), pipeline_mode=pl.Buffered(1)),
            ],
            out_specs=pl.BlockSpec((users, spots, width), lambda d, c, i: (d, 0, 0)),
            scratch_shapes=[pltpu.VMEM(table.shape, F32)],
        ),
        compiler_params=pltpu.CompilerParams(vmem_limit_bytes=24 << 20),
        name="lookup",
    )(core, ids, *in_hbm(features, table))


def weights_kernel(
    core_ref, qkv_a, qkv_b, out_a, out_b, bil_a, bil_b, up_a, up_b, down_a, down_b, qkv, up, tail
):
    half = D // 2
    for i in range(3):
        qkv[:, i * D : i * D + half] = qkv_a[i]
        qkv[:, i * D + half : (i + 1) * D] = qkv_b[i]
    ff = up_a.shape[1]
    up[:, :ff] = up_a[...]
    up[:, ff:] = up_b[...]

    @pl.when(core_ref[0] == 0)
    def _():
        tail[:D, :half] = bil_a[...]
        tail[:D, half:] = bil_b[...]

    @pl.when(core_ref[0] != 0)
    def _():
        tail[:D, :half] = bil_b[...]
        tail[:D, half:] = bil_a[...]

    tail[D : D + half, :] = out_a[...]
    tail[D + half : 2 * D, :] = out_b[...]
    tail[2 * D : 2 * D + ff, :] = down_a[...]
    tail[2 * D + ff :, :] = down_b[...]


def finish_weights(core, own, other):
    ff = own[3].shape[1]
    operands = [w for pair in zip(own, other) for w in pair]
    return pl.pallas_call(
        weights_kernel,
        out_shape=[
            pltpu.HBM((D, 3 * D), BF16),
            pltpu.HBM((D, 2 * ff), BF16),
            pltpu.HBM((2 * D + 2 * ff, D), BF16),
        ],
        in_specs=[pl.BlockSpec(memory_space=pltpu.SMEM)]
        + [pl.BlockSpec(memory_space=pltpu.VMEM)] * len(operands),
        out_specs=[pl.BlockSpec(memory_space=pltpu.VMEM)] * 3,
        compiler_params=pltpu.CompilerParams(vmem_limit_bytes=16 << 20),
        name="weights",
    )(core, *in_hbm(*operands))


def split(x):
    high = x.astype(BF16)
    return jnp.concatenate([high, (x - high.astype(F32)).astype(BF16)], axis=0)


def joined(x):
    half = x.shape[0] // 2
    return x[:half] + x[half:]


def encode_kernel(core_ref, x_ref, lens_ref, seed_ref, qkv_ref, up_ref, tail_ref, own_ref, other_ref, interest_ref):
    step = pl.program_id(0)
    history = x_ref.shape[0] * x_ref.shape[2]
    rows = BLOCK * history
    head = D // HEADS
    lanes = HEADS * history
    x = x_ref[...].astype(F32)
    x = jnp.swapaxes(x, 0, 1).reshape(rows, D).astype(BF16)
    qkv = jnp.dot(x, qkv_ref[...], preferred_element_type=F32)
    queries = (qkv[:, :D] * (1.0 / head**0.5)).astype(BF16)
    keys = qkv[:, D : 2 * D].astype(BF16)
    values = qkv[:, 2 * D :].astype(BF16)

    lane_head = lax.broadcasted_iota(jnp.int32, (history, D), 1) // head
    own_head = [(lane_head == h).astype(F32).astype(BF16) for h in range(HEADS)]
    row_head = lax.broadcasted_iota(jnp.int32, (lanes, D), 0) // history
    col_head = lax.broadcasted_iota(jnp.int32, (lanes, D), 1) // head
    ones = (row_head == col_head).astype(F32).astype(BF16)
    position = lax.broadcasted_iota(jnp.int32, (BLOCK, lanes), 1) % history
    lens = lens_ref[pl.ds(pl.multiple_of(step * BLOCK, BLOCK), BLOCK), :]
    key_valid = (position < lens).astype(F32)
    attended = []
    for u in range(BLOCK):
        at = slice(u * history, (u + 1) * history)
        key_wide = jnp.concatenate([keys[at] * m for m in own_head], axis=0)
        value_wide = jnp.concatenate([values[at] * m for m in own_head], axis=0)
        scores = lax.dot_general(
            queries[at], key_wide, (((1,), (1,)), ((), ())), preferred_element_type=F32
        )
        probs = jnp.where(key_valid[u : u + 1] > 0.0, jnp.exp(scores), 0.0)
        rounded = probs.astype(BF16)
        rest = (probs - rounded.astype(F32)).astype(BF16)
        totals = jnp.dot(rounded, ones, preferred_element_type=F32) + jnp.dot(
            rest, ones, preferred_element_type=F32
        )
        weighted = jnp.dot(rounded, value_wide, preferred_element_type=F32)
        attended.append((weighted / totals).astype(BF16))
    attended = jnp.concatenate(attended, axis=0)
    hidden = jax.nn.gelu(jnp.dot(x, up_ref[...], preferred_element_type=F32)).astype(BF16)
    everything = jnp.concatenate([x, attended, hidden], axis=1)
    interest = jnp.dot(everything, tail_ref[...], preferred_element_type=F32).astype(BF16)
    interest_ref[step] = interest

    @pl.when(step == pl.num_programs(0) - 1)
    def _():
        route(core_ref, lens_ref, seed_ref, own_ref, other_ref, interest_ref, history)


def route(core_ref, lens_ref, seed_ref, own_ref, other_ref, interest_ref, history):
    blocks = interest_ref.shape[0]
    lanes = GROUP * history
    groups = BLOCK // GROUP
    lane = lax.broadcasted_iota(jnp.int32, (BLOCK, lanes), 1)
    user = lax.broadcasted_iota(jnp.int32, (BLOCK, lanes), 0)
    mine = (lane // history) == (user % GROUP)
    base = (seed_ref[...].astype(F32) - 7.5) * 0.25
    base = jnp.concatenate([base] * GROUP, axis=1)
    base = jnp.broadcast_to(base[:, None, :], (CAPS, BLOCK, lanes))
    logits = [base] * blocks
    valid = []
    for b in range(blocks):
        real = mine & ((lane % history) < lens_ref[b * BLOCK : (b + 1) * BLOCK, :])
        valid.append([(real & ((user // GROUP) == g)).astype(F32) for g in range(groups)])
    capsules = [None] * blocks
    for sweep in range(ITERS):
        for b in range(blocks):
            top = jnp.max(logits[b], axis=0, keepdims=True)
            weights = jnp.exp(logits[b] - top)
            weights = weights / jnp.sum(weights, axis=0, keepdims=True)
            summed = 0.0
            for g in range(groups):
                part = (weights * valid[b][g][None]).reshape(CAPS * BLOCK, lanes)
                vectors = interest_ref[b, g * lanes : (g + 1) * lanes, :]
                summed = summed + jnp.dot(split(part), vectors, preferred_element_type=F32)
            summed = joined(summed)
            squares = jnp.sum(summed * summed, axis=1, keepdims=True)
            capsules[b] = summed * (jnp.sqrt(squares) / (1.0 + squares))
            if sweep + 1 < ITERS:
                caps = split(capsules[b])
                near = []
                for g in range(groups):
                    vectors = interest_ref[b, g * lanes : (g + 1) * lanes, :]
                    near.append(
                        joined(
                            lax.dot_general(
                                caps, vectors, (((1,), (1,)), ((), ())), preferred_element_type=F32
                            )
                        ).reshape(CAPS, BLOCK, lanes)
                    )
                added = near[-1]
                for g in range(groups - 1):
                    added = jnp.where(((user // GROUP) == g)[None], near[g], added)
                logits[b] = logits[b] + added
    half = D // 2
    low_own = core_ref[0] == 0
    for b in range(blocks):
        made = capsules[b].reshape(CAPS, BLOCK, D)
        low, high = made[:, :, :half], made[:, :, half:]
        own_ref[:, b * BLOCK : (b + 1) * BLOCK, :] = jnp.where(low_own, low, high)
        other_ref[:, b * BLOCK : (b + 1) * BLOCK, :] = jnp.where(low_own, high, low)


def encode(core, gathered, lens, seed, qkv, up, tail):
    pa_count, users, spots, _ = gathered.shape
    history = pa_count * spots
    half = D // 2
    fixed = lambda a: pl.BlockSpec(a.shape, lambda s, c: (0,) * a.ndim, pipeline_mode=pl.Buffered(1))
    made = jax.ShapeDtypeStruct((CAPS, users, half), F32)
    return pl.pallas_call(
        encode_kernel,
        out_shape=[made, made],
        grid_spec=pltpu.PrefetchScalarGridSpec(
            num_scalar_prefetch=1,
            grid=(users // BLOCK,),
            in_specs=[
                pl.BlockSpec((pa_count, BLOCK, spots, D), lambda s, c: (0, s, 0, 0)),
                fixed(lens),
                fixed(seed),
                fixed(qkv),
                fixed(up),
                fixed(tail),
            ],
            out_specs=[pl.BlockSpec(made.shape, lambda s, c: (0, 0, 0))] * 2,
            scratch_shapes=[pltpu.VMEM((users // BLOCK, BLOCK * history, D), BF16)],
        ),
        compiler_params=pltpu.CompilerParams(vmem_limit_bytes=40 << 20),
        name="encode",
    )(core, *in_hbm(gathered, lens, seed, qkv, up, tail))


def body(
    features, item_ids, item_table, lengths, routing_seed, w_qkv, w_out, w_bilinear, w_up, w_down
):
    pa_count = lax.axis_size("pa")
    dev_count = lax.axis_size("dev")
    spots = features.shape[1]
    per_core = lengths.shape[0] // (pa_count * dev_count)
    users = per_core // CHUNKS
    core_index = lax.axis_index("dev").astype(jnp.int32)
    core = core_index.reshape(1)
    swap = [(i, dev_count - 1 - i) for i in range(dev_count)]
    own = (w_qkv, w_out, w_bilinear, w_up, w_down)
    other = tuple(lax.ppermute(w, "dev", swap) for w in own)
    qkv, up, tail = finish_weights(core, own, other)
    first = (lax.axis_index("pa") * dev_count + core_index) * per_core
    lens = lax.dynamic_slice_in_dim(lengths, first, per_core).reshape(per_core, 1)
    ids = item_ids.T
    halves = []
    for chunk in range(CHUNKS):
        sent = lookup(core, ids, features, item_table, chunk, pa_count, dev_count)
        got = lax.all_to_all(sent, "pa", split_axis=0, concat_axis=0, tiled=True)
        got = got.reshape(pa_count, users, spots, D)
        kept, passed = encode(
            core, got, lens[chunk * users : (chunk + 1) * users], routing_seed, qkv, up, tail
        )
        halves.append((kept, lax.ppermute(passed, "dev", swap)))
    kept = jnp.concatenate([h[0] for h in halves], axis=1)
    came = jnp.concatenate([h[1] for h in halves], axis=1)
    made = jnp.where(
        core_index == 0,
        jnp.concatenate([kept, came], axis=1),
        jnp.concatenate([came, kept], axis=1),
    )
    return jnp.swapaxes(made, 0, 1)


def solution(mesh):
    in_specs = (
        P("au", "pa", None),
        P("au", "pa"),
        P(),
        P("au"),
        P(),
        P(None, None, "dev"),
        P("dev", None),
        P(None, "dev"),
        P(None, "dev"),
        P("dev", None),
    )
    out_specs = P(("au", "pa"), None, "dev")
    return jax.shard_map(body, mesh=mesh, in_specs=in_specs, out_specs=out_specs, check_vma=False)
```

```python
import functools

import jax
import jax.numpy as jnp
from jax import lax
from jax.experimental import pallas as pl
from jax.experimental.pallas import tpu as pltpu
from jax.sharding import PartitionSpec as P

D = 256
HEADS = 4
CAPS = 4
ITERS = 3
FIRST = (5, 8)
BLOCK = 8
STEPS = (5, 3)
TABLE_PARTS = 4
GROUP = 4
F32 = jnp.float32
BF16 = jnp.bfloat16


def in_hbm(*arrays):
    return tuple(pltpu.with_memory_space_constraint(a, pltpu.HBM) for a in arrays)


def lookup_kernel(
    core_ref, ids_hbm, feat_hbm, table_hbm, out_hbm, ids, feat, table, wide, out, id_sem, feat_sem, table_sem, out_sem,
    *, start, per_pair, per_core,
):
    pairs, users, spots, _ = feat.shape
    offset = core_ref[0] * per_core + start
    rows = table.shape[0] // TABLE_PARTS
    fetch_ids = pltpu.make_async_copy(ids_hbm, ids, id_sem)
    fetch_ids.start()
    fetch_table = []
    for i in range(TABLE_PARTS):
        at = pl.ds(i * rows, rows)
        fetch_table.append(pltpu.make_async_copy(table_hbm.at[at], table.at[at], table_sem.at[i]))
        fetch_table[-1].start()
    fetch_feat = []
    for d in range(pairs):
        at = pl.ds(d * per_pair + offset, users)
        fetch_feat.append(pltpu.make_async_copy(feat_hbm.at[at], feat.at[d], feat_sem.at[d]))
        fetch_feat[-1].start()
    for i in range(TABLE_PARTS):
        fetch_table[i].wait()

        def widen(j, carry, i=i):
            at = pl.ds(pl.multiple_of(i * rows + j * 128, 128), 128)
            wide[at, :] = table[at, :].astype(F32)
            return carry

        lax.fori_loop(0, rows // 128, widen, 0)
    fetch_ids.wait()
    spot = lax.broadcasted_iota(jnp.int32, (spots, D), 0)
    send = []
    for d in range(pairs):
        fetch_feat[d].wait()
        first = d * per_pair + offset

        def one(user, carry, d=d, first=first):
            rows = jnp.broadcast_to(wide[pl.ds(ids[0, first + user], 1), :], (spots, D))
            for p in range(1, spots):
                row = jnp.broadcast_to(wide[pl.ds(ids[p, first + user], 1), :], (spots, D))
                rows = jnp.where(spot == p, row, rows)
            out[d, user] = (feat[d, user].astype(F32) + rows).astype(BF16)
            return carry

        lax.fori_loop(0, users, one, 0, unroll=8)
        send.append(
            pltpu.make_async_copy(out.at[d], out_hbm.at[pl.ds(d * users, users)], out_sem.at[d])
        )
        send[-1].start()
    for copy in send:
        copy.wait()


def lookup(core, ids, features, table, start, users, pa_count, dev_count):
    all_users, spots, width = features.shape
    per_pair = all_users // pa_count
    per_core = per_pair // dev_count
    block = (pa_count, users, spots, width)
    hbm = pl.BlockSpec(memory_space=pltpu.HBM)
    return pl.pallas_call(
        functools.partial(lookup_kernel, start=start, per_pair=per_pair, per_core=per_core),
        out_shape=pltpu.HBM((pa_count * users, spots, width), BF16),
        in_specs=[pl.BlockSpec(memory_space=pltpu.SMEM), hbm, hbm, hbm],
        out_specs=hbm,
        scratch_shapes=[
            pltpu.SMEM(ids.shape, jnp.int32),
            pltpu.VMEM(block, BF16),
            pltpu.VMEM(table.shape, BF16),
            pltpu.VMEM(table.shape, F32),
            pltpu.VMEM(block, BF16),
            pltpu.SemaphoreType.DMA,
            pltpu.SemaphoreType.DMA((pa_count,)),
            pltpu.SemaphoreType.DMA((TABLE_PARTS,)),
            pltpu.SemaphoreType.DMA((pa_count,)),
        ],
        compiler_params=pltpu.CompilerParams(vmem_limit_bytes=24 << 20),
        name="lookup",
    )(core, *in_hbm(ids, features, table))


def weights_kernel(
    core_ref, qkv_a, qkv_b, out_a, out_b, bil_a, bil_b, up_a, up_b, down_a, down_b, qkv, up, tail
):
    half = D // 2
    for i in range(3):
        qkv[:, i * D : i * D + half] = qkv_a[i]
        qkv[:, i * D + half : (i + 1) * D] = qkv_b[i]
    ff = up_a.shape[1]
    up[:, :ff] = up_a[...]
    up[:, ff:] = up_b[...]

    @pl.when(core_ref[0] == 0)
    def _():
        tail[:D, :half] = bil_a[...]
        tail[:D, half:] = bil_b[...]

    @pl.when(core_ref[0] != 0)
    def _():
        tail[:D, :half] = bil_b[...]
        tail[:D, half:] = bil_a[...]

    tail[D : D + half, :] = out_a[...]
    tail[D + half : 2 * D, :] = out_b[...]
    tail[2 * D : 2 * D + ff, :] = down_a[...]
    tail[2 * D + ff :, :] = down_b[...]


def finish_weights(core, own, other):
    ff = own[3].shape[1]
    operands = [w for pair in zip(own, other) for w in pair]
    return pl.pallas_call(
        weights_kernel,
        out_shape=[
            pltpu.VMEM((D, 3 * D), BF16),
            pltpu.VMEM((D, 2 * ff), BF16),
            pltpu.VMEM((2 * D + 2 * ff, D), BF16),
        ],
        in_specs=[pl.BlockSpec(memory_space=pltpu.SMEM)]
        + [pl.BlockSpec(memory_space=pltpu.VMEM)] * len(operands),
        out_specs=[pl.BlockSpec(memory_space=pltpu.VMEM)] * 3,
        compiler_params=pltpu.CompilerParams(vmem_limit_bytes=16 << 20),
        name="weights",
    )(core, *in_hbm(*operands))


def split(x):
    high = x.astype(BF16)
    return jnp.concatenate([high, (x - high.astype(F32)).astype(BF16)], axis=0)


def joined(x):
    half = x.shape[0] // 2
    return x[:half] + x[half:]


def encode_kernel(core_ref, x_ref, lens_ref, seed_ref, qkv_ref, up_ref, tail_ref, own_ref, other_ref, interest_ref, *, steps):
    step = pl.program_id(0)
    pairs, all_users, spots, _ = x_ref.shape
    block = all_users // steps
    history = pairs * spots
    rows = block * history
    head = D // HEADS
    lanes = HEADS * history
    x = x_ref[:, pl.ds(step * block, block)].astype(F32)
    x = jnp.swapaxes(x, 0, 1).reshape(rows, D).astype(BF16)
    qkv = jnp.dot(x, qkv_ref[...], preferred_element_type=F32)
    queries = (qkv[:, :D] * (1.0 / head**0.5)).astype(BF16)
    keys = qkv[:, D : 2 * D].astype(BF16)
    values = qkv[:, 2 * D :].astype(BF16)

    lane_head = lax.broadcasted_iota(jnp.int32, (history, D), 1) // head
    own_head = [(lane_head == h).astype(F32).astype(BF16) for h in range(HEADS)]
    row_head = lax.broadcasted_iota(jnp.int32, (lanes, D), 0) // history
    col_head = lax.broadcasted_iota(jnp.int32, (lanes, D), 1) // head
    ones = (row_head == col_head).astype(F32).astype(BF16)
    position = lax.broadcasted_iota(jnp.int32, (block, lanes), 1) % history
    lens = lens_ref[pl.ds(pl.multiple_of(step * block, BLOCK), block), :]
    key_valid = (position < lens).astype(F32)
    users = [slice(u * history, (u + 1) * history) for u in range(block)]
    scores = []
    for at in users:
        key_wide = jnp.concatenate([keys[at] * m for m in own_head], axis=0)
        scores.append(
            lax.dot_general(
                queries[at], key_wide, (((1,), (1,)), ((), ())), preferred_element_type=F32
            )
        )
    rounded = [
        jnp.where(key_valid[u : u + 1] > 0.0, jnp.exp(s), 0.0).astype(BF16)
        for u, s in enumerate(scores)
    ]
    totals = jnp.dot(jnp.concatenate(rounded, axis=0), ones, preferred_element_type=F32)
    weighted = []
    for at, r in zip(users, rounded):
        value_wide = jnp.concatenate([values[at] * m for m in own_head], axis=0)
        weighted.append(jnp.dot(r, value_wide, preferred_element_type=F32))
    attended = (jnp.concatenate(weighted, axis=0) / totals).astype(BF16)
    hidden = jax.nn.gelu(jnp.dot(x, up_ref[...], preferred_element_type=F32)).astype(BF16)
    everything = jnp.concatenate([x, attended, hidden], axis=1)
    interest = jnp.dot(everything, tail_ref[...], preferred_element_type=F32).astype(BF16)
    interest_ref[pl.ds(pl.multiple_of(step * rows, rows), rows), :] = interest

    @pl.when(step == steps - 1)
    def _():
        route(core_ref, lens_ref, seed_ref, own_ref, other_ref, interest_ref, history)


def route(core_ref, lens_ref, seed_ref, own_ref, other_ref, interest_ref, history):
    lanes = GROUP * history
    groups = BLOCK // GROUP
    blocks = range(interest_ref.shape[0] // (BLOCK * history))
    lane = lax.broadcasted_iota(jnp.int32, (BLOCK, lanes), 1)
    user = lax.broadcasted_iota(jnp.int32, (BLOCK, lanes), 0)
    mine = (lane // history) == (user % GROUP)
    in_group = [(user // GROUP) == g for g in range(groups)]
    base = (seed_ref[...].astype(F32) - 7.5) * 0.25
    base = jnp.concatenate([base] * GROUP, axis=1)
    base = jnp.broadcast_to(base[:, None, :], (CAPS, BLOCK, lanes))
    logits = [base for _ in blocks]
    valid = []
    for b in blocks:
        real = mine & ((lane % history) < lens_ref[b * BLOCK : (b + 1) * BLOCK, :])
        valid.append([(real & here).astype(F32)[None] for here in in_group])

    def vectors(b, g):
        return interest_ref[(b * groups + g) * lanes : (b * groups + g + 1) * lanes, :]

    def softmax(x):
        weights = jnp.exp(x - jnp.max(x, axis=0, keepdims=True))
        return weights / jnp.sum(weights, axis=0, keepdims=True)

    def parts(weights, b):
        return [split((weights * v).reshape(CAPS * BLOCK, lanes)) for v in valid[b]]

    def squash(summed):
        squares = jnp.sum(summed * summed, axis=1, keepdims=True)
        return summed * (jnp.sqrt(squares) / (1.0 + squares))

    for sweep in range(ITERS):
        if sweep == 0:
            weights = [softmax(base)] * len(logits)
        else:
            weights = [softmax(x) for x in logits]
        weighted = [parts(weights[b], b) for b in blocks]
        summed = [
            joined(
                sum(
                    jnp.dot(weighted[b][g], vectors(b, g), preferred_element_type=F32)
                    for g in range(groups)
                )
            )
            for b in blocks
        ]
        capsules = [squash(x) for x in summed]
        if sweep + 1 < ITERS:
            caps = [split(x) for x in capsules]
            near = [
                [
                    lax.dot_general(
                        caps[b], vectors(b, g), (((1,), (1,)), ((), ())), preferred_element_type=F32
                    )
                    for g in range(groups)
                ]
                for b in blocks
            ]
            for b in blocks:
                added = [joined(x).reshape(CAPS, BLOCK, lanes) for x in near[b]]
                chosen = added[-1]
                for g in range(groups - 1):
                    chosen = jnp.where(in_group[g][None], added[g], chosen)
                logits[b] = logits[b] + chosen
    half = D // 2
    low_own = core_ref[0] == 0
    for b in blocks:
        made = capsules[b].reshape(CAPS, BLOCK, D)
        low, high = made[:, :, :half], made[:, :, half:]
        kept, passed = jnp.where(low_own, low, high), jnp.where(low_own, high, low)
        for j in range(CAPS):
            own_ref[b * BLOCK : (b + 1) * BLOCK, j, :] = kept[j]
            other_ref[b * BLOCK : (b + 1) * BLOCK, j, :] = passed[j]


def encode(core, gathered, lens, seed, qkv, up, tail, steps):
    pa_count, users, spots, _ = gathered.shape
    vmem = pl.BlockSpec(memory_space=pltpu.VMEM)
    made = jax.ShapeDtypeStruct((users, CAPS, D // 2), F32)
    return pl.pallas_call(
        functools.partial(encode_kernel, steps=steps),
        out_shape=[made, made],
        grid=(steps,),
        in_specs=[pl.BlockSpec(memory_space=pltpu.SMEM)] + [vmem] * 6,
        out_specs=[vmem] * 2,
        scratch_shapes=[pltpu.VMEM((users * pa_count * spots, D), BF16)],
        compiler_params=pltpu.CompilerParams(vmem_limit_bytes=40 << 20),
        name="encode",
    )(core, gathered, lens, seed, qkv, up, tail)


def body(
    features, item_ids, item_table, lengths, routing_seed, w_qkv, w_out, w_bilinear, w_up, w_down
):
    pa_count = lax.axis_size("pa")
    dev_count = lax.axis_size("dev")
    spots = features.shape[1]
    per_core = lengths.shape[0] // (pa_count * dev_count)
    core_index = lax.axis_index("dev").astype(jnp.int32)
    core = core_index.reshape(1)
    swap = [(i, dev_count - 1 - i) for i in range(dev_count)]
    own = (w_qkv, w_out, w_bilinear, w_up, w_down)
    other = tuple(lax.ppermute(w, "dev", swap) for w in own)
    qkv, up, tail = finish_weights(core, own, other)
    first = (lax.axis_index("pa") * dev_count + core_index) * per_core
    lens = lax.dynamic_slice_in_dim(lengths, first, per_core).reshape(per_core, 1)
    ids = item_ids.T
    cut = per_core * FIRST[0] // FIRST[1]
    halves = []
    for start, users, steps in ((0, cut, STEPS[0]), (cut, per_core - cut, STEPS[1])):
        if start:
            ids, qkv, up, tail = lax.optimization_barrier((ids, qkv, up, tail))
        sent = lookup(core, ids, features, item_table, start, users, pa_count, dev_count)
        got = lax.all_to_all(sent, "pa", split_axis=0, concat_axis=0, tiled=True)
        got = got.reshape(pa_count, users, spots, D)
        kept, passed = encode(
            core, got, lens[start : start + users], routing_seed, qkv, up, tail, steps
        )
        halves.append((kept, lax.ppermute(passed, "dev", swap)))
    kept = jnp.concatenate([h[0] for h in halves], axis=0)
    came = jnp.concatenate([h[1] for h in halves], axis=0)
    return jnp.where(
        core_index == 0,
        jnp.concatenate([kept, came], axis=0),
        jnp.concatenate([came, kept], axis=0),
    )


def solution(mesh):
    in_specs = (
        P("au", "pa", None),
        P("au", "pa"),
        P(),
        P("au"),
        P(),
        P(None, None, "dev"),
        P("dev", None),
        P(None, "dev"),
        P(None, "dev"),
        P("dev", None),
    )
    out_specs = P(("au", "pa"), None, "dev")
    return jax.shard_map(body, mesh=mesh, in_specs=in_specs, out_specs=out_specs, check_vma=False)
```

```python
import functools

import jax
import jax.numpy as jnp
from jax import lax
from jax.experimental import pallas as pl
from jax.experimental.pallas import tpu as pltpu
from jax.sharding import PartitionSpec as P

D = 256
HEADS = 4
FF = 1024
CAPS = 4
ITERS = 3
FIRST = (5, 8)
BLOCK = 8
STEPS = (2, 2)
TABLE_PARTS = 4
GROUP = 4
F32 = jnp.float32
BF16 = jnp.bfloat16


def in_hbm(*arrays):
    return tuple(pltpu.with_memory_space_constraint(a, pltpu.HBM) for a in arrays)


def lookup_kernel(
    core_ref, ids_hbm, feat_hbm, table_hbm, out_hbm, ids, feat, table, wide, out, id_sem, feat_sem, table_sem, out_sem,
    *, start, per_pair, per_core,
):
    pairs, users, spots, _ = feat.shape
    offset = core_ref[0] * per_core + start
    rows = table.shape[0] // TABLE_PARTS
    fetch_ids = pltpu.make_async_copy(ids_hbm, ids, id_sem)
    fetch_ids.start()
    fetch_table = []
    for i in range(TABLE_PARTS):
        at = pl.ds(i * rows, rows)
        fetch_table.append(pltpu.make_async_copy(table_hbm.at[at], table.at[at], table_sem.at[i]))
        fetch_table[-1].start()
    fetch_feat = []
    for d in range(pairs):
        at = pl.ds(d * per_pair + offset, users)
        fetch_feat.append(pltpu.make_async_copy(feat_hbm.at[at], feat.at[d], feat_sem.at[d]))
        fetch_feat[-1].start()
    for i in range(TABLE_PARTS):
        fetch_table[i].wait()

        def widen(j, carry, i=i):
            at = pl.ds(pl.multiple_of(i * rows + j * 128, 128), 128)
            for h in range(2):
                wide[h, at, :] = table[at, h * (D // 2) : (h + 1) * (D // 2)].astype(F32)
            return carry

        lax.fori_loop(0, rows // 128, widen, 0)
    fetch_ids.wait()
    spot = lax.broadcasted_iota(jnp.int32, (spots, D // 2), 0)
    send = []
    for d in range(pairs):
        fetch_feat[d].wait()
        first = d * per_pair + offset

        def one(user, carry, d=d, first=first):
            halves = [None, None]
            for p in range(spots):
                at = pl.ds(ids[p, first + user], 1)
                for h in range(2):
                    row = jnp.broadcast_to(wide[h, at, :], (spots, D // 2))
                    halves[h] = row if p == 0 else jnp.where(spot == p, row, halves[h])
            rows = jnp.concatenate(halves, axis=1)
            out[d, user] = (feat[d, user].astype(F32) + rows).astype(BF16)
            return carry

        lax.fori_loop(0, users, one, 0, unroll=8)
        send.append(
            pltpu.make_async_copy(out.at[d], out_hbm.at[pl.ds(d * users, users)], out_sem.at[d])
        )
        send[-1].start()
    for copy in send:
        copy.wait()


def lookup(core, ids, features, table, start, users, pa_count, dev_count):
    all_users, spots, width = features.shape
    per_pair = all_users // pa_count
    per_core = per_pair // dev_count
    block = (pa_count, users, spots, width)
    hbm = pl.BlockSpec(memory_space=pltpu.HBM)
    return pl.pallas_call(
        functools.partial(lookup_kernel, start=start, per_pair=per_pair, per_core=per_core),
        out_shape=pltpu.HBM((pa_count * users, spots, width), BF16),
        in_specs=[pl.BlockSpec(memory_space=pltpu.SMEM), hbm, hbm, hbm],
        out_specs=hbm,
        scratch_shapes=[
            pltpu.SMEM(ids.shape, jnp.int32),
            pltpu.VMEM(block, BF16),
            pltpu.VMEM(table.shape, BF16),
            pltpu.VMEM((2, table.shape[0], D // 2), F32),
            pltpu.VMEM(block, BF16),
            pltpu.SemaphoreType.DMA,
            pltpu.SemaphoreType.DMA((pa_count,)),
            pltpu.SemaphoreType.DMA((TABLE_PARTS,)),
            pltpu.SemaphoreType.DMA((pa_count,)),
        ],
        compiler_params=pltpu.CompilerParams(vmem_limit_bytes=12 << 20),
        name="lookup",
    )(core, *in_hbm(ids, features, table))


def weights_kernel(
    core_ref, qkv_a, qkv_b, out_a, out_b, bil_a, bil_b, up_a, up_b, down_a, down_b, all_ref
):
    half = D // 2
    at = 0
    for i in range(3):
        all_ref[at : at + D, :half] = qkv_a[i]
        all_ref[at : at + D, half:] = qkv_b[i]
        at += D
    for up in (up_a, up_b):
        for i in range(up.shape[1] // D):
            all_ref[at : at + D, :] = up[:, i * D : (i + 1) * D]
            at += D

    @pl.when(core_ref[0] == 0)
    def _():
        all_ref[at : at + D, :half] = bil_a[...]
        all_ref[at : at + D, half:] = bil_b[...]

    @pl.when(core_ref[0] != 0)
    def _():
        all_ref[at : at + D, :half] = bil_b[...]
        all_ref[at : at + D, half:] = bil_a[...]

    after = at + D
    for rows in (out_a, out_b, down_a, down_b):
        all_ref[after : after + rows.shape[0], :] = rows[...]
        after += rows.shape[0]


def finish_weights(core, own, other):
    ff = own[3].shape[1]
    operands = [w for pair in zip(own, other) for w in pair]
    return pl.pallas_call(
        weights_kernel,
        out_shape=pltpu.VMEM((5 * D + 4 * ff, D), BF16),
        in_specs=[pl.BlockSpec(memory_space=pltpu.SMEM)]
        + [pl.BlockSpec(memory_space=pltpu.VMEM)] * len(operands),
        out_specs=pl.BlockSpec(memory_space=pltpu.VMEM),
        compiler_params=pltpu.CompilerParams(vmem_limit_bytes=8 << 20),
        name="weights",
    )(core, *in_hbm(*operands))


def split(x):
    high = x.astype(BF16)
    return jnp.concatenate([high, (x - high.astype(F32)).astype(BF16)], axis=0)


def joined(x):
    half = x.shape[0] // 2
    return x[:half] + x[half:]


def encode_kernel(core_ref, x_ref, lens_ref, seed_ref, w_ref, own_ref, other_ref, interest_ref, *, steps):
    step = pl.program_id(0)
    pairs, all_users, spots, _ = x_ref.shape
    block = all_users // steps
    history = pairs * spots
    rows = block * history
    head = D // HEADS
    lanes = HEADS * history
    x = x_ref[:, pl.ds(step * block, block)].astype(F32)
    x = jnp.swapaxes(x, 0, 1).reshape(rows, D).astype(BF16)

    def through(i):
        return jnp.dot(x, w_ref[i * D : (i + 1) * D, :], preferred_element_type=F32)

    queries = (through(0) * (1.0 / head**0.5)).astype(BF16)
    keys = through(1).astype(BF16)
    values = through(2).astype(BF16)

    lane_head = lax.broadcasted_iota(jnp.int32, (history, D), 1) // head
    own_head = [(lane_head == h).astype(F32).astype(BF16) for h in range(HEADS)]
    odd_even = [own_head[0] + own_head[2], own_head[1] + own_head[3]]
    row_head = lax.broadcasted_iota(jnp.int32, (lanes, D), 0) // history
    col_head = lax.broadcasted_iota(jnp.int32, (lanes, D), 1) // head
    ones = (row_head == col_head).astype(F32).astype(BF16)
    position = lax.broadcasted_iota(jnp.int32, (block, lanes), 1) % history
    lens = lens_ref[pl.ds(step * block, block), :]
    key_valid = (position < lens).astype(F32)
    users = [slice(u * history, (u + 1) * history) for u in range(block)]
    scores = []
    none = jnp.zeros((history, D // 2), BF16)
    for first in range(0, block, 2):
        pair = users[first : first + 2]
        key_wide = jnp.concatenate([keys[at] * m for at in pair for m in odd_even], axis=0)
        query_wide = jnp.concatenate(
            [
                part
                for at in pair
                for part in (
                    jnp.concatenate([queries[at, : D // 2], none], axis=1),
                    jnp.concatenate([none, queries[at, D // 2 :]], axis=1),
                )
            ],
            axis=0,
        )
        both = lax.dot_general(
            query_wide, key_wide, (((1,), (1,)), ((), ())), preferred_element_type=F32
        )
        for u in range(2):
            rows_u = both[u * D // 2 : (u + 1) * D // 2, u * D // 2 : (u + 1) * D // 2]
            scores.append(jnp.concatenate([rows_u[:history], rows_u[history:]], axis=1))
    rounded = [
        jnp.where(key_valid[u : u + 1] > 0.0, jnp.exp(s), 0.0).astype(BF16)
        for u, s in enumerate(scores)
    ]
    totals = jnp.dot(jnp.concatenate(rounded, axis=0), ones, preferred_element_type=F32)
    weighted = []
    for first in range(0, block, 2):
        pair = users[first : first + 2]
        value_wide = jnp.concatenate([values[at] * m for at in pair for m in odd_even], axis=0)
        prob_wide = []
        for u in range(2):
            for g in range(2):
                part = rounded[first + u][:, g * D // 2 : (g + 1) * D // 2]
                prob_wide.append(jnp.concatenate([part, none] if u == 0 else [none, part], axis=1))
        both = jnp.dot(jnp.concatenate(prob_wide, axis=0), value_wide, preferred_element_type=F32)
        for u in range(2):
            rows_u = both[u * D // 2 : (u + 1) * D // 2]
            weighted.append(
                jnp.concatenate([rows_u[:history, : D // 2], rows_u[history:, D // 2 :]], axis=1)
            )
    attended = (jnp.concatenate(weighted, axis=0) / totals).astype(BF16)
    tail = 3 + FF // D
    hidden = [jax.nn.gelu(through(i)).astype(BF16) for i in range(3, tail)]
    everything = jnp.concatenate([x, attended] + hidden, axis=1)
    interest = jnp.dot(everything, w_ref[tail * D :, :], preferred_element_type=F32).astype(BF16)
    interest_ref[pl.ds(pl.multiple_of(step * rows, rows), rows), :] = interest

    @pl.when(step == steps - 1)
    def _():
        route(core_ref, lens_ref, seed_ref, own_ref, other_ref, interest_ref, history)


def route(core_ref, lens_ref, seed_ref, own_ref, other_ref, interest_ref, history):
    lanes = GROUP * history
    groups = BLOCK // GROUP
    blocks = range(interest_ref.shape[0] // (BLOCK * history))
    lane = lax.broadcasted_iota(jnp.int32, (BLOCK, lanes), 1)
    user = lax.broadcasted_iota(jnp.int32, (BLOCK, lanes), 0)
    mine = (lane // history) == (user % GROUP)
    in_group = [(user // GROUP) == g for g in range(groups)]
    base = (seed_ref[...].astype(F32) - 7.5) * 0.25
    base = jnp.concatenate([base] * GROUP, axis=1)
    base = jnp.broadcast_to(base[:, None, :], (CAPS, BLOCK, lanes))
    logits = [base for _ in blocks]
    valid = []
    for b in blocks:
        real = mine & ((lane % history) < lens_ref[b * BLOCK : (b + 1) * BLOCK, :])
        valid.append([(real & here).astype(F32)[None] for here in in_group])

    def vectors(b, g):
        return interest_ref[(b * groups + g) * lanes : (b * groups + g + 1) * lanes, :]

    def softmax(x):
        weights = jnp.exp(x - jnp.max(x, axis=0, keepdims=True))
        return weights / jnp.sum(weights, axis=0, keepdims=True)

    def parts(weights, b):
        return [split((weights * v).reshape(CAPS * BLOCK, lanes)) for v in valid[b]]

    def squash(summed):
        squares = jnp.sum(summed * summed, axis=1, keepdims=True)
        return summed * (jnp.sqrt(squares) / (1.0 + squares))

    for sweep in range(ITERS):
        if sweep == 0:
            weights = [softmax(base)] * len(logits)
        else:
            weights = [softmax(x) for x in logits]
        weighted = [parts(weights[b], b) for b in blocks]
        summed = [
            joined(
                sum(
                    jnp.dot(weighted[b][g], vectors(b, g), preferred_element_type=F32)
                    for g in range(groups)
                )
            )
            for b in blocks
        ]
        capsules = [squash(x) for x in summed]
        if sweep + 1 < ITERS:
            caps = [split(x) for x in capsules]
            near = [
                [
                    lax.dot_general(
                        caps[b], vectors(b, g), (((1,), (1,)), ((), ())), preferred_element_type=F32
                    )
                    for g in range(groups)
                ]
                for b in blocks
            ]
            for b in blocks:
                added = [joined(x).reshape(CAPS, BLOCK, lanes) for x in near[b]]
                chosen = added[-1]
                for g in range(groups - 1):
                    chosen = jnp.where(in_group[g][None], added[g], chosen)
                logits[b] = logits[b] + chosen
    half = D // 2
    low_own = core_ref[0] == 0
    for b in blocks:
        made = capsules[b].reshape(CAPS, BLOCK, D)
        low, high = made[:, :, :half], made[:, :, half:]
        kept, passed = jnp.where(low_own, low, high), jnp.where(low_own, high, low)
        for j in range(CAPS):
            own_ref[b * BLOCK : (b + 1) * BLOCK, j, :] = kept[j]
            other_ref[b * BLOCK : (b + 1) * BLOCK, j, :] = passed[j]


def encode(core, gathered, lens, seed, weights, steps):
    pa_count, users, spots, _ = gathered.shape
    vmem = pl.BlockSpec(memory_space=pltpu.VMEM)
    made = jax.ShapeDtypeStruct((users, CAPS, D // 2), F32)
    return pl.pallas_call(
        functools.partial(encode_kernel, steps=steps),
        out_shape=[made, made],
        grid=(steps,),
        in_specs=[pl.BlockSpec(memory_space=pltpu.SMEM)] + [vmem] * 4,
        out_specs=[vmem] * 2,
        scratch_shapes=[pltpu.VMEM((users * pa_count * spots, D), BF16)],
        compiler_params=pltpu.CompilerParams(vmem_limit_bytes=24 << 20),
        name="encode",
    )(core, gathered, lens, seed, weights)


def body(
    features, item_ids, item_table, lengths, routing_seed, w_qkv, w_out, w_bilinear, w_up, w_down
):
    pa_count = lax.axis_size("pa")
    dev_count = lax.axis_size("dev")
    spots = features.shape[1]
    per_core = lengths.shape[0] // (pa_count * dev_count)
    core_index = lax.axis_index("dev").astype(jnp.int32)
    core = core_index.reshape(1)
    swap = [(i, dev_count - 1 - i) for i in range(dev_count)]
    own = (w_qkv, w_out, w_bilinear, w_up, w_down)
    other = tuple(lax.ppermute(w, "dev", swap) for w in own)
    weights = finish_weights(core, own, other)
    first = (lax.axis_index("pa") * dev_count + core_index) * per_core
    lens = lax.dynamic_slice_in_dim(lengths, first, per_core).reshape(per_core, 1)
    cut = per_core * FIRST[0] // FIRST[1]
    lens = [lens[:cut], lens[cut:]]
    ids = item_ids.T
    halves = []
    for start, users, steps in ((0, cut, STEPS[0]), (cut, per_core - cut, STEPS[1])):
        if start:
            ids, weights, lens = lax.optimization_barrier((ids, weights, lens))
        sent = lookup(core, ids, features, item_table, start, users, pa_count, dev_count)
        got = lax.all_to_all(sent, "pa", split_axis=0, concat_axis=0, tiled=True)
        got = got.reshape(pa_count, users, spots, D)
        kept, passed = encode(
            core, got, lens[int(start > 0)], routing_seed, weights, steps
        )
        halves.append((kept, lax.ppermute(passed, "dev", swap)))
    kept = jnp.concatenate([h[0] for h in halves], axis=0)
    came = jnp.concatenate([h[1] for h in halves], axis=0)
    return jnp.where(
        core_index == 0,
        jnp.concatenate([kept, came], axis=0),
        jnp.concatenate([came, kept], axis=0),
    )


def solution(mesh):
    in_specs = (
        P("au", "pa", None),
        P("au", "pa"),
        P(),
        P("au"),
        P(),
        P(None, None, "dev"),
        P("dev", None),
        P(None, "dev"),
        P(None, "dev"),
        P("dev", None),
    )
    out_specs = P(("au", "pa"), None, "dev")
    return jax.shard_map(body, mesh=mesh, in_specs=in_specs, out_specs=out_specs, check_vma=False)
```

```python
import functools

import jax
import jax.numpy as jnp
from jax import lax
from jax.experimental import pallas as pl
from jax.experimental.pallas import tpu as pltpu
from jax.sharding import PartitionSpec as P

D = 256
HEADS = 4
FF = 1024
CAPS = 4
ITERS = 3
FIRST = (5, 8)
BLOCK = 8
STEPS = (2, 2)
TABLE_PARTS = 4
AHEAD = 5
Z_LO = 2
GROUP = 4
F32 = jnp.float32
BF16 = jnp.bfloat16


def in_hbm(*arrays):
    return tuple(pltpu.with_memory_space_constraint(a, pltpu.HBM) for a in arrays)


def lookup_kernel(
    core_ref, to_ref, ids_hbm, feat_hbm, table_hbm, *refs, start, per_pair, per_core
):
    out_hbm, scratch = refs[:-9], refs[-9:]
    ids, feat, table, wide, out, id_sem, feat_sem, table_sem, out_sem = scratch
    pairs, users, spots, _ = feat.shape
    offset = core_ref[0] * per_core + start
    rows = table.shape[0] // TABLE_PARTS
    fetch_ids = pltpu.make_async_copy(ids_hbm, ids, id_sem)
    fetch_ids.start()
    fetch_table = []
    for i in range(TABLE_PARTS):
        at = pl.ds(i * rows, rows)
        fetch_table.append(pltpu.make_async_copy(table_hbm.at[at], table.at[at], table_sem.at[i]))
        fetch_table[-1].start()
    fetch_feat = []
    for d in range(pairs):
        at = pl.ds(to_ref[d] * per_pair + offset, users)
        fetch_feat.append(pltpu.make_async_copy(feat_hbm.at[at], feat.at[d], feat_sem.at[d]))
        fetch_feat[-1].start()
    for i in range(TABLE_PARTS):
        fetch_table[i].wait()

        def widen(j, carry, i=i):
            at = pl.ds(pl.multiple_of(i * rows + j * 128, 128), 128)
            for h in range(2):
                wide[h, at, :] = table[at, h * (D // 2) : (h + 1) * (D // 2)].astype(F32)
            return carry

        lax.fori_loop(0, rows // 128, widen, 0)
    fetch_ids.wait()
    spot = lax.broadcasted_iota(jnp.int32, (spots, D // 2), 0)
    send = []
    for d in range(pairs):
        fetch_feat[d].wait()
        first = to_ref[d] * per_pair + offset

        def one(user, carry, d=d, first=first):
            halves = [None, None]
            for p in range(spots):
                at = pl.ds(ids[p, first + user], 1)
                for h in range(2):
                    row = jnp.broadcast_to(wide[h, at, :], (spots, D // 2))
                    halves[h] = row if p == 0 else jnp.where(spot == p, row, halves[h])
            rows = jnp.concatenate(halves, axis=1)
            out[d, user] = (feat[d, user].astype(F32) + rows).astype(BF16)
            return carry

        lax.fori_loop(0, users, one, 0, unroll=8)
        if len(out_hbm) == pairs:
            target = out_hbm[d]
        else:
            target = out_hbm[0].at[pl.ds(d * users, users)]
        send.append(pltpu.make_async_copy(out.at[d], target, out_sem.at[d]))
        send[-1].start()
    for copy in send:
        copy.wait()


def lookup(core, to, ids, features, table, start, users, pa_count, dev_count, apart):
    all_users, spots, width = features.shape
    per_pair = all_users // pa_count
    per_core = per_pair // dev_count
    block = (pa_count, users, spots, width)
    hbm = pl.BlockSpec(memory_space=pltpu.HBM)
    outs = pa_count if apart else 1
    return pl.pallas_call(
        functools.partial(lookup_kernel, start=start, per_pair=per_pair, per_core=per_core),
        out_shape=[pltpu.HBM((users * (1 if apart else pa_count), spots, width), BF16)] * outs,
        in_specs=[pl.BlockSpec(memory_space=pltpu.SMEM)] * 2 + [hbm, hbm, hbm],
        out_specs=[hbm] * outs,
        scratch_shapes=[
            pltpu.SMEM(ids.shape, jnp.int32),
            pltpu.VMEM(block, BF16),
            pltpu.VMEM(table.shape, BF16),
            pltpu.VMEM((2, table.shape[0], D // 2), F32),
            pltpu.VMEM(block, BF16),
            pltpu.SemaphoreType.DMA,
            pltpu.SemaphoreType.DMA((pa_count,)),
            pltpu.SemaphoreType.DMA((TABLE_PARTS,)),
            pltpu.SemaphoreType.DMA((pa_count,)),
        ],
        compiler_params=pltpu.CompilerParams(vmem_limit_bytes=12 << 20),
        name="lookup",
    )(core, to, *in_hbm(ids, features, table))


def weights_kernel(
    core_ref, qkv_a, qkv_b, out_a, out_b, bil_a, bil_b, up_a, up_b, down_a, down_b, all_ref
):
    half = D // 2
    at = 0
    for i in range(3):
        all_ref[at : at + D, :half] = qkv_a[i]
        all_ref[at : at + D, half:] = qkv_b[i]
        at += D
    for up in (up_a, up_b):
        for i in range(up.shape[1] // D):
            all_ref[at : at + D, :] = up[:, i * D : (i + 1) * D]
            at += D

    @pl.when(core_ref[0] == 0)
    def _():
        all_ref[at : at + D, :half] = bil_a[...]
        all_ref[at : at + D, half:] = bil_b[...]

    @pl.when(core_ref[0] != 0)
    def _():
        all_ref[at : at + D, :half] = bil_b[...]
        all_ref[at : at + D, half:] = bil_a[...]

    after = at + D
    for rows in (out_a, out_b, down_a, down_b):
        all_ref[after : after + rows.shape[0], :] = rows[...]
        after += rows.shape[0]


def finish_weights(core, own, other):
    ff = own[3].shape[1]
    operands = [w for pair in zip(own, other) for w in pair]
    return pl.pallas_call(
        weights_kernel,
        out_shape=pltpu.VMEM((5 * D + 4 * ff, D), BF16),
        in_specs=[pl.BlockSpec(memory_space=pltpu.SMEM)]
        + [pl.BlockSpec(memory_space=pltpu.VMEM)] * len(operands),
        out_specs=pl.BlockSpec(memory_space=pltpu.VMEM),
        compiler_params=pltpu.CompilerParams(vmem_limit_bytes=8 << 20),
        name="weights",
    )(core, *in_hbm(*operands))


def split(x):
    high = x.astype(BF16)
    return jnp.concatenate([high, (x - high.astype(F32)).astype(BF16)], axis=0)


def joined(x):
    half = x.shape[0] // 2
    return x[:half] + x[half:]


def encode_kernel(core_ref, from_ref, *refs, steps):
    parts = refs[:-7]
    lens_ref, seed_ref, w_ref, own_ref, other_ref, interest_ref, x_ref = refs[-7:]
    step = pl.program_id(0)
    if len(parts) == 1:
        x_ref = parts[0]
    else:

        @pl.when(step == 0)
        def _():
            for i, part in enumerate(parts):
                x_ref[from_ref[i]] = part[...]

    pairs, all_users, spots, _ = x_ref.shape
    block = all_users // steps
    history = pairs * spots
    rows = block * history
    head = D // HEADS
    lanes = HEADS * history
    x = x_ref[:, pl.ds(step * block, block)].astype(F32)
    x = jnp.swapaxes(x, 0, 1).reshape(rows, D).astype(BF16)

    def through(i):
        return jnp.dot(x, w_ref[i * D : (i + 1) * D, :], preferred_element_type=F32)

    queries = (through(0) * (1.0 / head**0.5)).astype(BF16)
    keys = through(1).astype(BF16)
    values = through(2).astype(BF16)

    lane_head = lax.broadcasted_iota(jnp.int32, (history, D), 1) // head
    own_head = [(lane_head == h).astype(F32).astype(BF16) for h in range(HEADS)]
    odd_even = [own_head[0] + own_head[2], own_head[1] + own_head[3]]
    row_head = lax.broadcasted_iota(jnp.int32, (lanes, D), 0) // history
    col_head = lax.broadcasted_iota(jnp.int32, (lanes, D), 1) // head
    ones = (row_head == col_head).astype(F32).astype(BF16)
    position = lax.broadcasted_iota(jnp.int32, (block, lanes), 1) % history
    lens = lens_ref[pl.ds(step * block, block), :]
    key_valid = (position < lens).astype(F32)
    users = [slice(u * history, (u + 1) * history) for u in range(block)]
    scores = []
    none = jnp.zeros((history, D // 2), BF16)
    for first in range(0, block, 2):
        pair = users[first : first + 2]
        key_wide = jnp.concatenate([keys[at] * m for at in pair for m in odd_even], axis=0)
        query_wide = jnp.concatenate(
            [
                part
                for at in pair
                for part in (
                    jnp.concatenate([queries[at, : D // 2], none], axis=1),
                    jnp.concatenate([none, queries[at, D // 2 :]], axis=1),
                )
            ],
            axis=0,
        )
        both = lax.dot_general(
            query_wide, key_wide, (((1,), (1,)), ((), ())), preferred_element_type=F32
        )
        for u in range(2):
            rows_u = both[u * D // 2 : (u + 1) * D // 2, u * D // 2 : (u + 1) * D // 2]
            scores.append(jnp.concatenate([rows_u[:history], rows_u[history:]], axis=1))
    rounded = [
        jnp.where(key_valid[u : u + 1] > 0.0, jnp.exp(s), 0.0).astype(BF16)
        for u, s in enumerate(scores)
    ]
    totals = jnp.dot(jnp.concatenate(rounded, axis=0), ones, preferred_element_type=F32)
    weighted = []
    for first in range(0, block, 2):
        pair = users[first : first + 2]
        value_wide = jnp.concatenate([values[at] * m for at in pair for m in odd_even], axis=0)
        prob_wide = []
        for u in range(2):
            for g in range(2):
                part = rounded[first + u][:, g * D // 2 : (g + 1) * D // 2]
                prob_wide.append(jnp.concatenate([part, none] if u == 0 else [none, part], axis=1))
        both = jnp.dot(jnp.concatenate(prob_wide, axis=0), value_wide, preferred_element_type=F32)
        for u in range(2):
            rows_u = both[u * D // 2 : (u + 1) * D // 2]
            weighted.append(
                jnp.concatenate([rows_u[:history, : D // 2], rows_u[history:, D // 2 :]], axis=1)
            )
    attended = (jnp.concatenate(weighted, axis=0) / totals).astype(BF16)
    tail = 3 + FF // D
    hidden = [jax.nn.gelu(through(i)).astype(BF16) for i in range(3, tail)]
    everything = jnp.concatenate([x, attended] + hidden, axis=1)
    interest = jnp.dot(everything, w_ref[tail * D :, :], preferred_element_type=F32).astype(BF16)
    interest_ref[pl.ds(pl.multiple_of(step * rows, rows), rows), :] = interest

    @pl.when(step == steps - 1)
    def _():
        route(core_ref, lens_ref, seed_ref, own_ref, other_ref, interest_ref, history)


def route(core_ref, lens_ref, seed_ref, own_ref, other_ref, interest_ref, history):
    lanes = GROUP * history
    groups = BLOCK // GROUP
    blocks = range(interest_ref.shape[0] // (BLOCK * history))
    lane = lax.broadcasted_iota(jnp.int32, (BLOCK, lanes), 1)
    user = lax.broadcasted_iota(jnp.int32, (BLOCK, lanes), 0)
    mine = (lane // history) == (user % GROUP)
    in_group = [(user // GROUP) == g for g in range(groups)]
    base = (seed_ref[...].astype(F32) - 7.5) * 0.25
    base = jnp.concatenate([base] * GROUP, axis=1)
    base = jnp.broadcast_to(base[:, None, :], (CAPS, BLOCK, lanes))
    logits = [base for _ in blocks]
    valid = []
    for b in blocks:
        real = mine & ((lane % history) < lens_ref[b * BLOCK : (b + 1) * BLOCK, :])
        valid.append([(real & here).astype(F32)[None] for here in in_group])

    def vectors(b, g):
        return interest_ref[(b * groups + g) * lanes : (b * groups + g + 1) * lanes, :]

    def softmax(x):
        weights = jnp.exp(x - jnp.max(x, axis=0, keepdims=True))
        return weights / jnp.sum(weights, axis=0, keepdims=True)

    def parts(weights, b):
        return [split((weights * v).reshape(CAPS * BLOCK, lanes)) for v in valid[b]]

    def squash(summed):
        squares = jnp.sum(summed * summed, axis=1, keepdims=True)
        return summed * (jnp.sqrt(squares) / (1.0 + squares))

    for sweep in range(ITERS):
        if sweep == 0:
            weights = [softmax(base)] * len(logits)
        else:
            weights = [softmax(x) for x in logits]
        weighted = [parts(weights[b], b) for b in blocks]
        summed = [
            joined(
                sum(
                    jnp.dot(weighted[b][g], vectors(b, g), preferred_element_type=F32)
                    for g in range(groups)
                )
            )
            for b in blocks
        ]
        capsules = [squash(x) for x in summed]
        if sweep + 1 < ITERS:
            caps = [split(x) for x in capsules]
            near = [
                [
                    lax.dot_general(
                        caps[b], vectors(b, g), (((1,), (1,)), ((), ())), preferred_element_type=F32
                    )
                    for g in range(groups)
                ]
                for b in blocks
            ]
            for b in blocks:
                added = [joined(x).reshape(CAPS, BLOCK, lanes) for x in near[b]]
                chosen = added[-1]
                for g in range(groups - 1):
                    chosen = jnp.where(in_group[g][None], added[g], chosen)
                logits[b] = logits[b] + chosen
    half = D // 2
    low_own = core_ref[0] == 0
    for b in blocks:
        made = capsules[b].reshape(CAPS, BLOCK, D)
        low, high = made[:, :, :half], made[:, :, half:]
        kept, passed = jnp.where(low_own, low, high), jnp.where(low_own, high, low)
        for j in range(CAPS):
            own_ref[b * BLOCK : (b + 1) * BLOCK, j, :] = kept[j]
            other_ref[b * BLOCK : (b + 1) * BLOCK, j, :] = passed[j]


def encode(core, origin, parts, lens, seed, weights, steps):
    users = lens.shape[0]
    spots = parts[0].shape[-2]
    pa_count = origin.shape[0]
    whole = (pa_count, users, spots, D)
    vmem = pl.BlockSpec(memory_space=pltpu.VMEM)
    made = jax.ShapeDtypeStruct((users, CAPS, D // 2), F32)
    return pl.pallas_call(
        functools.partial(encode_kernel, steps=steps),
        out_shape=[made, made],
        grid=(steps,),
        in_specs=[pl.BlockSpec(memory_space=pltpu.SMEM)] * 2 + [vmem] * (3 + len(parts)),
        out_specs=[vmem] * 2,
        scratch_shapes=[
            pltpu.VMEM((users * pa_count * spots, D), BF16),
            pltpu.VMEM(whole if len(parts) > 1 else (1, 1, spots, D), BF16),
        ],
        compiler_params=pltpu.CompilerParams(vmem_limit_bytes=24 << 20),
        name="encode",
    )(core, origin, *parts, lens, seed, weights)


def moved_to(place, along, across, count):
    rest = count // Z_LO
    return (place // Z_LO + along + rest) % rest * Z_LO + (place % Z_LO + across) % Z_LO


def body(
    features, item_ids, item_table, lengths, routing_seed, w_qkv, w_out, w_bilinear, w_up, w_down
):
    pa_count = lax.axis_size("pa")
    dev_count = lax.axis_size("dev")
    spots = features.shape[1]
    per_core = lengths.shape[0] // (pa_count * dev_count)
    core_index = lax.axis_index("dev").astype(jnp.int32)
    core = core_index.reshape(1)
    swap = [(i, dev_count - 1 - i) for i in range(dev_count)]
    own = (w_qkv, w_out, w_bilinear, w_up, w_down)
    other = tuple(lax.ppermute(w, "dev", swap) for w in own)
    weights = finish_weights(core, own, other)
    first = (lax.axis_index("pa") * dev_count + core_index) * per_core
    lens = lax.dynamic_slice_in_dim(lengths, first, per_core).reshape(per_core, 1)
    cut = per_core * FIRST[0] // FIRST[1]
    lens = [lens[:cut], lens[cut:]]
    ids = item_ids.T
    place = lax.axis_index("pa").astype(jnp.int32)
    moves = [(i // Z_LO, i % Z_LO) for i in range(pa_count)]
    index = jnp.arange(pa_count, dtype=jnp.int32)
    along, across = index // Z_LO, index % Z_LO
    moved = [moved_to(place, along, across, pa_count), moved_to(place, -along, across, pa_count)]
    sent = lookup(
        core, index, ids, features, item_table, 0, cut, pa_count, dev_count, False
    )[0]
    got = lax.all_to_all(sent, "pa", split_axis=0, concat_axis=0, tiled=True)
    ids, weights, lens = lax.optimization_barrier((ids, weights, lens))
    late = lookup(
        core, moved[0], ids, features, item_table, cut, per_core - cut, pa_count, dev_count, True
    )
    parts = [late[0]]
    for i in range(1, pa_count):
        pairs = [(p, moved_to(p, *moves[i], pa_count)) for p in range(pa_count)]
        block = late[i]
        if i > AHEAD:
            block, parts[i - AHEAD] = lax.optimization_barrier((block, parts[i - AHEAD]))
        parts.append(lax.ppermute(block, "pa", pairs))
    got = [got.reshape(pa_count, cut, spots, D)]
    halves = []
    for origin, given, lengths_here, steps in (
        (index, got, lens[0], STEPS[0]),
        (moved[1], parts, lens[1], STEPS[1]),
    ):
        kept, passed = encode(core, origin, given, lengths_here, routing_seed, weights, steps)
        halves.append((kept, lax.ppermute(passed, "dev", swap)))
    kept = jnp.concatenate([h[0] for h in halves], axis=0)
    came = jnp.concatenate([h[1] for h in halves], axis=0)
    return jnp.where(
        core_index == 0,
        jnp.concatenate([kept, came], axis=0),
        jnp.concatenate([came, kept], axis=0),
    )


def solution(mesh):
    in_specs = (
        P("au", "pa", None),
        P("au", "pa"),
        P(),
        P("au"),
        P(),
        P(None, None, "dev"),
        P("dev", None),
        P(None, "dev"),
        P(None, "dev"),
        P("dev", None),
    )
    out_specs = P(("au", "pa"), None, "dev")
    return jax.shard_map(body, mesh=mesh, in_specs=in_specs, out_specs=out_specs, check_vma=False)
```

```python
import functools

import jax
import jax.numpy as jnp
from jax import lax
from jax.experimental import pallas as pl
from jax.experimental.pallas import tpu as pltpu
from jax.sharding import PartitionSpec as P

D = 256
HEADS = 4
FF = 1024
CAPS = 4
ITERS = 3
FIRST = (3, 8)
BLOCK = 8
STEPS = (2, 2)
TABLE_PARTS = 4
AHEAD = 5
Z_LO = 2
GROUP = 4
F32 = jnp.float32
BF16 = jnp.bfloat16


def in_hbm(*arrays):
    return tuple(pltpu.with_memory_space_constraint(a, pltpu.HBM) for a in arrays)


def moved_to(place, along, across, count):
    rest = count // Z_LO
    return (place // Z_LO + along + rest) % rest * Z_LO + (place % Z_LO + across) % Z_LO


def lookup_kernel(*refs, start, per_pair, per_core, outs):
    later = outs > 1
    ids_hbm, feat_hbm, table_hbm = refs[:3]
    out_hbm, refs = refs[3 : 3 + outs], refs[3 + outs :]
    wide, table, table_sem, ids, feat, out, id_sem, feat_sem, out_sem = refs
    pairs, users, spots, _ = feat.shape
    place = lax.axis_index("pa")
    offset = lax.axis_index("dev") * per_core + start
    if later:
        owners = [moved_to(place, i // Z_LO, i % Z_LO, pairs) for i in range(pairs)]
    else:
        owners = list(range(pairs))
    fetch_ids = pltpu.make_async_copy(ids_hbm, ids, id_sem)
    fetch_ids.start()
    fetch_table = []
    rows = table.shape[0] // TABLE_PARTS
    for i in range(TABLE_PARTS):
        at = pl.ds(i * rows, rows)
        fetch_table.append(pltpu.make_async_copy(table_hbm.at[at], table.at[at], table_sem.at[i]))
        fetch_table[-1].start()
    fetch_feat = []
    for d in range(pairs):
        at = pl.ds(owners[d] * per_pair + offset, users)
        fetch_feat.append(pltpu.make_async_copy(feat_hbm.at[at], feat.at[d], feat_sem.at[d]))
        fetch_feat[-1].start()
    for i, fetch in enumerate(fetch_table):
        fetch.wait()

        def widen(j, carry, i=i):
            at = pl.ds(pl.multiple_of(i * rows + j * 128, 128), 128)
            for h in range(2):
                wide[h, at, :] = table[at, h * (D // 2) : (h + 1) * (D // 2)].astype(F32)
            return carry

        lax.fori_loop(0, rows // 128, widen, 0)
    fetch_ids.wait()
    spot = lax.broadcasted_iota(jnp.int32, (spots, D // 2), 0)
    send = []
    for d in range(pairs):
        fetch_feat[d].wait()
        first = owners[d] * per_pair + offset

        def one(user, carry, d=d, first=first):
            halves = [None, None]
            for p in range(spots):
                at = pl.ds(ids[p, first + user], 1)
                for h in range(2):
                    row = jnp.broadcast_to(wide[h, at, :], (spots, D // 2))
                    halves[h] = row if p == 0 else jnp.where(spot == p, row, halves[h])
            rows = jnp.concatenate(halves, axis=1)
            out[d, user] = (feat[d, user].astype(F32) + rows).astype(BF16)
            return carry

        lax.fori_loop(0, users, one, 0, unroll=8)
        if later:
            target = out_hbm[d]
        else:
            target = out_hbm[0].at[pl.ds(d * users, users)]
        send.append(pltpu.make_async_copy(out.at[d], target, out_sem.at[d]))
        send[-1].start()
    for copy in send:
        copy.wait()


def lookup(ids, features, table, start, users, pa_count, dev_count, later):
    all_users, spots, width = features.shape
    per_pair = all_users // pa_count
    per_core = per_pair // dev_count
    block = (pa_count, users, spots, width)
    hbm = pl.BlockSpec(memory_space=pltpu.HBM)
    outs = pa_count if later else 1
    made = [pltpu.HBM((users * (1 if later else pa_count), spots, width), BF16)] * outs
    scratch = [
        pltpu.VMEM((2, table.shape[0], D // 2), F32),
        pltpu.VMEM(table.shape, BF16),
        pltpu.SemaphoreType.DMA((TABLE_PARTS,)),
        pltpu.SMEM(ids.shape, jnp.int32),
        pltpu.VMEM(block, BF16),
        pltpu.VMEM(block, BF16),
        pltpu.SemaphoreType.DMA,
        pltpu.SemaphoreType.DMA((pa_count,)),
        pltpu.SemaphoreType.DMA((pa_count,)),
    ]
    return pl.pallas_call(
        functools.partial(
            lookup_kernel, start=start, per_pair=per_pair, per_core=per_core, outs=outs
        ),
        out_shape=made,
        in_specs=[hbm, hbm, hbm],
        out_specs=[hbm] * outs,
        scratch_shapes=scratch,
        compiler_params=pltpu.CompilerParams(vmem_limit_bytes=12 << 20),
        name="lookup",
    )(*in_hbm(ids, features, table))


def weights_kernel(
    qkv_a, qkv_b, out_a, out_b, bil_a, bil_b, up_a, up_b, down_a, down_b, all_ref
):
    half = D // 2
    low = lax.axis_index("dev") == 0
    at = 0
    for i in range(3):
        all_ref[at : at + D, :half] = qkv_a[i]
        all_ref[at : at + D, half:] = qkv_b[i]
        at += D
    for up in (up_a, up_b):
        for i in range(up.shape[1] // D):
            all_ref[at : at + D, :] = up[:, i * D : (i + 1) * D]
            at += D

    @pl.when(low)
    def _():
        all_ref[at : at + D, :half] = bil_a[...]
        all_ref[at : at + D, half:] = bil_b[...]

    @pl.when(jnp.logical_not(low))
    def _():
        all_ref[at : at + D, :half] = bil_b[...]
        all_ref[at : at + D, half:] = bil_a[...]

    after = at + D
    for rows in (out_a, out_b, down_a, down_b):
        all_ref[after : after + rows.shape[0], :] = rows[...]
        after += rows.shape[0]


def finish_weights(own, other):
    ff = own[3].shape[1]
    operands = [w for pair in zip(in_hbm(*own), other) for w in pair]
    return pl.pallas_call(
        weights_kernel,
        out_shape=pltpu.VMEM((5 * D + 4 * ff, D), BF16),
        in_specs=[pl.BlockSpec(memory_space=pltpu.VMEM)] * len(operands),
        out_specs=pl.BlockSpec(memory_space=pltpu.VMEM),
        compiler_params=pltpu.CompilerParams(vmem_limit_bytes=8 << 20),
        name="weights",
    )(*operands)


def split(x):
    high = x.astype(BF16)
    return jnp.concatenate([high, (x - high.astype(F32)).astype(BF16)], axis=0)


def joined(x):
    half = x.shape[0] // 2
    return x[:half] + x[half:]


def encode_kernel(*refs, steps, start, later):
    count = 2 if later else 0
    lens_ref, seed_ref, w_ref = refs[:3]
    parts = refs[3 + count : -4]
    own_ref, other_ref, interest_ref, x_ref = refs[-4:]
    step = pl.program_id(0)
    if later:
        place = lax.axis_index("pa")

        @pl.when(step == 0)
        def _():
            for i, part in enumerate(parts):
                origin = moved_to(place, -(i // Z_LO), i % Z_LO, len(parts))
                x_ref[origin] = part[...]
            own_ref[:start] = refs[3][:start]
            other_ref[:start] = refs[4][:start]

    else:
        x_ref = parts[0]
    pairs, all_users, spots, _ = x_ref.shape
    block = all_users // steps
    history = pairs * spots
    rows = block * history
    head = D // HEADS
    lanes = HEADS * history
    x = x_ref[:, pl.ds(step * block, block)].astype(F32)
    x = jnp.swapaxes(x, 0, 1).reshape(rows, D).astype(BF16)

    def through(i):
        return jnp.dot(x, w_ref[i * D : (i + 1) * D, :], preferred_element_type=F32)

    queries = (through(0) * (1.0 / head**0.5)).astype(BF16)
    keys = through(1).astype(BF16)
    values = through(2).astype(BF16)

    lane_head = lax.broadcasted_iota(jnp.int32, (history, D), 1) // head
    own_head = [(lane_head == h).astype(F32).astype(BF16) for h in range(HEADS)]
    odd_even = [own_head[0] + own_head[2], own_head[1] + own_head[3]]
    row_head = lax.broadcasted_iota(jnp.int32, (lanes, D), 0) // history
    col_head = lax.broadcasted_iota(jnp.int32, (lanes, D), 1) // head
    ones = (row_head == col_head).astype(F32).astype(BF16)
    position = lax.broadcasted_iota(jnp.int32, (block, lanes), 1) % history
    lens = lens_ref[pl.ds(step * block, block), :]
    key_valid = (position < lens).astype(F32)
    users = [slice(u * history, (u + 1) * history) for u in range(block)]
    scores = []
    none = jnp.zeros((history, D // 2), BF16)
    for first in range(0, block, 2):
        pair = users[first : first + 2]
        key_wide = jnp.concatenate([keys[at] * m for at in pair for m in odd_even], axis=0)
        query_wide = jnp.concatenate(
            [
                part
                for at in pair
                for part in (
                    jnp.concatenate([queries[at, : D // 2], none], axis=1),
                    jnp.concatenate([none, queries[at, D // 2 :]], axis=1),
                )
            ],
            axis=0,
        )
        both = lax.dot_general(
            query_wide, key_wide, (((1,), (1,)), ((), ())), preferred_element_type=F32
        )
        for u in range(2):
            rows_u = both[u * D // 2 : (u + 1) * D // 2, u * D // 2 : (u + 1) * D // 2]
            scores.append(jnp.concatenate([rows_u[:history], rows_u[history:]], axis=1))
    rounded = [
        jnp.where(key_valid[u : u + 1] > 0.0, jnp.exp(s), 0.0).astype(BF16)
        for u, s in enumerate(scores)
    ]
    totals = jnp.dot(jnp.concatenate(rounded, axis=0), ones, preferred_element_type=F32)
    weighted = []
    for first in range(0, block, 2):
        pair = users[first : first + 2]
        value_wide = jnp.concatenate([values[at] * m for at in pair for m in odd_even], axis=0)
        prob_wide = []
        for u in range(2):
            for g in range(2):
                part = rounded[first + u][:, g * D // 2 : (g + 1) * D // 2]
                prob_wide.append(jnp.concatenate([part, none] if u == 0 else [none, part], axis=1))
        both = jnp.dot(jnp.concatenate(prob_wide, axis=0), value_wide, preferred_element_type=F32)
        for u in range(2):
            rows_u = both[u * D // 2 : (u + 1) * D // 2]
            weighted.append(
                jnp.concatenate([rows_u[:history, : D // 2], rows_u[history:, D // 2 :]], axis=1)
            )
    attended = (jnp.concatenate(weighted, axis=0) / totals).astype(BF16)
    tail = 3 + FF // D
    hidden = [jax.nn.gelu(through(i)).astype(BF16) for i in range(3, tail)]
    everything = jnp.concatenate([x, attended] + hidden, axis=1)
    interest = jnp.dot(everything, w_ref[tail * D :, :], preferred_element_type=F32).astype(BF16)
    interest_ref[pl.ds(pl.multiple_of(step * rows, rows), rows), :] = interest

    @pl.when(step == steps - 1)
    def _():
        route(lens_ref, seed_ref, own_ref, other_ref, interest_ref, history, start)


def route(lens_ref, seed_ref, own_ref, other_ref, interest_ref, history, start):
    lanes = GROUP * history
    groups = BLOCK // GROUP
    blocks = range(interest_ref.shape[0] // (BLOCK * history))
    lane = lax.broadcasted_iota(jnp.int32, (BLOCK, lanes), 1)
    user = lax.broadcasted_iota(jnp.int32, (BLOCK, lanes), 0)
    mine = (lane // history) == (user % GROUP)
    in_group = [(user // GROUP) == g for g in range(groups)]
    base = (seed_ref[...].astype(F32) - 7.5) * 0.25
    base = jnp.concatenate([base] * GROUP, axis=1)
    base = jnp.broadcast_to(base[:, None, :], (CAPS, BLOCK, lanes))
    logits = [base for _ in blocks]
    valid = []
    for b in blocks:
        real = mine & ((lane % history) < lens_ref[b * BLOCK : (b + 1) * BLOCK, :])
        valid.append([(real & here).astype(F32)[None] for here in in_group])

    def vectors(b, g):
        return interest_ref[(b * groups + g) * lanes : (b * groups + g + 1) * lanes, :]

    def softmax(x):
        weights = jnp.exp(x - jnp.max(x, axis=0, keepdims=True))
        return weights / jnp.sum(weights, axis=0, keepdims=True)

    def parts(weights, b):
        return [split((weights * v).reshape(CAPS * BLOCK, lanes)) for v in valid[b]]

    def squash(summed):
        squares = jnp.sum(summed * summed, axis=1, keepdims=True)
        return summed * (jnp.sqrt(squares) / (1.0 + squares))

    for sweep in range(ITERS):
        if sweep == 0:
            weights = [softmax(base)] * len(logits)
        else:
            weights = [softmax(x) for x in logits]
        weighted = [parts(weights[b], b) for b in blocks]
        summed = [
            joined(
                sum(
                    jnp.dot(weighted[b][g], vectors(b, g), preferred_element_type=F32)
                    for g in range(groups)
                )
            )
            for b in blocks
        ]
        capsules = [squash(x) for x in summed]
        if sweep + 1 < ITERS:
            caps = [split(x) for x in capsules]
            near = [
                [
                    lax.dot_general(
                        caps[b], vectors(b, g), (((1,), (1,)), ((), ())), preferred_element_type=F32
                    )
                    for g in range(groups)
                ]
                for b in blocks
            ]
            for b in blocks:
                added = [joined(x).reshape(CAPS, BLOCK, lanes) for x in near[b]]
                chosen = added[-1]
                for g in range(groups - 1):
                    chosen = jnp.where(in_group[g][None], added[g], chosen)
                logits[b] = logits[b] + chosen
    half = D // 2
    low_own = lax.axis_index("dev") == 0
    for b in blocks:
        made = capsules[b].reshape(CAPS, BLOCK, D)
        low, high = made[:, :, :half], made[:, :, half:]
        kept, passed = jnp.where(low_own, low, high), jnp.where(low_own, high, low)
        for j in range(CAPS):
            at = slice(start + b * BLOCK, start + (b + 1) * BLOCK)
            own_ref[at, j, :] = kept[j]
            other_ref[at, j, :] = passed[j]


def encode(parts, lens, seed, weights, steps, start, all_users, before):
    users = lens.shape[0]
    later = len(before) > 0
    spots = parts[0].shape[-2]
    pa_count = len(parts) if later else parts[0].shape[0]
    whole = (pa_count, users, spots, D) if later else (1, 1, spots, D)
    vmem = pl.BlockSpec(memory_space=pltpu.VMEM)
    operands = [lens, seed, weights, *before, *parts]
    made = pltpu.VMEM((all_users, CAPS, D // 2), F32)
    return pl.pallas_call(
        functools.partial(encode_kernel, steps=steps, start=start, later=later),
        out_shape=[made, made],
        grid=(steps,),
        in_specs=[vmem] * len(operands),
        out_specs=[vmem] * 2,
        scratch_shapes=[
            pltpu.VMEM((users * pa_count * spots, D), BF16),
            pltpu.VMEM(whole, BF16),
        ],
        compiler_params=pltpu.CompilerParams(vmem_limit_bytes=24 << 20),
        name="encode",
    )(*operands)


def body(
    features, item_ids, item_table, lengths, routing_seed, w_qkv, w_out, w_bilinear, w_up, w_down
):
    pa_count = lax.axis_size("pa")
    dev_count = lax.axis_size("dev")
    spots = features.shape[1]
    per_core = lengths.shape[0] // (pa_count * dev_count)
    core = lax.axis_index("dev").astype(jnp.int32)
    swap = [(i, dev_count - 1 - i) for i in range(dev_count)]
    own = (w_qkv, w_out, w_bilinear, w_up, w_down)
    weights = finish_weights(own, tuple(lax.ppermute(w, "dev", swap) for w in own))
    first = (lax.axis_index("pa") * dev_count + core) * per_core
    lens = lax.dynamic_slice_in_dim(lengths, first, per_core).reshape(per_core, 1)
    cut = per_core * FIRST[0] // FIRST[1]
    lens = [lens[:cut], lens[cut:]]
    ids = item_ids.T
    counts = (pa_count, dev_count)
    sent = lookup(ids, features, item_table, 0, cut, *counts, False)[0]
    got = lax.all_to_all(sent, "pa", split_axis=0, concat_axis=0, tiled=True)
    got = got.reshape(pa_count, cut, spots, D)
    ids, weights, lens = lax.optimization_barrier((ids, weights, lens))
    late = lookup(ids, features, item_table, cut, per_core - cut, *counts, True)
    parts = [late[0]]
    for i in range(1, pa_count):
        pairs = [
            (p, moved_to(p, i // Z_LO, i % Z_LO, pa_count)) for p in range(pa_count)
        ]
        block = late[i]
        if i > AHEAD:
            block, parts[i - AHEAD] = lax.optimization_barrier((block, parts[i - AHEAD]))
        parts.append(lax.ppermute(block, "pa", pairs))
    made = encode([got], lens[0], routing_seed, weights, STEPS[0], 0, per_core, ())
    kept, passed = encode(
        parts, lens[1], routing_seed, weights, STEPS[1], cut, per_core, tuple(made)
    )
    came = lax.ppermute(passed, "dev", swap)
    return jnp.where(
        core == 0,
        jnp.concatenate([kept, came], axis=0),
        jnp.concatenate([came, kept], axis=0),
    )


def solution(mesh):
    in_specs = (
        P("au", "pa", None),
        P("au", "pa"),
        P(),
        P("au"),
        P(),
        P(None, None, "dev"),
        P("dev", None),
        P(None, "dev"),
        P(None, "dev"),
        P("dev", None),
    )
    out_specs = P(("au", "pa"), None, "dev")
    return jax.shard_map(body, mesh=mesh, in_specs=in_specs, out_specs=out_specs, check_vma=False)
```

```python
import functools

import jax
import jax.numpy as jnp
from jax import lax
from jax.experimental import pallas as pl
from jax.experimental.pallas import tpu as pltpu
from jax.sharding import PartitionSpec as P

D = 256
HEADS = 4
FF = 1024
CAPS = 4
ITERS = 3
FIRST = (4, 8)
BLOCK = 8
STEPS = (2, 2)
TABLE_PARTS = 4
AHEAD = 5
Z_LO = 2
GROUP = 4
F32 = jnp.float32
BF16 = jnp.bfloat16


def in_hbm(*arrays):
    return tuple(pltpu.with_memory_space_constraint(a, pltpu.HBM) for a in arrays)


def moved_to(place, along, across, count):
    rest = count // Z_LO
    return (place // Z_LO + along + rest) % rest * Z_LO + (place % Z_LO + across) % Z_LO


def lookup_kernel(*refs, start, per_pair, per_core, outs):
    later = outs > 1
    ids_hbm, feat_hbm, table_hbm = refs[:3]
    out_hbm, refs = refs[3 : 3 + outs], refs[3 + outs :]
    wide, table, table_sem, ids, feat, out, id_sem, feat_sem, out_sem = refs
    pairs, users, spots, _ = feat.shape
    place = lax.axis_index("pa")
    offset = lax.axis_index("dev") * per_core + start
    if later:
        owners = [moved_to(place, i // Z_LO, i % Z_LO, pairs) for i in range(pairs)]
    else:
        owners = list(range(pairs))
    fetch_ids = pltpu.make_async_copy(ids_hbm, ids, id_sem)
    fetch_ids.start()
    fetch_table = []
    rows = table.shape[0] // TABLE_PARTS
    for i in range(TABLE_PARTS):
        at = pl.ds(i * rows, rows)
        fetch_table.append(pltpu.make_async_copy(table_hbm.at[at], table.at[at], table_sem.at[i]))
        fetch_table[-1].start()
    fetch_feat = []
    for d in range(pairs):
        at = pl.ds(owners[d] * per_pair + offset, users)
        fetch_feat.append(pltpu.make_async_copy(feat_hbm.at[at], feat.at[d], feat_sem.at[d]))
        fetch_feat[-1].start()
    for i, fetch in enumerate(fetch_table):
        fetch.wait()

        def widen(j, carry, i=i):
            at = pl.ds(pl.multiple_of(i * rows + j * 128, 128), 128)
            for h in range(2):
                wide[h, at, :] = table[at, h * (D // 2) : (h + 1) * (D // 2)].astype(F32)
            return carry

        lax.fori_loop(0, rows // 128, widen, 0)
    fetch_ids.wait()
    spot = lax.broadcasted_iota(jnp.int32, (spots, D // 2), 0)
    send = []
    for d in range(pairs):
        fetch_feat[d].wait()
        first = owners[d] * per_pair + offset

        def one(user, carry, d=d, first=first):
            halves = [None, None]
            for p in range(spots):
                at = pl.ds(ids[p, first + user], 1)
                for h in range(2):
                    row = jnp.broadcast_to(wide[h, at, :], (spots, D // 2))
                    halves[h] = row if p == 0 else jnp.where(spot == p, row, halves[h])
            rows = jnp.concatenate(halves, axis=1)
            out[d, user] = (feat[d, user].astype(F32) + rows).astype(BF16)
            return carry

        lax.fori_loop(0, users, one, 0, unroll=8)
        if later:
            target = out_hbm[d]
        else:
            target = out_hbm[0].at[pl.ds(d * users, users)]
        send.append(pltpu.make_async_copy(out.at[d], target, out_sem.at[d]))
        send[-1].start()
    for copy in send:
        copy.wait()


def lookup(ids, features, table, start, users, pa_count, dev_count, later):
    all_users, spots, width = features.shape
    per_pair = all_users // pa_count
    per_core = per_pair // dev_count
    block = (pa_count, users, spots, width)
    hbm = pl.BlockSpec(memory_space=pltpu.HBM)
    outs = pa_count if later else 1
    made = [pltpu.HBM((users * (1 if later else pa_count), spots, width), BF16)] * outs
    scratch = [
        pltpu.VMEM((2, table.shape[0], D // 2), F32),
        pltpu.VMEM(table.shape, BF16),
        pltpu.SemaphoreType.DMA((TABLE_PARTS,)),
        pltpu.SMEM(ids.shape, jnp.int32),
        pltpu.VMEM(block, BF16),
        pltpu.VMEM(block, BF16),
        pltpu.SemaphoreType.DMA,
        pltpu.SemaphoreType.DMA((pa_count,)),
        pltpu.SemaphoreType.DMA((pa_count,)),
    ]
    return pl.pallas_call(
        functools.partial(
            lookup_kernel, start=start, per_pair=per_pair, per_core=per_core, outs=outs
        ),
        out_shape=made,
        in_specs=[hbm, hbm, hbm],
        out_specs=[hbm] * outs,
        scratch_shapes=scratch,
        compiler_params=pltpu.CompilerParams(vmem_limit_bytes=12 << 20),
        name="lookup",
    )(*in_hbm(ids, features, table))


def weights_kernel(
    qkv_a, qkv_b, out_a, out_b, bil_a, bil_b, up_a, up_b, down_a, down_b, all_ref
):
    half = D // 2
    low = lax.axis_index("dev") == 0
    at = 0
    for i in range(3):
        all_ref[at : at + D, :half] = qkv_a[i]
        all_ref[at : at + D, half:] = qkv_b[i]
        at += D
    for up in (up_a, up_b):
        for i in range(up.shape[1] // D):
            all_ref[at : at + D, :] = up[:, i * D : (i + 1) * D]
            at += D

    @pl.when(low)
    def _():
        all_ref[at : at + D, :half] = bil_a[...]
        all_ref[at : at + D, half:] = bil_b[...]

    @pl.when(jnp.logical_not(low))
    def _():
        all_ref[at : at + D, :half] = bil_b[...]
        all_ref[at : at + D, half:] = bil_a[...]

    after = at + D
    for rows in (out_a, out_b, down_a, down_b):
        all_ref[after : after + rows.shape[0], :] = rows[...]
        after += rows.shape[0]


def finish_weights(own, other):
    ff = own[3].shape[1]
    operands = [w for pair in zip(in_hbm(*own), other) for w in pair]
    return pl.pallas_call(
        weights_kernel,
        out_shape=pltpu.VMEM((5 * D + 4 * ff, D), BF16),
        in_specs=[pl.BlockSpec(memory_space=pltpu.VMEM)] * len(operands),
        out_specs=pl.BlockSpec(memory_space=pltpu.VMEM),
        compiler_params=pltpu.CompilerParams(vmem_limit_bytes=8 << 20),
        name="weights",
    )(*operands)


def split(x):
    high = x.astype(BF16)
    return jnp.concatenate([high, (x - high.astype(F32)).astype(BF16)], axis=0)


def joined(x):
    half = x.shape[0] // 2
    return x[:half] + x[half:]


def encode_kernel(*refs, steps, start, later):
    count = 2 if later else 0
    lens_ref, seed_ref, w_ref = refs[:3]
    parts = refs[3 + count : -4]
    own_ref, other_ref, interest_ref, x_ref = refs[-4:]
    step = pl.program_id(0)
    if later:
        place = lax.axis_index("pa")

        @pl.when(step == 0)
        def _():
            for i, part in enumerate(parts):
                origin = moved_to(place, -(i // Z_LO), i % Z_LO, len(parts))
                x_ref[origin] = part[...]
            own_ref[:start] = refs[3][:start]
            other_ref[:start] = refs[4][:start]

    else:
        x_ref = parts[0]
    pairs, all_users, spots, _ = x_ref.shape
    block = all_users // steps
    history = pairs * spots
    rows = block * history
    head = D // HEADS
    lanes = HEADS * history
    x = x_ref[:, pl.ds(step * block, block)].astype(F32)
    x = jnp.swapaxes(x, 0, 1).reshape(rows, D).astype(BF16)

    def through(i):
        return jnp.dot(x, w_ref[i * D : (i + 1) * D, :], preferred_element_type=F32)

    queries = (through(0) * (1.0 / head**0.5)).astype(BF16)
    keys = through(1).astype(BF16)
    values = through(2).astype(BF16)

    lane_head = lax.broadcasted_iota(jnp.int32, (history, D), 1) // head
    own_head = [(lane_head == h).astype(F32).astype(BF16) for h in range(HEADS)]
    odd_even = [own_head[0] + own_head[2], own_head[1] + own_head[3]]
    row_head = lax.broadcasted_iota(jnp.int32, (lanes, D), 0) // history
    col_head = lax.broadcasted_iota(jnp.int32, (lanes, D), 1) // head
    ones = (row_head == col_head).astype(F32).astype(BF16)
    position = lax.broadcasted_iota(jnp.int32, (block, lanes), 1) % history
    lens = lens_ref[pl.ds(step * block, block), :]
    key_valid = (position < lens).astype(F32)
    users = [slice(u * history, (u + 1) * history) for u in range(block)]
    scores = []
    none = jnp.zeros((history, D // 2), BF16)
    for first in range(0, block, 2):
        pair = users[first : first + 2]
        key_wide = jnp.concatenate([keys[at] * m for at in pair for m in odd_even], axis=0)
        query_wide = jnp.concatenate(
            [
                part
                for at in pair
                for part in (
                    jnp.concatenate([queries[at, : D // 2], none], axis=1),
                    jnp.concatenate([none, queries[at, D // 2 :]], axis=1),
                )
            ],
            axis=0,
        )
        both = lax.dot_general(
            query_wide, key_wide, (((1,), (1,)), ((), ())), preferred_element_type=F32
        )
        for u in range(2):
            rows_u = both[u * D // 2 : (u + 1) * D // 2, u * D // 2 : (u + 1) * D // 2]
            scores.append(jnp.concatenate([rows_u[:history], rows_u[history:]], axis=1))
    rounded = [
        jnp.where(key_valid[u : u + 1] > 0.0, jnp.exp(s), 0.0).astype(BF16)
        for u, s in enumerate(scores)
    ]
    totals = jnp.dot(jnp.concatenate(rounded, axis=0), ones, preferred_element_type=F32)
    weighted = []
    for first in range(0, block, 2):
        pair = users[first : first + 2]
        value_wide = jnp.concatenate([values[at] * m for at in pair for m in odd_even], axis=0)
        prob_wide = []
        for u in range(2):
            for g in range(2):
                part = rounded[first + u][:, g * D // 2 : (g + 1) * D // 2]
                prob_wide.append(jnp.concatenate([part, none] if u == 0 else [none, part], axis=1))
        both = jnp.dot(jnp.concatenate(prob_wide, axis=0), value_wide, preferred_element_type=F32)
        for u in range(2):
            rows_u = both[u * D // 2 : (u + 1) * D // 2]
            weighted.append(
                jnp.concatenate([rows_u[:history, : D // 2], rows_u[history:, D // 2 :]], axis=1)
            )
    attended = (jnp.concatenate(weighted, axis=0) / totals).astype(BF16)
    tail = 3 + FF // D
    hidden = [jax.nn.gelu(through(i)).astype(BF16) for i in range(3, tail)]
    everything = jnp.concatenate([x, attended] + hidden, axis=1)
    interest = jnp.dot(everything, w_ref[tail * D :, :], preferred_element_type=F32).astype(BF16)
    interest_ref[pl.ds(pl.multiple_of(step * rows, rows), rows), :] = interest

    @pl.when(step == steps - 1)
    def _():
        route(lens_ref, seed_ref, own_ref, other_ref, interest_ref, history, start)


def route(lens_ref, seed_ref, own_ref, other_ref, interest_ref, history, start):
    lanes = GROUP * history
    groups = BLOCK // GROUP
    blocks = range(interest_ref.shape[0] // (BLOCK * history))
    lane = lax.broadcasted_iota(jnp.int32, (BLOCK, lanes), 1)
    user = lax.broadcasted_iota(jnp.int32, (BLOCK, lanes), 0)
    mine = (lane // history) == (user % GROUP)
    in_group = [(user // GROUP) == g for g in range(groups)]
    base = (seed_ref[...].astype(F32) - 7.5) * 0.25
    base = jnp.concatenate([base] * GROUP, axis=1)
    base = jnp.broadcast_to(base[:, None, :], (CAPS, BLOCK, lanes))
    logits = [base for _ in blocks]
    valid = []
    for b in blocks:
        real = mine & ((lane % history) < lens_ref[b * BLOCK : (b + 1) * BLOCK, :])
        valid.append([(real & here).astype(F32)[None] for here in in_group])

    def vectors(b, g):
        return interest_ref[(b * groups + g) * lanes : (b * groups + g + 1) * lanes, :]

    def softmax(x):
        weights = jnp.exp(x - jnp.max(x, axis=0, keepdims=True))
        return weights / jnp.sum(weights, axis=0, keepdims=True)

    def parts(weights, b):
        return [split((weights * v).reshape(CAPS * BLOCK, lanes)) for v in valid[b]]

    def squash(summed):
        squares = jnp.sum(summed * summed, axis=1, keepdims=True)
        return summed * (jnp.sqrt(squares) / (1.0 + squares))

    for sweep in range(ITERS):
        if sweep == 0:
            weights = [softmax(base)] * len(logits)
        else:
            weights = [softmax(x) for x in logits]
        weighted = [parts(weights[b], b) for b in blocks]
        summed = [
            joined(
                sum(
                    jnp.dot(weighted[b][g], vectors(b, g), preferred_element_type=F32)
                    for g in range(groups)
                )
            )
            for b in blocks
        ]
        capsules = [squash(x) for x in summed]
        if sweep + 1 < ITERS:
            caps = [split(x) for x in capsules]
            near = [
                [
                    lax.dot_general(
                        caps[b], vectors(b, g), (((1,), (1,)), ((), ())), preferred_element_type=F32
                    )
                    for g in range(groups)
                ]
                for b in blocks
            ]
            for b in blocks:
                added = [joined(x).reshape(CAPS, BLOCK, lanes) for x in near[b]]
                chosen = added[-1]
                for g in range(groups - 1):
                    chosen = jnp.where(in_group[g][None], added[g], chosen)
                logits[b] = logits[b] + chosen
    half = D // 2
    low_own = lax.axis_index("dev") == 0
    for b in blocks:
        made = capsules[b].reshape(CAPS, BLOCK, D)
        low, high = made[:, :, :half], made[:, :, half:]
        kept, passed = jnp.where(low_own, low, high), jnp.where(low_own, high, low)
        for j in range(CAPS):
            at = slice(start + b * BLOCK, start + (b + 1) * BLOCK)
            own_ref[at, j, :] = kept[j]
            other_ref[at, j, :] = passed[j]


def encode(parts, lens, seed, weights, steps, start, all_users, before):
    users = lens.shape[0]
    later = len(before) > 0
    spots = parts[0].shape[-2]
    pa_count = len(parts) if later else parts[0].shape[0]
    whole = (pa_count, users, spots, D) if later else (1, 1, spots, D)
    vmem = pl.BlockSpec(memory_space=pltpu.VMEM)
    operands = [lens, seed, weights, *before, *parts]
    made = pltpu.VMEM((all_users, CAPS, D // 2), F32)
    return pl.pallas_call(
        functools.partial(encode_kernel, steps=steps, start=start, later=later),
        out_shape=[made, made],
        grid=(steps,),
        in_specs=[vmem] * len(operands),
        out_specs=[vmem] * 2,
        scratch_shapes=[
            pltpu.VMEM((users * pa_count * spots, D), BF16),
            pltpu.VMEM(whole, BF16),
        ],
        compiler_params=pltpu.CompilerParams(vmem_limit_bytes=24 << 20),
        name="encode",
    )(*operands)


def body(
    features, item_ids, item_table, lengths, routing_seed, w_qkv, w_out, w_bilinear, w_up, w_down
):
    pa_count = lax.axis_size("pa")
    dev_count = lax.axis_size("dev")
    spots = features.shape[1]
    per_core = lengths.shape[0] // (pa_count * dev_count)
    core = lax.axis_index("dev").astype(jnp.int32)
    swap = [(i, dev_count - 1 - i) for i in range(dev_count)]
    own = (w_qkv, w_out, w_bilinear, w_up, w_down)
    first = (lax.axis_index("pa") * dev_count + core) * per_core
    lens = lax.dynamic_slice_in_dim(lengths, first, per_core).reshape(per_core, 1)
    cut = per_core * FIRST[0] // FIRST[1]
    lens = [lens[:cut], lens[cut:]]
    ids = item_ids.T
    counts = (pa_count, dev_count)
    sent = lookup(ids, features, item_table, 0, cut, *counts, False)[0]
    own, sent = lax.optimization_barrier((own, sent))
    got = lax.all_to_all(sent, "pa", split_axis=0, concat_axis=0, tiled=True)
    got = got.reshape(pa_count, cut, spots, D)
    weights = finish_weights(own, tuple(lax.ppermute(w, "dev", swap) for w in own))
    ids, weights, lens = lax.optimization_barrier((ids, weights, lens))
    late = lookup(ids, features, item_table, cut, per_core - cut, *counts, True)
    parts = [late[0]]
    for i in range(1, pa_count):
        pairs = [
            (p, moved_to(p, i // Z_LO, i % Z_LO, pa_count)) for p in range(pa_count)
        ]
        block = late[i]
        if i > AHEAD:
            block, parts[i - AHEAD] = lax.optimization_barrier((block, parts[i - AHEAD]))
        parts.append(lax.ppermute(block, "pa", pairs))
    made = encode([got], lens[0], routing_seed, weights, STEPS[0], 0, per_core, ())
    kept, passed = encode(
        parts, lens[1], routing_seed, weights, STEPS[1], cut, per_core, tuple(made)
    )
    came = lax.ppermute(passed, "dev", swap)
    return jnp.where(
        core == 0,
        jnp.concatenate([kept, came], axis=0),
        jnp.concatenate([came, kept], axis=0),
    )


def solution(mesh):
    in_specs = (
        P("au", "pa", None),
        P("au", "pa"),
        P(),
        P("au"),
        P(),
        P(None, None, "dev"),
        P("dev", None),
        P(None, "dev"),
        P(None, "dev"),
        P("dev", None),
    )
    out_specs = P(("au", "pa"), None, "dev")
    return jax.shard_map(body, mesh=mesh, in_specs=in_specs, out_specs=out_specs, check_vma=False)
```

```python
import functools

import jax
import jax.numpy as jnp
from jax import lax
from jax.experimental import pallas as pl
from jax.experimental.pallas import tpu as pltpu
from jax.sharding import PartitionSpec as P

D = 256
HEADS = 4
FF = 1024
CAPS = 4
ITERS = 3
FIRST = (4, 8)
BLOCK = 8
STEPS = (2, 2)
TABLE_PARTS = 4
AHEAD = 5
Z_LO = 2
GROUP = 4
F32 = jnp.float32
BF16 = jnp.bfloat16


def in_hbm(*arrays):
    return tuple(pltpu.with_memory_space_constraint(a, pltpu.HBM) for a in arrays)


def moved_to(place, along, across, count):
    rest = count // Z_LO
    return (place // Z_LO + along + rest) % rest * Z_LO + (place % Z_LO + across) % Z_LO


def lookup_kernel(*refs, start, per_pair, per_core, outs):
    later = outs > 1
    ids_hbm, feat_hbm, table_hbm = refs[:3]
    out_hbm, refs = refs[3 : 3 + outs], refs[3 + outs :]
    wide, table, table_sem, ids, feat, out, id_sem, feat_sem, out_sem = refs
    pairs, users, spots, _ = feat.shape
    place = lax.axis_index("pa")
    offset = lax.axis_index("dev") * per_core + start
    if later:
        owners = [moved_to(place, i // Z_LO, i % Z_LO, pairs) for i in range(pairs)]
    else:
        owners = list(range(pairs))
    fetch_ids = pltpu.make_async_copy(ids_hbm, ids, id_sem)
    fetch_ids.start()
    fetch_table = []
    rows = table.shape[0] // TABLE_PARTS
    for i in range(TABLE_PARTS):
        at = pl.ds(i * rows, rows)
        fetch_table.append(pltpu.make_async_copy(table_hbm.at[at], table.at[at], table_sem.at[i]))
        fetch_table[-1].start()
    fetch_feat = []
    for d in range(pairs):
        at = pl.ds(owners[d] * per_pair + offset, users)
        fetch_feat.append(pltpu.make_async_copy(feat_hbm.at[at], feat.at[d], feat_sem.at[d]))
        fetch_feat[-1].start()
    for i, fetch in enumerate(fetch_table):
        fetch.wait()

        def widen(j, carry, i=i):
            at = pl.ds(pl.multiple_of(i * rows + j * 128, 128), 128)
            for h in range(2):
                wide[h, at, :] = table[at, h * (D // 2) : (h + 1) * (D // 2)].astype(F32)
            return carry

        lax.fori_loop(0, rows // 128, widen, 0)
    fetch_ids.wait()
    spot = lax.broadcasted_iota(jnp.int32, (spots, D // 2), 0)
    send = []
    for d in range(pairs):
        fetch_feat[d].wait()
        first = owners[d] * per_pair + offset

        def one(user, carry, d=d, first=first):
            halves = [None, None]
            for p in range(spots):
                at = pl.ds(ids[p, first + user], 1)
                for h in range(2):
                    row = jnp.broadcast_to(wide[h, at, :], (spots, D // 2))
                    halves[h] = row if p == 0 else jnp.where(spot == p, row, halves[h])
            rows = jnp.concatenate(halves, axis=1)
            out[d, user] = (feat[d, user].astype(F32) + rows).astype(BF16)
            return carry

        lax.fori_loop(0, users, one, 0, unroll=8)
        if later:
            target = out_hbm[d]
        else:
            target = out_hbm[0].at[pl.ds(d * users, users)]
        send.append(pltpu.make_async_copy(out.at[d], target, out_sem.at[d]))
        send[-1].start()
    for copy in send:
        copy.wait()


def lookup(ids, features, table, start, users, pa_count, dev_count, later):
    all_users, spots, width = features.shape
    per_pair = all_users // pa_count
    per_core = per_pair // dev_count
    block = (pa_count, users, spots, width)
    hbm = pl.BlockSpec(memory_space=pltpu.HBM)
    outs = pa_count if later else 1
    made = [pltpu.HBM((users * (1 if later else pa_count), spots, width), BF16)] * outs
    scratch = [
        pltpu.VMEM((2, table.shape[0], D // 2), F32),
        pltpu.VMEM(table.shape, BF16),
        pltpu.SemaphoreType.DMA((TABLE_PARTS,)),
        pltpu.SMEM(ids.shape, jnp.int32),
        pltpu.VMEM(block, BF16),
        pltpu.VMEM(block, BF16),
        pltpu.SemaphoreType.DMA,
        pltpu.SemaphoreType.DMA((pa_count,)),
        pltpu.SemaphoreType.DMA((pa_count,)),
    ]
    return pl.pallas_call(
        functools.partial(
            lookup_kernel, start=start, per_pair=per_pair, per_core=per_core, outs=outs
        ),
        out_shape=made,
        in_specs=[hbm, hbm, hbm],
        out_specs=[hbm] * outs,
        scratch_shapes=scratch,
        compiler_params=pltpu.CompilerParams(vmem_limit_bytes=12 << 20),
        name="lookup",
    )(*in_hbm(ids, features, table))


def weights_kernel(
    lens_ref, seed_ref, qkv_a, qkv_b, out_a, out_b, bil_a, bil_b, up_a, up_b, down_a, down_b,
    all_ref, valid_ref, base_ref, *, cut,
):
    pairs = lens_ref.shape[0]
    history = seed_ref.shape[1]
    spots = history // pairs
    place = lax.axis_index("pa")

    def arrival(lane):
        position = lane % history
        for i in range(pairs):
            origin = moved_to(place, -(i // Z_LO), i % Z_LO, pairs)
            here = (lane % history) // spots == i
            position = jnp.where(here, origin * spots + lane % spots, position)
        return position

    owned = (valid_ref.shape[0], lens_ref.shape[1])
    at = lax.broadcasted_iota(jnp.int32, owned, 0) + lax.axis_index("dev") * owned[0]
    near = lax.broadcasted_iota(jnp.int32, owned, 1) == at
    row = jnp.broadcast_to(lens_ref[pl.ds(place, 1), :].astype(F32), owned)
    lens = jnp.sum(jnp.where(near, row, 0.0), axis=1, keepdims=True)
    lane = lax.broadcasted_iota(jnp.int32, valid_ref.shape, 1)
    first = lax.broadcasted_iota(jnp.int32, valid_ref.shape, 0) < cut
    position = jnp.where(first, lane % history, arrival(lane))
    valid_ref[...] = (position.astype(F32) < lens).astype(F32)

    seed = seed_ref[...].astype(F32)
    chosen = lax.broadcasted_iota(jnp.int32, (history, history), 0) == arrival(
        lax.broadcasted_iota(jnp.int32, (history, history), 1)
    )
    moved = jnp.dot(
        seed.astype(BF16), chosen.astype(F32).astype(BF16), preferred_element_type=F32
    )
    for i, table in enumerate((seed, moved)):
        base_ref[i] = jnp.concatenate([(table - 7.5) * 0.25] * GROUP, axis=1)

    half = D // 2
    low = lax.axis_index("dev") == 0
    at = 0
    for i in range(3):
        all_ref[at : at + D, :half] = qkv_a[i]
        all_ref[at : at + D, half:] = qkv_b[i]
        at += D
    for up in (up_a, up_b):
        for i in range(up.shape[1] // D):
            all_ref[at : at + D, :] = up[:, i * D : (i + 1) * D]
            at += D

    @pl.when(low)
    def _():
        all_ref[at : at + D, :half] = bil_a[...]
        all_ref[at : at + D, half:] = bil_b[...]

    @pl.when(jnp.logical_not(low))
    def _():
        all_ref[at : at + D, :half] = bil_b[...]
        all_ref[at : at + D, half:] = bil_a[...]

    after = at + D
    for rows in (out_a, out_b, down_a, down_b):
        all_ref[after : after + rows.shape[0], :] = rows[...]
        after += rows.shape[0]


def finish_weights(own, other, lens, seed, cut, per_core):
    ff = own[3].shape[1]
    operands = [*in_hbm(lens, seed)] + [w for pair in zip(in_hbm(*own), other) for w in pair]
    vmem = pl.BlockSpec(memory_space=pltpu.VMEM)
    lanes = GROUP * seed.shape[1]
    return pl.pallas_call(
        functools.partial(weights_kernel, cut=cut),
        out_shape=[
            pltpu.VMEM((5 * D + 4 * ff, D), BF16),
            pltpu.VMEM((per_core, lanes), F32),
            pltpu.VMEM((2, CAPS, lanes), F32),
        ],
        in_specs=[vmem] * len(operands),
        out_specs=[vmem] * 3,
        compiler_params=pltpu.CompilerParams(vmem_limit_bytes=8 << 20),
        name="weights",
    )(*operands)


def split(x):
    high = x.astype(BF16)
    return jnp.concatenate([high, (x - high.astype(F32)).astype(BF16)], axis=0)


def joined(x):
    half = x.shape[0] // 2
    return x[:half] + x[half:]


def encode_kernel(*refs, steps, start, later):
    valid_ref, base_ref, w_ref = refs[:3]
    parts = refs[3 + (2 if later else 0) : -3]
    own_ref, other_ref, interest_ref = refs[-3:]
    step = pl.program_id(0)
    if later:
        own_ref[:start] = refs[3][:start]
        other_ref[:start] = refs[4][:start]
        pairs, (all_users, spots, _) = len(parts), parts[0].shape
    else:
        pairs, all_users, spots, _ = parts[0].shape
    block = all_users // steps
    history = pairs * spots
    rows = block * history
    head = D // HEADS
    lanes = HEADS * history
    at = pl.ds(step * block, block)
    if later:
        x = jnp.stack([part[at].astype(F32) for part in parts], axis=1)
    else:
        x = jnp.swapaxes(parts[0][:, at].astype(F32), 0, 1)
    x = x.reshape(rows, D).astype(BF16)

    def through(i):
        return jnp.dot(x, w_ref[i * D : (i + 1) * D, :], preferred_element_type=F32)

    queries = (through(0) * (1.0 / head**0.5)).astype(BF16)
    keys = through(1).astype(BF16)
    values = through(2).astype(BF16)

    lane_head = lax.broadcasted_iota(jnp.int32, (history, D), 1) // head
    own_head = [(lane_head == h).astype(F32).astype(BF16) for h in range(HEADS)]
    odd_even = [own_head[0] + own_head[2], own_head[1] + own_head[3]]
    row_head = lax.broadcasted_iota(jnp.int32, (lanes, D), 0) // history
    col_head = lax.broadcasted_iota(jnp.int32, (lanes, D), 1) // head
    ones = (row_head == col_head).astype(F32).astype(BF16)
    key_valid = valid_ref[pl.ds(start + step * block, block), :]
    users = [slice(u * history, (u + 1) * history) for u in range(block)]
    scores = []
    none = jnp.zeros((history, D // 2), BF16)
    for first in range(0, block, 2):
        pair = users[first : first + 2]
        key_wide = jnp.concatenate([keys[at] * m for at in pair for m in odd_even], axis=0)
        query_wide = jnp.concatenate(
            [
                part
                for at in pair
                for part in (
                    jnp.concatenate([queries[at, : D // 2], none], axis=1),
                    jnp.concatenate([none, queries[at, D // 2 :]], axis=1),
                )
            ],
            axis=0,
        )
        both = lax.dot_general(
            query_wide, key_wide, (((1,), (1,)), ((), ())), preferred_element_type=F32
        )
        for u in range(2):
            rows_u = both[u * D // 2 : (u + 1) * D // 2, u * D // 2 : (u + 1) * D // 2]
            scores.append(jnp.concatenate([rows_u[:history], rows_u[history:]], axis=1))
    rounded = [
        jnp.where(key_valid[u : u + 1] > 0.0, jnp.exp(s), 0.0).astype(BF16)
        for u, s in enumerate(scores)
    ]
    totals = jnp.dot(jnp.concatenate(rounded, axis=0), ones, preferred_element_type=F32)
    weighted = []
    for first in range(0, block, 2):
        pair = users[first : first + 2]
        value_wide = jnp.concatenate([values[at] * m for at in pair for m in odd_even], axis=0)
        prob_wide = []
        for u in range(2):
            for g in range(2):
                part = rounded[first + u][:, g * D // 2 : (g + 1) * D // 2]
                prob_wide.append(jnp.concatenate([part, none] if u == 0 else [none, part], axis=1))
        both = jnp.dot(jnp.concatenate(prob_wide, axis=0), value_wide, preferred_element_type=F32)
        for u in range(2):
            rows_u = both[u * D // 2 : (u + 1) * D // 2]
            weighted.append(
                jnp.concatenate([rows_u[:history, : D // 2], rows_u[history:, D // 2 :]], axis=1)
            )
    attended = (jnp.concatenate(weighted, axis=0) / totals).astype(BF16)
    tail = 3 + FF // D
    hidden = [jax.nn.gelu(through(i)).astype(BF16) for i in range(3, tail)]
    everything = jnp.concatenate([x, attended] + hidden, axis=1)
    interest = jnp.dot(everything, w_ref[tail * D :, :], preferred_element_type=F32).astype(BF16)
    interest_ref[pl.ds(pl.multiple_of(step * rows, rows), rows), :] = interest

    @pl.when(step == steps - 1)
    def _():
        base = base_ref[int(later)]
        route(valid_ref, base, own_ref, other_ref, interest_ref, history, start)


def route(valid_ref, base, own_ref, other_ref, interest_ref, history, start):
    lanes = GROUP * history
    groups = BLOCK // GROUP
    blocks = range(interest_ref.shape[0] // (BLOCK * history))
    lane = lax.broadcasted_iota(jnp.int32, (BLOCK, lanes), 1)
    user = lax.broadcasted_iota(jnp.int32, (BLOCK, lanes), 0)
    mine = (lane // history) == (user % GROUP)
    in_group = [(user // GROUP) == g for g in range(groups)]
    base = jnp.broadcast_to(base[:, None, :], (CAPS, BLOCK, lanes))
    logits = [base for _ in blocks]
    valid = []
    for b in blocks:
        at = slice(start + b * BLOCK, start + (b + 1) * BLOCK)
        real = mine & (valid_ref[at, :] > 0.0)
        valid.append([(real & here).astype(F32)[None] for here in in_group])

    def vectors(b, g):
        return interest_ref[(b * groups + g) * lanes : (b * groups + g + 1) * lanes, :]

    def softmax(x):
        weights = jnp.exp(x - jnp.max(x, axis=0, keepdims=True))
        return weights / jnp.sum(weights, axis=0, keepdims=True)

    def parts(weights, b):
        return [split((weights * v).reshape(CAPS * BLOCK, lanes)) for v in valid[b]]

    def squash(summed):
        squares = jnp.sum(summed * summed, axis=1, keepdims=True)
        return summed * (jnp.sqrt(squares) / (1.0 + squares))

    for sweep in range(ITERS):
        if sweep == 0:
            weights = [softmax(base)] * len(logits)
        else:
            weights = [softmax(x) for x in logits]
        weighted = [parts(weights[b], b) for b in blocks]
        summed = [
            joined(
                sum(
                    jnp.dot(weighted[b][g], vectors(b, g), preferred_element_type=F32)
                    for g in range(groups)
                )
            )
            for b in blocks
        ]
        capsules = [squash(x) for x in summed]
        if sweep + 1 < ITERS:
            caps = [split(x) for x in capsules]
            near = [
                [
                    lax.dot_general(
                        caps[b], vectors(b, g), (((1,), (1,)), ((), ())), preferred_element_type=F32
                    )
                    for g in range(groups)
                ]
                for b in blocks
            ]
            for b in blocks:
                added = [joined(x).reshape(CAPS, BLOCK, lanes) for x in near[b]]
                chosen = added[-1]
                for g in range(groups - 1):
                    chosen = jnp.where(in_group[g][None], added[g], chosen)
                logits[b] = logits[b] + chosen
    half = D // 2
    low_own = lax.axis_index("dev") == 0
    for b in blocks:
        made = capsules[b].reshape(CAPS, BLOCK, D)
        low, high = made[:, :, :half], made[:, :, half:]
        kept, passed = jnp.where(low_own, low, high), jnp.where(low_own, high, low)
        for j in range(CAPS):
            at = slice(start + b * BLOCK, start + (b + 1) * BLOCK)
            own_ref[at, j, :] = kept[j]
            other_ref[at, j, :] = passed[j]


def encode(parts, valid, base, weights, steps, start, before):
    later = len(before) > 0
    rows = len(parts) * parts[0].size // D
    vmem = pl.BlockSpec(memory_space=pltpu.VMEM)
    operands = [valid, base, weights, *before, *parts]
    made = pltpu.VMEM((valid.shape[0], CAPS, D // 2), F32)
    return pl.pallas_call(
        functools.partial(encode_kernel, steps=steps, start=start, later=later),
        out_shape=[made, made],
        grid=(steps,),
        in_specs=[vmem] * len(operands),
        out_specs=[vmem] * 2,
        scratch_shapes=[pltpu.VMEM((rows, D), BF16)],
        compiler_params=pltpu.CompilerParams(vmem_limit_bytes=24 << 20),
        name="encode",
    )(*operands)


def body(
    features, item_ids, item_table, lengths, routing_seed, w_qkv, w_out, w_bilinear, w_up, w_down
):
    pa_count = lax.axis_size("pa")
    dev_count = lax.axis_size("dev")
    spots = features.shape[1]
    per_core = lengths.shape[0] // (pa_count * dev_count)
    core = lax.axis_index("dev").astype(jnp.int32)
    swap = [(i, dev_count - 1 - i) for i in range(dev_count)]
    own = (w_qkv, w_out, w_bilinear, w_up, w_down)
    cut = per_core * FIRST[0] // FIRST[1]
    ids = item_ids.T
    counts = (pa_count, dev_count)
    sent = lookup(ids, features, item_table, 0, cut, *counts, False)[0]
    got = lax.all_to_all(sent, "pa", split_axis=0, concat_axis=0, tiled=True)
    got = got.reshape(pa_count, cut, spots, D)
    other = tuple(lax.ppermute(w, "dev", swap) for w in own)
    weights, valid, base = finish_weights(
        own, other, lengths.reshape(pa_count, -1), routing_seed, cut, per_core
    )
    ids, weights, valid, base = lax.optimization_barrier((ids, weights, valid, base))
    late = lookup(ids, features, item_table, cut, per_core - cut, *counts, True)
    parts = [late[0]]
    for i in range(1, pa_count):
        pairs = [
            (p, moved_to(p, i // Z_LO, i % Z_LO, pa_count)) for p in range(pa_count)
        ]
        block = late[i]
        if i > AHEAD:
            block, parts[i - AHEAD] = lax.optimization_barrier((block, parts[i - AHEAD]))
        parts.append(lax.ppermute(block, "pa", pairs))
    made = encode([got], valid, base, weights, STEPS[0], 0, ())
    kept, passed = encode(parts, valid, base, weights, STEPS[1], cut, tuple(made))
    came = lax.ppermute(passed, "dev", swap)
    out = jnp.zeros((dev_count * per_core, CAPS, D // dev_count), F32)
    out = lax.dynamic_update_slice_in_dim(out, kept, core * per_core, 0)
    return lax.dynamic_update_slice_in_dim(out, came, (1 - core) * per_core, 0)


def solution(mesh):
    in_specs = (
        P("au", "pa", None),
        P("au", "pa"),
        P(),
        P("au"),
        P(),
        P(None, None, "dev"),
        P("dev", None),
        P(None, "dev"),
        P(None, "dev"),
        P("dev", None),
    )
    out_specs = P(("au", "pa"), None, "dev")
    return jax.shard_map(body, mesh=mesh, in_specs=in_specs, out_specs=out_specs, check_vma=False)
```

```python
import functools

import jax
import jax.numpy as jnp
from jax import lax
from jax.experimental import pallas as pl
from jax.experimental.pallas import tpu as pltpu
from jax.sharding import PartitionSpec as P

D = 256
HEADS = 4
FF = 1024
CAPS = 4
ITERS = 3
FIRST = (4, 8)
BLOCK = 8
STEPS = (2, 2)
TABLE_PARTS = 4
AHEAD = 5
Z_LO = 2
GROUP = 4
F32 = jnp.float32
BF16 = jnp.bfloat16


def in_hbm(*arrays):
    return tuple(pltpu.with_memory_space_constraint(a, pltpu.HBM) for a in arrays)


def moved_to(place, along, across, count):
    rest = count // Z_LO
    return (place // Z_LO + along + rest) % rest * Z_LO + (place % Z_LO + across) % Z_LO


def lookup_kernel(
    ids_hbm, feat_hbm, table_hbm, *refs, cut, per_pair, per_core
):
    refs, scratch = refs[:-9], refs[-9:]
    first_hbm, late_hbm = refs[0], refs[1:]
    wide, table, table_sem, ids, feat, out, id_sem, feat_sem, out_sem = scratch
    pairs, users, spots, _ = feat.shape
    place = lax.axis_index("pa")
    offset = lax.axis_index("dev") * per_core
    rows = table.shape[0] // TABLE_PARTS
    fetch_ids = pltpu.make_async_copy(ids_hbm, ids, id_sem)
    fetch_ids.start()
    fetch_table, fetch_feat, send = [], [], []
    for i in range(TABLE_PARTS):
        at = pl.ds(i * rows, rows)
        fetch_table.append(pltpu.make_async_copy(table_hbm.at[at], table.at[at], table_sem.at[i]))
        fetch_table[-1].start()
    for d in range(pairs):
        at = pl.ds(d * per_pair + offset, users)
        fetch_feat.append(pltpu.make_async_copy(feat_hbm.at[at], feat.at[d], feat_sem.at[d]))
        fetch_feat[-1].start()
    for i, fetch in enumerate(fetch_table):
        fetch.wait()

        def widen(j, carry, i=i):
            at = pl.ds(pl.multiple_of(i * rows + j * 128, 128), 128)
            for h in range(2):
                wide[h, at, :] = table[at, h * (D // 2) : (h + 1) * (D // 2)].astype(F32)
            return carry

        lax.fori_loop(0, rows // 128, widen, 0)
    fetch_ids.wait()
    spot = lax.broadcasted_iota(jnp.int32, (spots, D // 2), 0)

    def add(slot, owner, start, stop, target, sem):
        first = owner * per_pair + offset

        def one(user, carry):
            halves = [None, None]
            for p in range(spots):
                at = pl.ds(ids[p, first + user], 1)
                for h in range(2):
                    row = jnp.broadcast_to(wide[h, at, :], (spots, D // 2))
                    halves[h] = row if p == 0 else jnp.where(spot == p, row, halves[h])
            rows = jnp.concatenate(halves, axis=1)
            out[slot, user] = (feat[owner, user].astype(F32) + rows).astype(BF16)
            return carry

        lax.fori_loop(start, stop, one, 0, unroll=8)
        send.append(pltpu.make_async_copy(out.at[slot, pl.ds(start, stop - start)], target, sem))
        send[-1].start()

    for d in range(pairs):
        fetch_feat[d].wait()
        add(d, d, 0, cut, first_hbm.at[pl.ds(d * cut, cut)], out_sem.at[0, d])
    for i in range(pairs):
        owner = moved_to(place, i // Z_LO, i % Z_LO, pairs)
        add(i, owner, cut, users, late_hbm[i], out_sem.at[1, i])
    for copy in send:
        copy.wait()


def lookup(ids, features, table, cut, pa_count, dev_count):
    all_users, spots, width = features.shape
    per_pair = all_users // pa_count
    per_core = per_pair // dev_count
    block = (pa_count, per_core, spots, width)
    hbm = pl.BlockSpec(memory_space=pltpu.HBM)
    late = pltpu.HBM((per_core - cut, spots, width), BF16)
    made = [pltpu.HBM((cut * pa_count, spots, width), BF16)] + [late] * pa_count
    return pl.pallas_call(
        functools.partial(lookup_kernel, cut=cut, per_pair=per_pair, per_core=per_core),
        out_shape=made,
        in_specs=[hbm, hbm, hbm],
        out_specs=[hbm] * len(made),
        scratch_shapes=[
            pltpu.VMEM((2, table.shape[0], D // 2), F32),
            pltpu.VMEM(table.shape, BF16),
            pltpu.SemaphoreType.DMA((TABLE_PARTS,)),
            pltpu.SMEM(ids.shape, jnp.int32),
            pltpu.VMEM(block, BF16),
            pltpu.VMEM(block, BF16),
            pltpu.SemaphoreType.DMA,
            pltpu.SemaphoreType.DMA((pa_count,)),
            pltpu.SemaphoreType.DMA((2, pa_count)),
        ],
        compiler_params=pltpu.CompilerParams(vmem_limit_bytes=14 << 20),
        name="lookup",
    )(*in_hbm(ids, features, table))


def weights_kernel(
    lens_ref, seed_ref, qkv_a, qkv_b, out_a, out_b, bil_a, bil_b, up_a, up_b, down_a, down_b,
    all_ref, valid_ref, base_ref, *, cut,
):
    pairs = lens_ref.shape[0]
    history = seed_ref.shape[1]
    spots = history // pairs
    place = lax.axis_index("pa")

    def arrival(lane):
        position = lane % history
        for i in range(pairs):
            origin = moved_to(place, -(i // Z_LO), i % Z_LO, pairs)
            here = (lane % history) // spots == i
            position = jnp.where(here, origin * spots + lane % spots, position)
        return position

    owned = (valid_ref.shape[0], lens_ref.shape[1])
    at = lax.broadcasted_iota(jnp.int32, owned, 0) + lax.axis_index("dev") * owned[0]
    near = lax.broadcasted_iota(jnp.int32, owned, 1) == at
    row = jnp.broadcast_to(lens_ref[pl.ds(place, 1), :].astype(F32), owned)
    lens = jnp.sum(jnp.where(near, row, 0.0), axis=1, keepdims=True)
    lane = lax.broadcasted_iota(jnp.int32, valid_ref.shape, 1)
    first = lax.broadcasted_iota(jnp.int32, valid_ref.shape, 0) < cut
    position = jnp.where(first, lane % history, arrival(lane))
    valid_ref[...] = (position.astype(F32) < lens).astype(F32)

    seed = seed_ref[...].astype(F32)
    chosen = lax.broadcasted_iota(jnp.int32, (history, history), 0) == arrival(
        lax.broadcasted_iota(jnp.int32, (history, history), 1)
    )
    moved = jnp.dot(
        seed.astype(BF16), chosen.astype(F32).astype(BF16), preferred_element_type=F32
    )
    for i, table in enumerate((seed, moved)):
        base_ref[i] = jnp.concatenate([(table - 7.5) * 0.25] * GROUP, axis=1)

    half = D // 2
    low = lax.axis_index("dev") == 0
    at = 0
    for i in range(3):
        all_ref[at : at + D, :half] = qkv_a[i]
        all_ref[at : at + D, half:] = qkv_b[i]
        at += D
    for up in (up_a, up_b):
        for i in range(up.shape[1] // D):
            all_ref[at : at + D, :] = up[:, i * D : (i + 1) * D]
            at += D

    @pl.when(low)
    def _():
        all_ref[at : at + D, :half] = bil_a[...]
        all_ref[at : at + D, half:] = bil_b[...]

    @pl.when(jnp.logical_not(low))
    def _():
        all_ref[at : at + D, :half] = bil_b[...]
        all_ref[at : at + D, half:] = bil_a[...]

    after = at + D
    for rows in (out_a, out_b, down_a, down_b):
        all_ref[after : after + rows.shape[0], :] = rows[...]
        after += rows.shape[0]


def finish_weights(own, other, lens, seed, cut, per_core):
    ff = own[3].shape[1]
    operands = [*in_hbm(lens, seed)] + [w for pair in zip(in_hbm(*own), other) for w in pair]
    vmem = pl.BlockSpec(memory_space=pltpu.VMEM)
    lanes = GROUP * seed.shape[1]
    return pl.pallas_call(
        functools.partial(weights_kernel, cut=cut),
        out_shape=[
            pltpu.VMEM((5 * D + 4 * ff, D), BF16),
            pltpu.VMEM((per_core, lanes), F32),
            pltpu.VMEM((2, CAPS, lanes), F32),
        ],
        in_specs=[vmem] * len(operands),
        out_specs=[vmem] * 3,
        compiler_params=pltpu.CompilerParams(vmem_limit_bytes=8 << 20),
        name="weights",
    )(*operands)


def split(x):
    high = x.astype(BF16)
    return jnp.concatenate([high, (x - high.astype(F32)).astype(BF16)], axis=0)


def joined(x):
    half = x.shape[0] // 2
    return x[:half] + x[half:]


def encode_kernel(*refs, steps, start, later):
    valid_ref, base_ref, w_ref = refs[:3]
    parts = refs[3 + (2 if later else 0) : -3]
    own_ref, other_ref, interest_ref = refs[-3:]
    step = pl.program_id(0)
    if later:
        own_ref[:start] = refs[3][:start]
        other_ref[:start] = refs[4][:start]
        pairs, (all_users, spots, _) = len(parts), parts[0].shape
    else:
        pairs, all_users, spots, _ = parts[0].shape
    block = all_users // steps
    history = pairs * spots
    rows = block * history
    head = D // HEADS
    lanes = HEADS * history
    at = pl.ds(step * block, block)
    if later:
        x = jnp.stack([part[at].astype(F32) for part in parts], axis=1)
    else:
        x = jnp.swapaxes(parts[0][:, at].astype(F32), 0, 1)
    x = x.reshape(rows, D).astype(BF16)

    def through(i):
        return jnp.dot(x, w_ref[i * D : (i + 1) * D, :], preferred_element_type=F32)

    queries = (through(0) * (1.0 / head**0.5)).astype(BF16)
    keys = through(1).astype(BF16)
    values = through(2).astype(BF16)

    lane_head = lax.broadcasted_iota(jnp.int32, (history, D), 1) // head
    own_head = [(lane_head == h).astype(F32).astype(BF16) for h in range(HEADS)]
    odd_even = [own_head[0] + own_head[2], own_head[1] + own_head[3]]
    row_head = lax.broadcasted_iota(jnp.int32, (lanes, D), 0) // history
    col_head = lax.broadcasted_iota(jnp.int32, (lanes, D), 1) // head
    ones = (row_head == col_head).astype(F32).astype(BF16)
    key_valid = valid_ref[pl.ds(start + step * block, block), :]
    users = [slice(u * history, (u + 1) * history) for u in range(block)]
    scores = []
    none = jnp.zeros((history, D // 2), BF16)
    for first in range(0, block, 2):
        pair = users[first : first + 2]
        key_wide = jnp.concatenate([keys[at] * m for at in pair for m in odd_even], axis=0)
        query_wide = jnp.concatenate(
            [
                part
                for at in pair
                for part in (
                    jnp.concatenate([queries[at, : D // 2], none], axis=1),
                    jnp.concatenate([none, queries[at, D // 2 :]], axis=1),
                )
            ],
            axis=0,
        )
        both = lax.dot_general(
            query_wide, key_wide, (((1,), (1,)), ((), ())), preferred_element_type=F32
        )
        for u in range(2):
            rows_u = both[u * D // 2 : (u + 1) * D // 2, u * D // 2 : (u + 1) * D // 2]
            scores.append(jnp.concatenate([rows_u[:history], rows_u[history:]], axis=1))
    rounded = [
        jnp.where(key_valid[u : u + 1] > 0.0, jnp.exp(s), 0.0).astype(BF16)
        for u, s in enumerate(scores)
    ]
    totals = jnp.dot(jnp.concatenate(rounded, axis=0), ones, preferred_element_type=F32)
    weighted = []
    for first in range(0, block, 2):
        pair = users[first : first + 2]
        value_wide = jnp.concatenate([values[at] * m for at in pair for m in odd_even], axis=0)
        prob_wide = []
        for u in range(2):
            for g in range(2):
                part = rounded[first + u][:, g * D // 2 : (g + 1) * D // 2]
                prob_wide.append(jnp.concatenate([part, none] if u == 0 else [none, part], axis=1))
        both = jnp.dot(jnp.concatenate(prob_wide, axis=0), value_wide, preferred_element_type=F32)
        for u in range(2):
            rows_u = both[u * D // 2 : (u + 1) * D // 2]
            weighted.append(
                jnp.concatenate([rows_u[:history, : D // 2], rows_u[history:, D // 2 :]], axis=1)
            )
    attended = (jnp.concatenate(weighted, axis=0) / totals).astype(BF16)
    tail = 3 + FF // D
    hidden = [jax.nn.gelu(through(i)).astype(BF16) for i in range(3, tail)]
    everything = jnp.concatenate([x, attended] + hidden, axis=1)
    interest = jnp.dot(everything, w_ref[tail * D :, :], preferred_element_type=F32).astype(BF16)
    interest_ref[pl.ds(pl.multiple_of(step * rows, rows), rows), :] = interest

    @pl.when(step == steps - 1)
    def _():
        base = base_ref[int(later)]
        route(valid_ref, base, own_ref, other_ref, interest_ref, history, start)


def route(valid_ref, base, own_ref, other_ref, interest_ref, history, start):
    lanes = GROUP * history
    groups = BLOCK // GROUP
    blocks = range(interest_ref.shape[0] // (BLOCK * history))
    lane = lax.broadcasted_iota(jnp.int32, (BLOCK, lanes), 1)
    user = lax.broadcasted_iota(jnp.int32, (BLOCK, lanes), 0)
    mine = (lane // history) == (user % GROUP)
    in_group = [(user // GROUP) == g for g in range(groups)]
    base = jnp.broadcast_to(base[:, None, :], (CAPS, BLOCK, lanes))
    logits = [base for _ in blocks]
    valid = []
    for b in blocks:
        at = slice(start + b * BLOCK, start + (b + 1) * BLOCK)
        real = mine & (valid_ref[at, :] > 0.0)
        valid.append([(real & here).astype(F32)[None] for here in in_group])

    def vectors(b, g):
        return interest_ref[(b * groups + g) * lanes : (b * groups + g + 1) * lanes, :]

    def softmax(x):
        weights = jnp.exp(x - jnp.max(x, axis=0, keepdims=True))
        return weights / jnp.sum(weights, axis=0, keepdims=True)

    def parts(weights, b):
        return [split((weights * v).reshape(CAPS * BLOCK, lanes)) for v in valid[b]]

    def squash(summed):
        squares = jnp.sum(summed * summed, axis=1, keepdims=True)
        return summed * (jnp.sqrt(squares) / (1.0 + squares))

    for sweep in range(ITERS):
        if sweep == 0:
            weights = [softmax(base)] * len(logits)
        else:
            weights = [softmax(x) for x in logits]
        weighted = [parts(weights[b], b) for b in blocks]
        summed = [
            joined(
                sum(
                    jnp.dot(weighted[b][g], vectors(b, g), preferred_element_type=F32)
                    for g in range(groups)
                )
            )
            for b in blocks
        ]
        capsules = [squash(x) for x in summed]
        if sweep + 1 < ITERS:
            caps = [split(x) for x in capsules]
            near = [
                [
                    lax.dot_general(
                        caps[b], vectors(b, g), (((1,), (1,)), ((), ())), preferred_element_type=F32
                    )
                    for g in range(groups)
                ]
                for b in blocks
            ]
            for b in blocks:
                added = [joined(x).reshape(CAPS, BLOCK, lanes) for x in near[b]]
                chosen = added[-1]
                for g in range(groups - 1):
                    chosen = jnp.where(in_group[g][None], added[g], chosen)
                logits[b] = logits[b] + chosen
    half = D // 2
    low_own = lax.axis_index("dev") == 0
    for b in blocks:
        made = capsules[b].reshape(CAPS, BLOCK, D)
        low, high = made[:, :, :half], made[:, :, half:]
        kept, passed = jnp.where(low_own, low, high), jnp.where(low_own, high, low)
        for j in range(CAPS):
            at = slice(start + b * BLOCK, start + (b + 1) * BLOCK)
            own_ref[at, j, :] = kept[j]
            other_ref[at, j, :] = passed[j]


def encode(parts, valid, base, weights, steps, start, before):
    later = len(before) > 0
    rows = len(parts) * parts[0].size // D
    vmem = pl.BlockSpec(memory_space=pltpu.VMEM)
    parts = [pltpu.with_memory_space_constraint(p, pltpu.VMEM) for p in parts]
    operands = [valid, base, weights, *before, *parts]
    made = pltpu.VMEM((valid.shape[0], CAPS, D // 2), F32)
    return pl.pallas_call(
        functools.partial(encode_kernel, steps=steps, start=start, later=later),
        out_shape=[made, made],
        grid=(steps,),
        in_specs=[vmem] * len(operands),
        out_specs=[vmem] * 2,
        scratch_shapes=[pltpu.VMEM((rows, D), BF16)],
        compiler_params=pltpu.CompilerParams(vmem_limit_bytes=24 << 20),
        name="encode",
    )(*operands)


def body(
    features, item_ids, item_table, lengths, routing_seed, w_qkv, w_out, w_bilinear, w_up, w_down
):
    pa_count = lax.axis_size("pa")
    dev_count = lax.axis_size("dev")
    spots = features.shape[1]
    per_core = lengths.shape[0] // (pa_count * dev_count)
    core = lax.axis_index("dev").astype(jnp.int32)
    swap = [(i, dev_count - 1 - i) for i in range(dev_count)]
    own = (w_qkv, w_out, w_bilinear, w_up, w_down)
    cut = per_core * FIRST[0] // FIRST[1]
    sent, *late = lookup(item_ids.T, features, item_table, cut, pa_count, dev_count)
    got = lax.all_to_all(sent, "pa", split_axis=0, concat_axis=0, tiled=True)
    got = got.reshape(pa_count, cut, spots, D)
    other = tuple(lax.ppermute(w, "dev", swap) for w in own)
    weights, valid, base = finish_weights(
        own, other, lengths.reshape(pa_count, -1), routing_seed, cut, per_core
    )
    late, weights, valid, base = lax.optimization_barrier((late, weights, valid, base))
    parts = [late[0]]
    for i in range(1, pa_count):
        pairs = [
            (p, moved_to(p, i // Z_LO, i % Z_LO, pa_count)) for p in range(pa_count)
        ]
        block = late[i]
        if i > AHEAD:
            block, parts[i - AHEAD] = lax.optimization_barrier((block, parts[i - AHEAD]))
        parts.append(lax.ppermute(block, "pa", pairs))
    made = encode([got], valid, base, weights, STEPS[0], 0, ())
    kept, passed = encode(parts, valid, base, weights, STEPS[1], cut, tuple(made))
    came = lax.ppermute(passed, "dev", swap)
    out = jnp.zeros((dev_count * per_core, CAPS, D // dev_count), F32)
    out = lax.dynamic_update_slice_in_dim(out, kept, core * per_core, 0)
    return lax.dynamic_update_slice_in_dim(out, came, (1 - core) * per_core, 0)


def solution(mesh):
    in_specs = (
        P("au", "pa", None),
        P("au", "pa"),
        P(),
        P("au"),
        P(),
        P(None, None, "dev"),
        P("dev", None),
        P(None, "dev"),
        P(None, "dev"),
        P("dev", None),
    )
    out_specs = P(("au", "pa"), None, "dev")
    return jax.shard_map(body, mesh=mesh, in_specs=in_specs, out_specs=out_specs, check_vma=False)
```

```python
import functools

import jax
import jax.numpy as jnp
from jax import lax
from jax.experimental import pallas as pl
from jax.experimental.pallas import tpu as pltpu
from jax.sharding import PartitionSpec as P

D = 256
HEADS = 4
FF = 1024
CAPS = 4
ITERS = 3
FIRST = (4, 8)
BLOCK = 8
STEPS = (2, 2)
TABLE_PARTS = 4
AHEAD = 5
Z_LO = 2
GROUP = 4
F32 = jnp.float32
BF16 = jnp.bfloat16


def in_hbm(*arrays):
    return tuple(pltpu.with_memory_space_constraint(a, pltpu.HBM) for a in arrays)


def moved_to(place, along, across, count):
    rest = count // Z_LO
    return (place // Z_LO + along + rest) % rest * Z_LO + (place % Z_LO + across) % Z_LO


def packed_pieces(qkv, out, bilinear, up, down):
    half = D // 2
    pieces = [qkv.at[i] for i in range(3)] + [bilinear]
    for w in (up, out, down):
        pieces += [w.at[:, pl.ds(i, half)] for i in range(0, w.shape[1], half)]
    return pieces


def lookup_kernel(*refs, start, per_pair, per_core, outs):
    later = outs > 1
    ids_hbm, feat_hbm, table_hbm, refs = *refs[:3], refs[3:]
    if not later:
        own, refs = refs[:5], refs[5:]
    out_hbm, refs = refs[:outs], refs[outs:]
    pack = []
    if not later:
        packed, pack_sem, refs = refs[0], refs[-1], refs[1:-1]
        at = 0
        for piece in packed_pieces(*own):
            target = packed.at[pl.ds(at, piece.shape[0])]
            pack.append(pltpu.make_async_copy(piece, target, pack_sem.at[len(pack)]))
            at += piece.shape[0]
    wide, table, table_sem, ids, feat, out, id_sem, feat_sem, out_sem = refs
    pairs, users, spots, _ = feat.shape
    place = lax.axis_index("pa")
    offset = lax.axis_index("dev") * per_core + start
    if later:
        owners = [moved_to(place, i // Z_LO, i % Z_LO, pairs) for i in range(pairs)]
    else:
        owners = list(range(pairs))
    fetch_ids = pltpu.make_async_copy(ids_hbm, ids, id_sem)
    fetch_ids.start()
    fetch_table = []
    rows = table.shape[0] // TABLE_PARTS
    for i in range(TABLE_PARTS):
        at = pl.ds(i * rows, rows)
        fetch_table.append(pltpu.make_async_copy(table_hbm.at[at], table.at[at], table_sem.at[i]))
        fetch_table[-1].start()
    for copy in pack:
        copy.start()
    fetch_feat = []
    for d in range(pairs):
        at = pl.ds(owners[d] * per_pair + offset, users)
        fetch_feat.append(pltpu.make_async_copy(feat_hbm.at[at], feat.at[d], feat_sem.at[d]))
        fetch_feat[-1].start()
    for i, fetch in enumerate(fetch_table):
        fetch.wait()

        def widen(j, carry, i=i):
            at = pl.ds(pl.multiple_of(i * rows + j * 128, 128), 128)
            for h in range(2):
                wide[h, at, :] = table[at, h * (D // 2) : (h + 1) * (D // 2)].astype(F32)
            return carry

        lax.fori_loop(0, rows // 128, widen, 0)
    fetch_ids.wait()
    spot = lax.broadcasted_iota(jnp.int32, (spots, D // 2), 0)
    send = []
    for d in range(pairs):
        fetch_feat[d].wait()
        first = owners[d] * per_pair + offset

        def one(user, carry, d=d, first=first):
            halves = [None, None]
            for p in range(spots):
                at = pl.ds(ids[p, first + user], 1)
                for h in range(2):
                    row = jnp.broadcast_to(wide[h, at, :], (spots, D // 2))
                    halves[h] = row if p == 0 else jnp.where(spot == p, row, halves[h])
            rows = jnp.concatenate(halves, axis=1)
            out[d, user] = (feat[d, user].astype(F32) + rows).astype(BF16)
            return carry

        lax.fori_loop(0, users, one, 0, unroll=8)
        if later:
            target = out_hbm[d]
        else:
            target = out_hbm[0].at[pl.ds(d * users, users)]
        send.append(pltpu.make_async_copy(out.at[d], target, out_sem.at[d]))
        send[-1].start()
    for copy in send + pack:
        copy.wait()


def lookup(ids, features, table, start, users, pa_count, dev_count, later, own=()):
    all_users, spots, width = features.shape
    per_pair = all_users // pa_count
    per_core = per_pair // dev_count
    block = (pa_count, users, spots, width)
    hbm = pl.BlockSpec(memory_space=pltpu.HBM)
    outs = pa_count if later else 1
    made = [pltpu.HBM((users * (1 if later else pa_count), spots, width), BF16)] * outs
    if own:
        made.append(pltpu.HBM((sum(w.size for w in own) // (D // 2), D // 2), BF16))
    scratch = [
        pltpu.VMEM((2, table.shape[0], D // 2), F32),
        pltpu.VMEM(table.shape, BF16),
        pltpu.SemaphoreType.DMA((TABLE_PARTS,)),
        pltpu.SMEM(ids.shape, jnp.int32),
        pltpu.VMEM(block, BF16),
        pltpu.VMEM(block, BF16),
        pltpu.SemaphoreType.DMA,
        pltpu.SemaphoreType.DMA((pa_count,)),
        pltpu.SemaphoreType.DMA((pa_count,)),
    ]
    if own:
        pieces = 4 + sum(w.shape[1] // (D // 2) for w in (own[1], own[3], own[4]))
        scratch.append(pltpu.SemaphoreType.DMA((pieces,)))
    return pl.pallas_call(
        functools.partial(
            lookup_kernel, start=start, per_pair=per_pair, per_core=per_core, outs=outs
        ),
        out_shape=made,
        in_specs=[hbm] * (3 + len(own)),
        out_specs=[hbm] * len(made),
        scratch_shapes=scratch,
        compiler_params=pltpu.CompilerParams(vmem_limit_bytes=12 << 20),
        name="lookup",
    )(*in_hbm(ids, features, table, *own))


def weights_kernel(
    lens_ref, seed_ref, own, other, all_ref, valid_ref, base_ref, *, cut, ff
):
    pairs = lens_ref.shape[0]
    history = seed_ref.shape[1]
    spots = history // pairs
    place = lax.axis_index("pa")

    def arrival(lane):
        position = lane % history
        for i in range(pairs):
            origin = moved_to(place, -(i // Z_LO), i % Z_LO, pairs)
            here = (lane % history) // spots == i
            position = jnp.where(here, origin * spots + lane % spots, position)
        return position

    owned = (valid_ref.shape[0], lens_ref.shape[1])
    at = lax.broadcasted_iota(jnp.int32, owned, 0) + lax.axis_index("dev") * owned[0]
    near = lax.broadcasted_iota(jnp.int32, owned, 1) == at
    row = jnp.broadcast_to(lens_ref[pl.ds(place, 1), :].astype(F32), owned)
    lens = jnp.sum(jnp.where(near, row, 0.0), axis=1, keepdims=True)
    lane = lax.broadcasted_iota(jnp.int32, valid_ref.shape, 1)
    first = lax.broadcasted_iota(jnp.int32, valid_ref.shape, 0) < cut
    position = jnp.where(first, lane % history, arrival(lane))
    valid_ref[...] = (position.astype(F32) < lens).astype(F32)

    seed = seed_ref[...].astype(F32)
    chosen = lax.broadcasted_iota(jnp.int32, (history, history), 0) == arrival(
        lax.broadcasted_iota(jnp.int32, (history, history), 1)
    )
    moved = jnp.dot(
        seed.astype(BF16), chosen.astype(F32).astype(BF16), preferred_element_type=F32
    )
    for i, table in enumerate((seed, moved)):
        base_ref[i] = jnp.concatenate([(table - 7.5) * 0.25] * GROUP, axis=1)

    half = D // 2
    low = lax.axis_index("dev") == 0
    at = 0
    for i in range(3):
        all_ref[at : at + D, :half] = own[at : at + D]
        all_ref[at : at + D, half:] = other[at : at + D]
        at += D
    bilinear = slice(at, at + D)
    source = at + D
    for part in (own, other):
        for i in range(ff // D):
            for h in range(2):
                rows = slice(source + (2 * i + h) * D, source + (2 * i + h + 1) * D)
                all_ref[at : at + D, h * half : (h + 1) * half] = part[rows]
            at += D

    @pl.when(low)
    def _():
        all_ref[at : at + D, :half] = own[bilinear]
        all_ref[at : at + D, half:] = other[bilinear]

    @pl.when(jnp.logical_not(low))
    def _():
        all_ref[at : at + D, :half] = other[bilinear]
        all_ref[at : at + D, half:] = own[bilinear]

    after = at + D
    source += 2 * ff
    for count in (half, ff):
        for part in (own, other):
            for h in range(2):
                rows = slice(source + h * count, source + (h + 1) * count)
                all_ref[after : after + count, h * half : (h + 1) * half] = part[rows]
            after += count
        source += 2 * count


def finish_weights(own, other, lens, seed, cut, per_core, ff):
    operands = in_hbm(lens, seed, own, other)
    vmem = pl.BlockSpec(memory_space=pltpu.VMEM)
    lanes = GROUP * seed.shape[1]
    return pl.pallas_call(
        functools.partial(weights_kernel, cut=cut, ff=ff),
        out_shape=[
            pltpu.VMEM((5 * D + 4 * ff, D), BF16),
            pltpu.VMEM((per_core, lanes), F32),
            pltpu.VMEM((2, CAPS, lanes), F32),
        ],
        in_specs=[vmem] * len(operands),
        out_specs=[vmem] * 3,
        compiler_params=pltpu.CompilerParams(vmem_limit_bytes=8 << 20),
        name="weights",
    )(*operands)


def split(x):
    high = x.astype(BF16)
    return jnp.concatenate([high, (x - high.astype(F32)).astype(BF16)], axis=0)


def joined(x):
    half = x.shape[0] // 2
    return x[:half] + x[half:]


def encode_kernel(*refs, steps, start, later):
    valid_ref, base_ref, w_ref = refs[:3]
    parts = refs[3 + (2 if later else 0) : -3]
    own_ref, other_ref, interest_ref = refs[-3:]
    step = pl.program_id(0)
    if later:
        own_ref[:start] = refs[3][:start]
        other_ref[:start] = refs[4][:start]
        pairs, (all_users, spots, _) = len(parts), parts[0].shape
    else:
        pairs, all_users, spots, _ = parts[0].shape
    block = all_users // steps
    history = pairs * spots
    rows = block * history
    head = D // HEADS
    lanes = HEADS * history
    at = pl.ds(step * block, block)
    if later:
        x = jnp.stack([part[at].astype(F32) for part in parts], axis=1)
    else:
        x = jnp.swapaxes(parts[0][:, at].astype(F32), 0, 1)
    x = x.reshape(rows, D).astype(BF16)

    def through(i):
        return jnp.dot(x, w_ref[i * D : (i + 1) * D, :], preferred_element_type=F32)

    queries = (through(0) * (1.0 / head**0.5)).astype(BF16)
    keys = through(1).astype(BF16)
    values = through(2).astype(BF16)

    lane_head = lax.broadcasted_iota(jnp.int32, (history, D), 1) // head
    own_head = [(lane_head == h).astype(F32).astype(BF16) for h in range(HEADS)]
    odd_even = [own_head[0] + own_head[2], own_head[1] + own_head[3]]
    row_head = lax.broadcasted_iota(jnp.int32, (lanes, D), 0) // history
    col_head = lax.broadcasted_iota(jnp.int32, (lanes, D), 1) // head
    ones = (row_head == col_head).astype(F32).astype(BF16)
    key_valid = valid_ref[pl.ds(start + step * block, block), :]
    users = [slice(u * history, (u + 1) * history) for u in range(block)]
    scores = []
    none = jnp.zeros((history, D // 2), BF16)
    for first in range(0, block, 2):
        pair = users[first : first + 2]
        key_wide = jnp.concatenate([keys[at] * m for at in pair for m in odd_even], axis=0)
        query_wide = jnp.concatenate(
            [
                part
                for at in pair
                for part in (
                    jnp.concatenate([queries[at, : D // 2], none], axis=1),
                    jnp.concatenate([none, queries[at, D // 2 :]], axis=1),
                )
            ],
            axis=0,
        )
        both = lax.dot_general(
            query_wide, key_wide, (((1,), (1,)), ((), ())), preferred_element_type=F32
        )
        for u in range(2):
            rows_u = both[u * D // 2 : (u + 1) * D // 2, u * D // 2 : (u + 1) * D // 2]
            scores.append(jnp.concatenate([rows_u[:history], rows_u[history:]], axis=1))
    rounded = [
        jnp.where(key_valid[u : u + 1] > 0.0, jnp.exp(s), 0.0).astype(BF16)
        for u, s in enumerate(scores)
    ]
    totals = jnp.dot(jnp.concatenate(rounded, axis=0), ones, preferred_element_type=F32)
    weighted = []
    for first in range(0, block, 2):
        pair = users[first : first + 2]
        value_wide = jnp.concatenate([values[at] * m for at in pair for m in odd_even], axis=0)
        prob_wide = []
        for u in range(2):
            for g in range(2):
                part = rounded[first + u][:, g * D // 2 : (g + 1) * D // 2]
                prob_wide.append(jnp.concatenate([part, none] if u == 0 else [none, part], axis=1))
        both = jnp.dot(jnp.concatenate(prob_wide, axis=0), value_wide, preferred_element_type=F32)
        for u in range(2):
            rows_u = both[u * D // 2 : (u + 1) * D // 2]
            weighted.append(
                jnp.concatenate([rows_u[:history, : D // 2], rows_u[history:, D // 2 :]], axis=1)
            )
    attended = (jnp.concatenate(weighted, axis=0) / totals).astype(BF16)
    tail = 3 + FF // D
    hidden = [jax.nn.gelu(through(i)).astype(BF16) for i in range(3, tail)]
    everything = jnp.concatenate([x, attended] + hidden, axis=1)
    interest = jnp.dot(everything, w_ref[tail * D :, :], preferred_element_type=F32).astype(BF16)
    interest_ref[pl.ds(pl.multiple_of(step * rows, rows), rows), :] = interest

    @pl.when(step == steps - 1)
    def _():
        base = base_ref[int(later)]
        route(valid_ref, base, own_ref, other_ref, interest_ref, history, start)


def route(valid_ref, base, own_ref, other_ref, interest_ref, history, start):
    lanes = GROUP * history
    groups = BLOCK // GROUP
    blocks = range(interest_ref.shape[0] // (BLOCK * history))
    lane = lax.broadcasted_iota(jnp.int32, (BLOCK, lanes), 1)
    user = lax.broadcasted_iota(jnp.int32, (BLOCK, lanes), 0)
    mine = (lane // history) == (user % GROUP)
    in_group = [(user // GROUP) == g for g in range(groups)]
    base = jnp.broadcast_to(base[:, None, :], (CAPS, BLOCK, lanes))
    logits = [base for _ in blocks]
    valid = []
    for b in blocks:
        at = slice(start + b * BLOCK, start + (b + 1) * BLOCK)
        real = mine & (valid_ref[at, :] > 0.0)
        valid.append([(real & here).astype(F32)[None] for here in in_group])

    def vectors(b, g):
        return interest_ref[(b * groups + g) * lanes : (b * groups + g + 1) * lanes, :]

    def softmax(x):
        weights = jnp.exp(x - jnp.max(x, axis=0, keepdims=True))
        return weights / jnp.sum(weights, axis=0, keepdims=True)

    def parts(weights, b):
        return [split((weights * v).reshape(CAPS * BLOCK, lanes)) for v in valid[b]]

    def squash(summed):
        squares = jnp.sum(summed * summed, axis=1, keepdims=True)
        return summed * (jnp.sqrt(squares) / (1.0 + squares))

    for sweep in range(ITERS):
        if sweep == 0:
            weights = [softmax(base)] * len(logits)
        else:
            weights = [softmax(x) for x in logits]
        weighted = [parts(weights[b], b) for b in blocks]
        summed = [
            joined(
                sum(
                    jnp.dot(weighted[b][g], vectors(b, g), preferred_element_type=F32)
                    for g in range(groups)
                )
            )
            for b in blocks
        ]
        capsules = [squash(x) for x in summed]
        if sweep + 1 < ITERS:
            caps = [split(x) for x in capsules]
            near = [
                [
                    lax.dot_general(
                        caps[b], vectors(b, g), (((1,), (1,)), ((), ())), preferred_element_type=F32
                    )
                    for g in range(groups)
                ]
                for b in blocks
            ]
            for b in blocks:
                added = [joined(x).reshape(CAPS, BLOCK, lanes) for x in near[b]]
                chosen = added[-1]
                for g in range(groups - 1):
                    chosen = jnp.where(in_group[g][None], added[g], chosen)
                logits[b] = logits[b] + chosen
    half = D // 2
    low_own = lax.axis_index("dev") == 0
    for b in blocks:
        made = capsules[b].reshape(CAPS, BLOCK, D)
        low, high = made[:, :, :half], made[:, :, half:]
        kept, passed = jnp.where(low_own, low, high), jnp.where(low_own, high, low)
        for j in range(CAPS):
            at = slice(start + b * BLOCK, start + (b + 1) * BLOCK)
            own_ref[at, j, :] = kept[j]
            other_ref[at, j, :] = passed[j]


def encode(parts, valid, base, weights, steps, start, before):
    later = len(before) > 0
    rows = len(parts) * parts[0].size // D
    vmem = pl.BlockSpec(memory_space=pltpu.VMEM)
    operands = [valid, base, weights, *before, *parts]
    made = pltpu.VMEM((valid.shape[0], CAPS, D // 2), F32)
    return pl.pallas_call(
        functools.partial(encode_kernel, steps=steps, start=start, later=later),
        out_shape=[made, made],
        grid=(steps,),
        in_specs=[vmem] * len(operands),
        out_specs=[vmem] * 2,
        scratch_shapes=[pltpu.VMEM((rows, D), BF16)],
        compiler_params=pltpu.CompilerParams(vmem_limit_bytes=10 << 20),
        name="encode",
    )(*operands)


def body(
    features, item_ids, item_table, lengths, routing_seed, w_qkv, w_out, w_bilinear, w_up, w_down
):
    pa_count = lax.axis_size("pa")
    dev_count = lax.axis_size("dev")
    spots = features.shape[1]
    per_core = lengths.shape[0] // (pa_count * dev_count)
    core = lax.axis_index("dev").astype(jnp.int32)
    swap = [(i, dev_count - 1 - i) for i in range(dev_count)]
    own = (w_qkv, w_out, w_bilinear, w_up, w_down)
    cut = per_core * FIRST[0] // FIRST[1]
    ids = item_ids.T
    counts = (pa_count, dev_count)
    sent, packed = lookup(ids, features, item_table, 0, cut, *counts, False, own)
    got = lax.all_to_all(sent, "pa", split_axis=0, concat_axis=0, tiled=True)
    got = got.reshape(pa_count, cut, spots, D)
    other = lax.ppermute(packed, "dev", swap)
    ids, other = lax.optimization_barrier((ids, other))
    late = lookup(ids, features, item_table, cut, per_core - cut, *counts, True)
    lens, late = lax.optimization_barrier((lengths.reshape(pa_count, -1), late))
    ff = w_up.shape[1]
    weights, valid, base = finish_weights(packed, other, lens, routing_seed, cut, per_core, ff)
    parts = [late[0]]
    for i in range(1, pa_count):
        pairs = [
            (p, moved_to(p, i // Z_LO, i % Z_LO, pa_count)) for p in range(pa_count)
        ]
        block = late[i]
        if i > AHEAD:
            block, parts[i - AHEAD], valid = lax.optimization_barrier(
                (block, parts[i - AHEAD], valid)
            )
        parts.append(lax.ppermute(block, "pa", pairs))
    made = encode([got], valid, base, weights, STEPS[0], 0, ())
    kept, passed = encode(parts, valid, base, weights, STEPS[1], cut, tuple(made))
    came = lax.ppermute(passed, "dev", swap)
    out = jnp.zeros((dev_count * per_core, CAPS, D // dev_count), F32)
    out = lax.dynamic_update_slice_in_dim(out, kept, core * per_core, 0)
    return lax.dynamic_update_slice_in_dim(out, came, (1 - core) * per_core, 0)


def solution(mesh):
    in_specs = (
        P("au", "pa", None),
        P("au", "pa"),
        P(),
        P("au"),
        P(),
        P(None, None, "dev"),
        P("dev", None),
        P(None, "dev"),
        P(None, "dev"),
        P("dev", None),
    )
    out_specs = P(("au", "pa"), None, "dev")
    return jax.shard_map(body, mesh=mesh, in_specs=in_specs, out_specs=out_specs, check_vma=False)
```

```python
import functools

import jax
import jax.numpy as jnp
from jax import lax
from jax.experimental import pallas as pl
from jax.experimental.pallas import tpu as pltpu
from jax.sharding import PartitionSpec as P

D = 256
HEADS = 4
FF = 1024
CAPS = 4
ITERS = 3
FIRST = (4, 8)
BLOCK = 8
STEPS = (2, 2)
TABLE_PARTS = 2
AHEAD = 5
Z_LO = 2
GROUP = 4
F32 = jnp.float32
BF16 = jnp.bfloat16


def in_hbm(*arrays):
    return tuple(pltpu.with_memory_space_constraint(a, pltpu.HBM) for a in arrays)


def moved_to(place, along, across, count):
    rest = count // Z_LO
    return (place // Z_LO + along + rest) % rest * Z_LO + (place % Z_LO + across) % Z_LO


def packed_pieces(qkv, out, bilinear, up, down):
    half = D // 2
    pieces = [(qkv, (i,)) for i in range(3)] + [(bilinear, ())]
    for w in (up, out, down):
        pieces += [(w, (slice(None), slice(i, i + half))) for i in range(0, w.shape[1], half)]
    return pieces


def lookup_kernel(*refs, start, per_pair, per_core, outs):
    later = outs > 1
    ids_hbm, feat_hbm, table_hbm, refs = *refs[:3], refs[3:]
    if not later:
        own, refs = refs[:5], refs[5:]
    out_hbm, refs = refs[:outs], refs[outs:]
    fetch_own = []
    if not later:
        packed_hbm, held, packed, own_sem = refs[0], refs[-7:-2], refs[-2], refs[-1]
        refs = refs[1:-7]
        for i, w in enumerate(own):
            fetch_own.append(pltpu.make_async_copy(w, held[i], own_sem.at[i]))
    wide, table, table_sem, ids, feat, out, id_sem, feat_sem, out_sem = refs
    pairs, users, spots, _ = feat.shape
    place = lax.axis_index("pa")
    offset = lax.axis_index("dev") * per_core + start
    if later:
        owners = [moved_to(place, i // Z_LO, i % Z_LO, pairs) for i in range(pairs)]
    else:
        owners = list(range(pairs))
    fetch_ids = pltpu.make_async_copy(ids_hbm, ids, id_sem)
    fetch_ids.start()
    fetch_table = []
    rows = table.shape[0] // TABLE_PARTS
    for i in range(TABLE_PARTS):
        at = pl.ds(i * rows, rows)
        fetch_table.append(pltpu.make_async_copy(table_hbm.at[at], table.at[at], table_sem.at[i]))
        fetch_table[-1].start()
    for copy in fetch_own:
        copy.start()
    fetch_feat = []
    for d in range(pairs):
        at = pl.ds(owners[d] * per_pair + offset, users)
        fetch_feat.append(pltpu.make_async_copy(feat_hbm.at[at], feat.at[d], feat_sem.at[d]))
        fetch_feat[-1].start()
    for i, fetch in enumerate(fetch_table):
        fetch.wait()

        def widen(j, carry, i=i):
            at = pl.ds(pl.multiple_of(i * rows + j * 128, 128), 128)
            for h in range(2):
                wide[h, at, :] = table[at, h * (D // 2) : (h + 1) * (D // 2)].astype(F32)
            return carry

        lax.fori_loop(0, rows // 128, widen, 0)
    send = []
    if not later:
        for copy in fetch_own:
            copy.wait()
        at = 0
        for ref, index in packed_pieces(*held):
            piece = ref[(*index, Ellipsis)]
            packed[at : at + piece.shape[0], :] = piece
            at += piece.shape[0]
        send.append(pltpu.make_async_copy(packed, packed_hbm, own_sem.at[len(own)]))
        send[-1].start()
    fetch_ids.wait()
    spot = lax.broadcasted_iota(jnp.int32, (spots, D // 2), 0)
    for d in range(pairs):
        fetch_feat[d].wait()
        first = owners[d] * per_pair + offset

        def one(user, carry, d=d, first=first):
            halves = [None, None]
            for p in range(spots):
                at = pl.ds(ids[p, first + user], 1)
                for h in range(2):
                    row = jnp.broadcast_to(wide[h, at, :], (spots, D // 2))
                    halves[h] = row if p == 0 else jnp.where(spot == p, row, halves[h])
            rows = jnp.concatenate(halves, axis=1)
            out[d, user] = (feat[d, user].astype(F32) + rows).astype(BF16)
            return carry

        lax.fori_loop(0, users, one, 0, unroll=16)
        if later:
            target = out_hbm[d]
        else:
            target = out_hbm[0].at[pl.ds(d * users, users)]
        send.append(pltpu.make_async_copy(out.at[d], target, out_sem.at[d]))
        send[-1].start()
    for copy in send:
        copy.wait()


def lookup(ids, features, table, start, users, pa_count, dev_count, later, own=()):
    all_users, spots, width = features.shape
    per_pair = all_users // pa_count
    per_core = per_pair // dev_count
    block = (pa_count, users, spots, width)
    hbm = pl.BlockSpec(memory_space=pltpu.HBM)
    outs = pa_count if later else 1
    made = [pltpu.HBM((users * (1 if later else pa_count), spots, width), BF16)] * outs
    if own:
        made.append(pltpu.HBM((sum(w.size for w in own) // (D // 2), D // 2), BF16))
    scratch = [
        pltpu.VMEM((2, table.shape[0], D // 2), F32),
        pltpu.VMEM(table.shape, BF16),
        pltpu.SemaphoreType.DMA((TABLE_PARTS,)),
        pltpu.SMEM(ids.shape, jnp.int32),
        pltpu.VMEM(block, BF16),
        pltpu.VMEM(block, BF16),
        pltpu.SemaphoreType.DMA,
        pltpu.SemaphoreType.DMA((pa_count,)),
        pltpu.SemaphoreType.DMA((pa_count,)),
    ]
    if own:
        scratch += [pltpu.VMEM(w.shape, BF16) for w in own]
        scratch += [pltpu.VMEM(made[-1].shape, BF16), pltpu.SemaphoreType.DMA((len(own) + 1,))]
    return pl.pallas_call(
        functools.partial(
            lookup_kernel, start=start, per_pair=per_pair, per_core=per_core, outs=outs
        ),
        out_shape=made,
        in_specs=[hbm] * (3 + len(own)),
        out_specs=[hbm] * len(made),
        scratch_shapes=scratch,
        compiler_params=pltpu.CompilerParams(vmem_limit_bytes=12 << 20),
        name="lookup",
    )(*in_hbm(ids, features, table, *own))


def weights_kernel(
    lens_ref, seed_ref, own, other, all_ref, valid_ref, base_ref, *, cut, ff
):
    pairs = lens_ref.shape[0]
    history = seed_ref.shape[1]
    spots = history // pairs
    place = lax.axis_index("pa")

    def arrival(lane):
        position = lane % history
        for i in range(pairs):
            origin = moved_to(place, -(i // Z_LO), i % Z_LO, pairs)
            here = (lane % history) // spots == i
            position = jnp.where(here, origin * spots + lane % spots, position)
        return position

    owned = (valid_ref.shape[0], lens_ref.shape[1])
    at = lax.broadcasted_iota(jnp.int32, owned, 0) + lax.axis_index("dev") * owned[0]
    near = lax.broadcasted_iota(jnp.int32, owned, 1) == at
    row = jnp.broadcast_to(lens_ref[pl.ds(place, 1), :].astype(F32), owned)
    lens = jnp.sum(jnp.where(near, row, 0.0), axis=1, keepdims=True)
    lane = lax.broadcasted_iota(jnp.int32, valid_ref.shape, 1)
    first = lax.broadcasted_iota(jnp.int32, valid_ref.shape, 0) < cut
    position = jnp.where(first, lane % history, arrival(lane))
    valid_ref[...] = (position.astype(F32) < lens).astype(F32)

    seed = seed_ref[...].astype(F32)
    chosen = lax.broadcasted_iota(jnp.int32, (history, history), 0) == arrival(
        lax.broadcasted_iota(jnp.int32, (history, history), 1)
    )
    moved = jnp.dot(
        seed.astype(BF16), chosen.astype(F32).astype(BF16), preferred_element_type=F32
    )
    for i, table in enumerate((seed, moved)):
        base_ref[i] = jnp.concatenate([(table - 7.5) * 0.25] * GROUP, axis=1)

    half = D // 2
    low = lax.axis_index("dev") == 0
    at = 0
    for i in range(3):
        all_ref[at : at + D, :half] = own[at : at + D]
        all_ref[at : at + D, half:] = other[at : at + D]
        at += D
    bilinear = slice(at, at + D)
    source = at + D
    for part in (own, other):
        for i in range(ff // D):
            for h in range(2):
                rows = slice(source + (2 * i + h) * D, source + (2 * i + h + 1) * D)
                all_ref[at : at + D, h * half : (h + 1) * half] = part[rows]
            at += D

    @pl.when(low)
    def _():
        all_ref[at : at + D, :half] = own[bilinear]
        all_ref[at : at + D, half:] = other[bilinear]

    @pl.when(jnp.logical_not(low))
    def _():
        all_ref[at : at + D, :half] = other[bilinear]
        all_ref[at : at + D, half:] = own[bilinear]

    after = at + D
    source += 2 * ff
    for count in (half, ff):
        for part in (own, other):
            for h in range(2):
                rows = slice(source + h * count, source + (h + 1) * count)
                all_ref[after : after + count, h * half : (h + 1) * half] = part[rows]
            after += count
        source += 2 * count


def finish_weights(own, other, lens, seed, cut, per_core, ff):
    operands = in_hbm(lens, seed, own, other)
    vmem = pl.BlockSpec(memory_space=pltpu.VMEM)
    lanes = GROUP * seed.shape[1]
    return pl.pallas_call(
        functools.partial(weights_kernel, cut=cut, ff=ff),
        out_shape=[
            pltpu.VMEM((5 * D + 4 * ff, D), BF16),
            pltpu.VMEM((per_core, lanes), F32),
            pltpu.VMEM((2, CAPS, lanes), F32),
        ],
        in_specs=[vmem] * len(operands),
        out_specs=[vmem] * 3,
        compiler_params=pltpu.CompilerParams(vmem_limit_bytes=8 << 20),
        name="weights",
    )(*operands)


def split(x):
    high = x.astype(BF16)
    return jnp.concatenate([high, (x - high.astype(F32)).astype(BF16)], axis=0)


def joined(x):
    half = x.shape[0] // 2
    return x[:half] + x[half:]


def encode_kernel(*refs, steps, start, later):
    valid_ref, base_ref, w_ref = refs[:3]
    parts = refs[3 + (2 if later else 0) : -3]
    own_ref, other_ref, interest_ref = refs[-3:]
    step = pl.program_id(0)
    if later:
        own_ref[:start] = refs[3][:start]
        other_ref[:start] = refs[4][:start]
        pairs, (all_users, spots, _) = len(parts), parts[0].shape
    else:
        pairs, all_users, spots, _ = parts[0].shape
    block = all_users // steps
    history = pairs * spots
    rows = block * history
    head = D // HEADS
    lanes = HEADS * history
    at = pl.ds(step * block, block)
    if later:
        x = jnp.stack([part[at].astype(F32) for part in parts], axis=1)
    else:
        x = jnp.swapaxes(parts[0][:, at].astype(F32), 0, 1)
    x = x.reshape(rows, D).astype(BF16)

    def through(i):
        return jnp.dot(x, w_ref[i * D : (i + 1) * D, :], preferred_element_type=F32)

    queries = (through(0) * (1.0 / head**0.5)).astype(BF16)
    keys = through(1).astype(BF16)
    values = through(2).astype(BF16)

    lane_head = lax.broadcasted_iota(jnp.int32, (history, D), 1) // head
    own_head = [(lane_head == h).astype(F32).astype(BF16) for h in range(HEADS)]
    odd_even = [own_head[0] + own_head[2], own_head[1] + own_head[3]]
    row_head = lax.broadcasted_iota(jnp.int32, (lanes, D), 0) // history
    col_head = lax.broadcasted_iota(jnp.int32, (lanes, D), 1) // head
    ones = (row_head == col_head).astype(F32).astype(BF16)
    key_valid = [valid_ref[pl.ds(start + step * block + u, 1), :] for u in range(block)]
    users = [slice(u * history, (u + 1) * history) for u in range(block)]
    scores = []
    none = jnp.zeros((history, D // 2), BF16)
    for first in range(0, block, 2):
        pair = users[first : first + 2]
        key_wide = jnp.concatenate([keys[at] * m for at in pair for m in odd_even], axis=0)
        query_wide = jnp.concatenate(
            [
                part
                for at in pair
                for part in (
                    jnp.concatenate([queries[at, : D // 2], none], axis=1),
                    jnp.concatenate([none, queries[at, D // 2 :]], axis=1),
                )
            ],
            axis=0,
        )
        both = lax.dot_general(
            query_wide, key_wide, (((1,), (1,)), ((), ())), preferred_element_type=F32
        )
        for u in range(2):
            rows_u = both[u * D // 2 : (u + 1) * D // 2, u * D // 2 : (u + 1) * D // 2]
            scores.append(jnp.concatenate([rows_u[:history], rows_u[history:]], axis=1))
    rounded = [
        jnp.where(key_valid[u] > 0.0, jnp.exp(s), 0.0).astype(BF16)
        for u, s in enumerate(scores)
    ]
    totals = jnp.dot(jnp.concatenate(rounded, axis=0), ones, preferred_element_type=F32)
    weighted = []
    for first in range(0, block, 2):
        pair = users[first : first + 2]
        value_wide = jnp.concatenate([values[at] * m for at in pair for m in odd_even], axis=0)
        prob_wide = []
        for u in range(2):
            for g in range(2):
                part = rounded[first + u][:, g * D // 2 : (g + 1) * D // 2]
                prob_wide.append(jnp.concatenate([part, none] if u == 0 else [none, part], axis=1))
        both = jnp.dot(jnp.concatenate(prob_wide, axis=0), value_wide, preferred_element_type=F32)
        for u in range(2):
            rows_u = both[u * D // 2 : (u + 1) * D // 2]
            weighted.append(
                jnp.concatenate([rows_u[:history, : D // 2], rows_u[history:, D // 2 :]], axis=1)
            )
    attended = (jnp.concatenate(weighted, axis=0) / totals).astype(BF16)
    tail = 3 + FF // D
    hidden = [jax.nn.gelu(through(i)).astype(BF16) for i in range(3, tail)]
    everything = jnp.concatenate([x, attended] + hidden, axis=1)
    interest = jnp.dot(everything, w_ref[tail * D :, :], preferred_element_type=F32).astype(BF16)
    interest_ref[pl.ds(pl.multiple_of(step * rows, rows), rows), :] = interest

    @pl.when(step == steps - 1)
    def _():
        base = base_ref[int(later)]
        route(valid_ref, base, own_ref, other_ref, interest_ref, history, start)


def route(valid_ref, base, own_ref, other_ref, interest_ref, history, start):
    lanes = GROUP * history
    groups = BLOCK // GROUP
    blocks = range(interest_ref.shape[0] // (BLOCK * history))
    lane = lax.broadcasted_iota(jnp.int32, (BLOCK, lanes), 1)
    user = lax.broadcasted_iota(jnp.int32, (BLOCK, lanes), 0)
    mine = (lane // history) == (user % GROUP)
    in_group = [(user // GROUP) == g for g in range(groups)]
    base = jnp.broadcast_to(base[:, None, :], (CAPS, BLOCK, lanes))
    logits = [base for _ in blocks]
    valid = []
    for b in blocks:
        at = slice(start + b * BLOCK, start + (b + 1) * BLOCK)
        real = mine & (valid_ref[at, :] > 0.0)
        valid.append([(real & here).astype(F32)[None] for here in in_group])

    def vectors(b, g):
        return interest_ref[(b * groups + g) * lanes : (b * groups + g + 1) * lanes, :]

    def softmax(x):
        weights = jnp.exp(x - jnp.max(x, axis=0, keepdims=True))
        return weights / jnp.sum(weights, axis=0, keepdims=True)

    def parts(weights, b):
        return [split((weights * v).reshape(CAPS * BLOCK, lanes)) for v in valid[b]]

    def squash(summed):
        squares = jnp.sum(summed * summed, axis=1, keepdims=True)
        return summed * (jnp.sqrt(squares) / (1.0 + squares))

    for sweep in range(ITERS):
        if sweep == 0:
            weights = [softmax(base)] * len(logits)
        else:
            weights = [softmax(x) for x in logits]
        weighted = [parts(weights[b], b) for b in blocks]
        summed = [
            joined(
                sum(
                    jnp.dot(weighted[b][g], vectors(b, g), preferred_element_type=F32)
                    for g in range(groups)
                )
            )
            for b in blocks
        ]
        capsules = [squash(x) for x in summed]
        if sweep + 1 < ITERS:
            caps = [split(x) for x in capsules]
            near = [
                [
                    lax.dot_general(
                        caps[b], vectors(b, g), (((1,), (1,)), ((), ())), preferred_element_type=F32
                    )
                    for g in range(groups)
                ]
                for b in blocks
            ]
            for b in blocks:
                added = [joined(x).reshape(CAPS, BLOCK, lanes) for x in near[b]]
                chosen = added[-1]
                for g in range(groups - 1):
                    chosen = jnp.where(in_group[g][None], added[g], chosen)
                logits[b] = logits[b] + chosen
    half = D // 2
    low_own = lax.axis_index("dev") == 0
    for b in blocks:
        made = capsules[b].reshape(CAPS, BLOCK, D)
        low, high = made[:, :, :half], made[:, :, half:]
        kept, passed = jnp.where(low_own, low, high), jnp.where(low_own, high, low)
        for j in range(CAPS):
            at = slice(start + b * BLOCK, start + (b + 1) * BLOCK)
            own_ref[at, j, :] = kept[j]
            other_ref[at, j, :] = passed[j]


def encode(parts, valid, base, weights, steps, start, before):
    later = len(before) > 0
    rows = len(parts) * parts[0].size // D
    vmem = pl.BlockSpec(memory_space=pltpu.VMEM)
    operands = [valid, base, weights, *before, *parts]
    made = pltpu.VMEM((valid.shape[0], CAPS, D // 2), F32)
    return pl.pallas_call(
        functools.partial(encode_kernel, steps=steps, start=start, later=later),
        out_shape=[made, made],
        grid=(steps,),
        in_specs=[vmem] * len(operands),
        out_specs=[vmem] * 2,
        scratch_shapes=[pltpu.VMEM((rows, D), BF16)],
        compiler_params=pltpu.CompilerParams(vmem_limit_bytes=10 << 20),
        name="encode",
    )(*operands)


def body(
    features, item_ids, item_table, lengths, routing_seed, w_qkv, w_out, w_bilinear, w_up, w_down
):
    pa_count = lax.axis_size("pa")
    dev_count = lax.axis_size("dev")
    spots = features.shape[1]
    per_core = lengths.shape[0] // (pa_count * dev_count)
    core = lax.axis_index("dev").astype(jnp.int32)
    swap = [(i, dev_count - 1 - i) for i in range(dev_count)]
    own = (w_qkv, w_out, w_bilinear, w_up, w_down)
    cut = per_core * FIRST[0] // FIRST[1]
    ids = item_ids.T
    counts = (pa_count, dev_count)
    sent, packed = lookup(ids, features, item_table, 0, cut, *counts, False, own)
    got = lax.all_to_all(sent, "pa", split_axis=0, concat_axis=0, tiled=True)
    got = got.reshape(pa_count, cut, spots, D)
    other = lax.ppermute(packed, "dev", swap)
    ids, other = lax.optimization_barrier((ids, other))
    late = lookup(ids, features, item_table, cut, per_core - cut, *counts, True)
    lens, late = lax.optimization_barrier((lengths.reshape(pa_count, -1), late))
    ff = w_up.shape[1]
    weights, valid, base = finish_weights(packed, other, lens, routing_seed, cut, per_core, ff)
    parts = [late[0]]
    for i in range(1, pa_count):
        pairs = [
            (p, moved_to(p, i // Z_LO, i % Z_LO, pa_count)) for p in range(pa_count)
        ]
        block = late[i]
        if i > AHEAD:
            block, parts[i - AHEAD], valid = lax.optimization_barrier(
                (block, parts[i - AHEAD], valid)
            )
        parts.append(lax.ppermute(block, "pa", pairs))
    made = encode([got], valid, base, weights, STEPS[0], 0, ())
    kept, passed = encode(parts, valid, base, weights, STEPS[1], cut, tuple(made))
    came = lax.ppermute(passed, "dev", swap)
    out = jnp.zeros((dev_count * per_core, CAPS, D // dev_count), F32)
    out = lax.dynamic_update_slice_in_dim(out, kept, core * per_core, 0)
    return lax.dynamic_update_slice_in_dim(out, came, (1 - core) * per_core, 0)


def solution(mesh):
    in_specs = (
        P("au", "pa", None),
        P("au", "pa"),
        P(),
        P("au"),
        P(),
        P(None, None, "dev"),
        P("dev", None),
        P(None, "dev"),
        P(None, "dev"),
        P("dev", None),
    )
    out_specs = P(("au", "pa"), None, "dev")
    return jax.shard_map(body, mesh=mesh, in_specs=in_specs, out_specs=out_specs, check_vma=False)
```

```python
import functools

import jax
import jax.numpy as jnp
from jax import lax
from jax.experimental import pallas as pl
from jax.experimental.pallas import tpu as pltpu
from jax.sharding import PartitionSpec as P

D = 256
HEADS = 4
FF = 1024
CAPS = 4
ITERS = 3
FIRST = (4, 8)
BLOCK = 8
STEPS = (2, 2)
TABLE_PARTS = 2
AHEAD = 5
Z_LO = 2
GROUP = 4
F32 = jnp.float32
BF16 = jnp.bfloat16


def in_hbm(*arrays):
    return tuple(pltpu.with_memory_space_constraint(a, pltpu.HBM) for a in arrays)


def moved_to(place, along, across, count):
    rest = count // Z_LO
    return (place // Z_LO + along + rest) % rest * Z_LO + (place % Z_LO + across) % Z_LO


def packed_pieces(qkv, out, bilinear, up, down):
    half = D // 2
    pieces = [(qkv, (i,)) for i in range(3)] + [(bilinear, ())]
    for w in (up, out, down):
        pieces += [(w, (slice(None), slice(i, i + half))) for i in range(0, w.shape[1], half)]
    return pieces


def lookup_kernel(*refs, start, per_pair, per_core, outs):
    later = outs > 1
    ids_hbm, feat_hbm, table_hbm, refs = *refs[:3], refs[3:]
    if not later:
        own, refs = refs[:5], refs[5:]
    out_hbm, refs = refs[:outs], refs[outs:]
    fetch_own = []
    if not later:
        packed_hbm, held, packed, own_sem = refs[0], refs[-7:-2], refs[-2], refs[-1]
        refs = refs[1:-7]
        for i, w in enumerate(own):
            fetch_own.append(pltpu.make_async_copy(w, held[i], own_sem.at[i]))
    wide, table, table_sem, ids, feat, out, id_sem, feat_sem, out_sem = refs
    pairs, users, spots, _ = feat.shape
    place = lax.axis_index("pa")
    offset = lax.axis_index("dev") * per_core + start
    if later:
        owners = [moved_to(place, i // Z_LO, i % Z_LO, pairs) for i in range(pairs)]
    else:
        owners = list(range(pairs))
    fetch_ids = pltpu.make_async_copy(ids_hbm, ids, id_sem)
    fetch_ids.start()
    fetch_table = []
    rows = table.shape[0] // TABLE_PARTS
    for i in range(TABLE_PARTS):
        at = pl.ds(i * rows, rows)
        fetch_table.append(pltpu.make_async_copy(table_hbm.at[at], table.at[at], table_sem.at[i]))
        fetch_table[-1].start()
    for copy in fetch_own:
        copy.start()
    fetch_feat = []
    for d in range(pairs):
        at = pl.ds(owners[d] * per_pair + offset, users)
        fetch_feat.append(pltpu.make_async_copy(feat_hbm.at[at], feat.at[d], feat_sem.at[d]))
        fetch_feat[-1].start()
    for i, fetch in enumerate(fetch_table):
        fetch.wait()

        def widen(j, carry, i=i):
            at = pl.ds(pl.multiple_of(i * rows + j * 128, 128), 128)
            for h in range(2):
                wide[h, at, :] = table[at, h * (D // 2) : (h + 1) * (D // 2)].astype(F32)
            return carry

        lax.fori_loop(0, rows // 128, widen, 0)
    send = []
    if not later:
        for copy in fetch_own:
            copy.wait()
        at = 0
        for ref, index in packed_pieces(*held):
            piece = ref[(*index, Ellipsis)]
            packed[at : at + piece.shape[0], :] = piece
            at += piece.shape[0]
        send.append(pltpu.make_async_copy(packed, packed_hbm, own_sem.at[len(own)]))
        send[-1].start()
    fetch_ids.wait()
    spot = lax.broadcasted_iota(jnp.int32, (spots, D // 2), 0)
    for d in range(pairs):
        fetch_feat[d].wait()
        first = owners[d] * per_pair + offset

        def one(user, carry, d=d, first=first):
            halves = [None, None]
            for p in range(spots):
                at = pl.ds(ids[p, first + user], 1)
                for h in range(2):
                    row = jnp.broadcast_to(wide[h, at, :], (spots, D // 2))
                    halves[h] = row if p == 0 else jnp.where(spot == p, row, halves[h])
            rows = jnp.concatenate(halves, axis=1)
            out[d, user] = (feat[d, user].astype(F32) + rows).astype(BF16)
            return carry

        lax.fori_loop(0, users, one, 0, unroll=16)
        if later:
            target = out_hbm[d]
        else:
            target = out_hbm[0].at[pl.ds(d * users, users)]
        send.append(pltpu.make_async_copy(out.at[d], target, out_sem.at[d]))
        send[-1].start()
    for copy in send:
        copy.wait()


def lookup(ids, features, table, start, users, pa_count, dev_count, later, own=()):
    all_users, spots, width = features.shape
    per_pair = all_users // pa_count
    per_core = per_pair // dev_count
    block = (pa_count, users, spots, width)
    hbm = pl.BlockSpec(memory_space=pltpu.HBM)
    outs = pa_count if later else 1
    made = [pltpu.HBM((users * (1 if later else pa_count), spots, width), BF16)] * outs
    if own:
        made.append(pltpu.HBM((sum(w.size for w in own) // (D // 2), D // 2), BF16))
    scratch = [
        pltpu.VMEM((2, table.shape[0], D // 2), F32),
        pltpu.VMEM(table.shape, BF16),
        pltpu.SemaphoreType.DMA((TABLE_PARTS,)),
        pltpu.SMEM(ids.shape, jnp.int32),
        pltpu.VMEM(block, BF16),
        pltpu.VMEM(block, BF16),
        pltpu.SemaphoreType.DMA,
        pltpu.SemaphoreType.DMA((pa_count,)),
        pltpu.SemaphoreType.DMA((pa_count,)),
    ]
    if own:
        scratch += [pltpu.VMEM(w.shape, BF16) for w in own]
        scratch += [pltpu.VMEM(made[-1].shape, BF16), pltpu.SemaphoreType.DMA((len(own) + 1,))]
    return pl.pallas_call(
        functools.partial(
            lookup_kernel, start=start, per_pair=per_pair, per_core=per_core, outs=outs
        ),
        out_shape=made,
        in_specs=[hbm] * (3 + len(own)),
        out_specs=[hbm] * len(made),
        scratch_shapes=scratch,
        compiler_params=pltpu.CompilerParams(vmem_limit_bytes=12 << 20),
        name="lookup",
    )(*in_hbm(ids, features, table, *own))


def weights_kernel(
    lens_ref, seed_ref, own, other, all_ref, valid_ref, base_ref, *, cut, ff
):
    pairs = lens_ref.shape[0]
    history = seed_ref.shape[1]
    spots = history // pairs
    place = lax.axis_index("pa")

    def arrival(lane):
        position = lane % history
        for i in range(pairs):
            origin = moved_to(place, -(i // Z_LO), i % Z_LO, pairs)
            here = (lane % history) // spots == i
            position = jnp.where(here, origin * spots + lane % spots, position)
        return position

    owned = (valid_ref.shape[0], lens_ref.shape[1])
    at = lax.broadcasted_iota(jnp.int32, owned, 0) + lax.axis_index("dev") * owned[0]
    near = lax.broadcasted_iota(jnp.int32, owned, 1) == at
    row = jnp.broadcast_to(lens_ref[pl.ds(place, 1), :].astype(F32), owned)
    lens = jnp.sum(jnp.where(near, row, 0.0), axis=1, keepdims=True)
    lane = lax.broadcasted_iota(jnp.int32, valid_ref.shape, 1)
    first = lax.broadcasted_iota(jnp.int32, valid_ref.shape, 0) < cut
    position = jnp.where(first, lane % history, arrival(lane))
    valid_ref[...] = (position.astype(F32) < lens).astype(F32)

    seed = seed_ref[...].astype(F32)
    chosen = lax.broadcasted_iota(jnp.int32, (history, history), 0) == arrival(
        lax.broadcasted_iota(jnp.int32, (history, history), 1)
    )
    moved = jnp.dot(
        seed.astype(BF16), chosen.astype(F32).astype(BF16), preferred_element_type=F32
    )
    for i, table in enumerate((seed, moved)):
        base_ref[i] = jnp.concatenate([(table - 7.5) * 0.25] * GROUP, axis=1)

    half = D // 2
    low = lax.axis_index("dev") == 0
    at = 0
    for i in range(3):
        all_ref[at : at + D, :half] = own[at : at + D]
        all_ref[at : at + D, half:] = other[at : at + D]
        at += D
    bilinear = slice(at, at + D)
    source = at + D
    for part in (own, other):
        for i in range(ff // D):
            for h in range(2):
                rows = slice(source + (2 * i + h) * D, source + (2 * i + h + 1) * D)
                all_ref[at : at + D, h * half : (h + 1) * half] = part[rows]
            at += D

    @pl.when(low)
    def _():
        all_ref[at : at + D, :half] = own[bilinear]
        all_ref[at : at + D, half:] = other[bilinear]

    @pl.when(jnp.logical_not(low))
    def _():
        all_ref[at : at + D, :half] = other[bilinear]
        all_ref[at : at + D, half:] = own[bilinear]

    after = at + D
    source += 2 * ff
    for count in (half, ff):
        for part in (own, other):
            for h in range(2):
                rows = slice(source + h * count, source + (h + 1) * count)
                all_ref[after : after + count, h * half : (h + 1) * half] = part[rows]
            after += count
        source += 2 * count


def finish_weights(own, other, lens, seed, cut, per_core, ff):
    operands = in_hbm(lens, seed, own, other)
    vmem = pl.BlockSpec(memory_space=pltpu.VMEM)
    lanes = GROUP * seed.shape[1]
    return pl.pallas_call(
        functools.partial(weights_kernel, cut=cut, ff=ff),
        out_shape=[
            pltpu.VMEM((5 * D + 4 * ff, D), BF16),
            pltpu.VMEM((per_core, lanes), F32),
            pltpu.VMEM((2, CAPS, lanes), F32),
        ],
        in_specs=[vmem] * len(operands),
        out_specs=[vmem] * 3,
        compiler_params=pltpu.CompilerParams(vmem_limit_bytes=8 << 20),
        name="weights",
    )(*operands)


def split(x):
    high = x.astype(BF16)
    return jnp.concatenate([high, (x - high.astype(F32)).astype(BF16)], axis=0)


def joined(x):
    half = x.shape[0] // 2
    return x[:half] + x[half:]


def encode_kernel(*refs, steps, start, later):
    valid_ref, base_ref, w_ref = refs[:3]
    parts = refs[3 + (2 if later else 0) : -3]
    own_ref, other_ref, interest_ref = refs[-3:]
    step = pl.program_id(0)
    if later:
        pairs, (all_users, spots, _) = len(parts), parts[0].shape
    else:
        pairs, all_users, spots, _ = parts[0].shape
    block = all_users // steps
    history = pairs * spots
    rows = block * history
    head = D // HEADS
    lanes = HEADS * history
    at = pl.ds(step * block, block)
    if later:
        x = jnp.stack([part[at].astype(F32) for part in parts], axis=1)
    else:
        x = jnp.swapaxes(parts[0][:, at].astype(F32), 0, 1)
    x = x.reshape(rows, D).astype(BF16)

    def through(i):
        return jnp.dot(x, w_ref[i * D : (i + 1) * D, :], preferred_element_type=F32)

    queries = (through(0) * (1.0 / head**0.5)).astype(BF16)
    keys = through(1).astype(BF16)
    values = through(2).astype(BF16)

    lane_head = lax.broadcasted_iota(jnp.int32, (history, D), 1) // head
    own_head = [(lane_head == h).astype(F32).astype(BF16) for h in range(HEADS)]
    odd_even = [own_head[0] + own_head[2], own_head[1] + own_head[3]]
    row_head = lax.broadcasted_iota(jnp.int32, (lanes, D), 0) // history
    col_head = lax.broadcasted_iota(jnp.int32, (lanes, D), 1) // head
    ones = (row_head == col_head).astype(F32).astype(BF16)
    key_valid = [valid_ref[pl.ds(start + step * block + u, 1), :] for u in range(block)]
    users = [slice(u * history, (u + 1) * history) for u in range(block)]
    scores = []
    none = jnp.zeros((history, D // 2), BF16)
    for first in range(0, block, 2):
        pair = users[first : first + 2]
        key_wide = jnp.concatenate([keys[at] * m for at in pair for m in odd_even], axis=0)
        query_wide = jnp.concatenate(
            [
                part
                for at in pair
                for part in (
                    jnp.concatenate([queries[at, : D // 2], none], axis=1),
                    jnp.concatenate([none, queries[at, D // 2 :]], axis=1),
                )
            ],
            axis=0,
        )
        both = lax.dot_general(
            query_wide, key_wide, (((1,), (1,)), ((), ())), preferred_element_type=F32
        )
        for u in range(2):
            rows_u = both[u * D // 2 : (u + 1) * D // 2, u * D // 2 : (u + 1) * D // 2]
            scores.append(jnp.concatenate([rows_u[:history], rows_u[history:]], axis=1))
    rounded = [
        jnp.where(key_valid[u] > 0.0, jnp.exp(s), 0.0).astype(BF16)
        for u, s in enumerate(scores)
    ]
    totals = jnp.dot(jnp.concatenate(rounded, axis=0), ones, preferred_element_type=F32)
    weighted = []
    for first in range(0, block, 2):
        pair = users[first : first + 2]
        value_wide = jnp.concatenate([values[at] * m for at in pair for m in odd_even], axis=0)
        prob_wide = []
        for u in range(2):
            for g in range(2):
                part = rounded[first + u][:, g * D // 2 : (g + 1) * D // 2]
                prob_wide.append(jnp.concatenate([part, none] if u == 0 else [none, part], axis=1))
        both = jnp.dot(jnp.concatenate(prob_wide, axis=0), value_wide, preferred_element_type=F32)
        for u in range(2):
            rows_u = both[u * D // 2 : (u + 1) * D // 2]
            weighted.append(
                jnp.concatenate([rows_u[:history, : D // 2], rows_u[history:, D // 2 :]], axis=1)
            )
    attended = (jnp.concatenate(weighted, axis=0) / totals).astype(BF16)
    tail = 3 + FF // D
    hidden = [jax.nn.gelu(through(i)).astype(BF16) for i in range(3, tail)]
    everything = jnp.concatenate([x, attended] + hidden, axis=1)
    interest = jnp.dot(everything, w_ref[tail * D :, :], preferred_element_type=F32).astype(BF16)
    interest_ref[pl.ds(pl.multiple_of(step * rows, rows), rows), :] = interest

    @pl.when(step == steps - 1)
    def _():
        if later:
            own_ref[:start] = refs[3][:start]
            other_ref[:start] = refs[4][:start]
        base = base_ref[int(later)]
        route(valid_ref, base, own_ref, other_ref, interest_ref, history, start)


def route(valid_ref, base, own_ref, other_ref, interest_ref, history, start):
    lanes = GROUP * history
    groups = BLOCK // GROUP
    blocks = range(interest_ref.shape[0] // (BLOCK * history))
    lane = lax.broadcasted_iota(jnp.int32, (BLOCK, lanes), 1)
    user = lax.broadcasted_iota(jnp.int32, (BLOCK, lanes), 0)
    mine = (lane // history) == (user % GROUP)
    in_group = [(user // GROUP) == g for g in range(groups)]
    base = jnp.broadcast_to(base[:, None, :], (CAPS, BLOCK, lanes))
    logits = [base for _ in blocks]
    valid = []
    for b in blocks:
        at = slice(start + b * BLOCK, start + (b + 1) * BLOCK)
        real = mine & (valid_ref[at, :] > 0.0)
        valid.append([(real & here).astype(F32)[None] for here in in_group])

    def vectors(b, g):
        return interest_ref[(b * groups + g) * lanes : (b * groups + g + 1) * lanes, :]

    def softmax(x):
        weights = jnp.exp(x - jnp.max(x, axis=0, keepdims=True))
        return weights / jnp.sum(weights, axis=0, keepdims=True)

    def parts(weights, b):
        return [split((weights * v).reshape(CAPS * BLOCK, lanes)) for v in valid[b]]

    def squash(summed):
        squares = jnp.sum(summed * summed, axis=1, keepdims=True)
        return summed * (jnp.sqrt(squares) / (1.0 + squares))

    for sweep in range(ITERS):
        if sweep == 0:
            weights = [softmax(base)] * len(logits)
        else:
            weights = [softmax(x) for x in logits]
        weighted = [parts(weights[b], b) for b in blocks]
        summed = [
            joined(
                sum(
                    jnp.dot(weighted[b][g], vectors(b, g), preferred_element_type=F32)
                    for g in range(groups)
                )
            )
            for b in blocks
        ]
        capsules = [squash(x) for x in summed]
        if sweep + 1 < ITERS:
            caps = [split(x) for x in capsules]
            near = [
                [
                    lax.dot_general(
                        caps[b], vectors(b, g), (((1,), (1,)), ((), ())), preferred_element_type=F32
                    )
                    for g in range(groups)
                ]
                for b in blocks
            ]
            for b in blocks:
                added = [joined(x).reshape(CAPS, BLOCK, lanes) for x in near[b]]
                chosen = added[-1]
                for g in range(groups - 1):
                    chosen = jnp.where(in_group[g][None], added[g], chosen)
                logits[b] = logits[b] + chosen
    half = D // 2
    low_own = lax.axis_index("dev") == 0
    for b in blocks:
        made = capsules[b].reshape(CAPS, BLOCK, D)
        low, high = made[:, :, :half], made[:, :, half:]
        kept, passed = jnp.where(low_own, low, high), jnp.where(low_own, high, low)
        for j in range(CAPS):
            at = slice(start + b * BLOCK, start + (b + 1) * BLOCK)
            own_ref[at, j, :] = kept[j]
            other_ref[at, j, :] = passed[j]


def encode(parts, valid, base, weights, steps, start, before):
    later = len(before) > 0
    rows = len(parts) * parts[0].size // D
    vmem = pl.BlockSpec(memory_space=pltpu.VMEM)
    operands = [valid, base, weights, *before, *parts]
    made = pltpu.VMEM((valid.shape[0], CAPS, D // 2), F32)
    return pl.pallas_call(
        functools.partial(encode_kernel, steps=steps, start=start, later=later),
        out_shape=[made, made],
        grid=(steps,),
        in_specs=[vmem] * len(operands),
        out_specs=[vmem] * 2,
        scratch_shapes=[pltpu.VMEM((rows, D), BF16)],
        compiler_params=pltpu.CompilerParams(vmem_limit_bytes=10 << 20),
        name="encode",
    )(*operands)


def body(
    features, item_ids, item_table, lengths, routing_seed, w_qkv, w_out, w_bilinear, w_up, w_down
):
    pa_count = lax.axis_size("pa")
    dev_count = lax.axis_size("dev")
    spots = features.shape[1]
    per_core = lengths.shape[0] // (pa_count * dev_count)
    core = lax.axis_index("dev").astype(jnp.int32)
    swap = [(i, dev_count - 1 - i) for i in range(dev_count)]
    own = (w_qkv, w_out, w_bilinear, w_up, w_down)
    cut = per_core * FIRST[0] // FIRST[1]
    ids = item_ids.T
    counts = (pa_count, dev_count)
    sent, packed = lookup(ids, features, item_table, 0, cut, *counts, False, own)
    got = lax.all_to_all(sent, "pa", split_axis=0, concat_axis=0, tiled=True)
    got = got.reshape(pa_count, cut, spots, D)
    other = lax.ppermute(packed, "dev", swap)
    late = lookup(ids, features, item_table, cut, per_core - cut, *counts, True)
    lens, late = lax.optimization_barrier((lengths.reshape(pa_count, -1), late))
    ff = w_up.shape[1]
    weights, valid, base = finish_weights(packed, other, lens, routing_seed, cut, per_core, ff)
    parts = [late[0]]
    for i in range(1, pa_count):
        pairs = [
            (p, moved_to(p, i // Z_LO, i % Z_LO, pa_count)) for p in range(pa_count)
        ]
        block = late[i]
        if i > AHEAD:
            block, parts[i - AHEAD], valid = lax.optimization_barrier(
                (block, parts[i - AHEAD], valid)
            )
        parts.append(lax.ppermute(block, "pa", pairs))
    made = encode([got], valid, base, weights, STEPS[0], 0, ())
    kept, passed = encode(parts, valid, base, weights, STEPS[1], cut, tuple(made))
    came = lax.ppermute(passed, "dev", swap)
    out = jnp.zeros((dev_count * per_core, CAPS, D // dev_count), F32)
    out = lax.dynamic_update_slice_in_dim(out, kept, core * per_core, 0)
    return lax.dynamic_update_slice_in_dim(out, came, (1 - core) * per_core, 0)


def solution(mesh):
    in_specs = (
        P("au", "pa", None),
        P("au", "pa"),
        P(),
        P("au"),
        P(),
        P(None, None, "dev"),
        P("dev", None),
        P(None, "dev"),
        P(None, "dev"),
        P("dev", None),
    )
    out_specs = P(("au", "pa"), None, "dev")
    return jax.shard_map(body, mesh=mesh, in_specs=in_specs, out_specs=out_specs, check_vma=False)
```
